32 devices in a mesh: band: 16 (over z, y, x), member: 2 (over core).
Axes of the slice: x: 2, y: 2, z: 4, core: 2. Of those that a mesh axis runs over, the one named last changes fastest.
Arguments:
- scaled_atmosphere_field: float32 [80, 4096], P(None, 'band'), may hold values from -6 to 6
- perturbation: bfloat16 [2, 80, 4096], P('member', None, 'band'), may hold values from -6 to 6
- target: bfloat16 [2, 80, 4096], P('member', None, 'band'), may hold values from -6 to 6
- weight_map: bfloat16 [80, 4096], P(None, 'band'), may hold values from 0.01 to 10
- enc_send: int32 [16, 16, 32], P('band'), may hold values from -1 to 255, as said below
- enc_recv: int32 [16, 16, 32], P('band'), may hold values from -1 to 255, as said below
- dec_send: int32 [16, 16, 32], P('band'), may hold values from -1 to 255, as said below
- dec_recv: int32 [16, 16, 32], P('band'), may hold values from -1 to 255, as said below
- lattice_lift_matrix: bfloat16 [80, 512], replicated, may hold values from -0.625 to 0.625
- mixing_rescale_factor: float32 [512], replicated, may hold values from 0.1 to 1.9
- expand_matrix: bfloat16 [512, 512], replicated, may hold values from -0.25 to 0.25
- contract_matrix: bfloat16 [512, 512], replicated, may hold values from -0.25 to 0.25
- readout_matrix: bfloat16 [512, 80], replicated, may hold values from -0.25 to 0.25
Outputs:
- student_outputs: float32 [2, 80, 4096], P('member', None, 'band')
- mesh_grad: bfloat16 [2, 4096, 512], P('member', 'band')
- grad_up: float32 [2, 512, 512], P('member')
- grad_down: float32 [2, 512, 512], P('member')
- grad_dec: float32 [2, 512, 80], P('member')
- grad_gain: float32 [2, 512], P('member')
The draws below stay inside these ranges and needn't reach their ends.
Inputs may be any that keep to these rules, and one draw needn't show every extreme that they name: enc_send[s, d, k] is a local grid cell of band s (0 to 255) or -1 for an empty slot; in every draw one band fills all its slots and one partition receives full blocks of 32 from every band. enc_recv[d, s, k] is a local mesh node of partition d, and -1 exactly where enc_send[s, d, k] is -1. dec_send[s, d, k] is a local mesh node of partition s or -1 for an empty slot; in every draw one partition fills all its slots and one band receives full blocks of 32 from every partition. dec_recv[d, s, k] is a local grid cell of band d, and -1 exactly where dec_send[s, d, k] is -1.
All inputs are finite; a program needn't handle non-finite values.
Results may differ from the reference program's by a relative error of at most 0.0062.
Values may be sent and summed in bfloat16 or wider, within the bound.
No kernel may reach another device: no remote copies, remote signals or barrier semaphores. Data moves between devices by JAX's collectives and lax.ppermute only.
A program may use at most 64 MiB of HBM per device.

```python
import math
import jax
import jax.numpy as jnp
from jax import lax

CH = 80
LAT = 512
HID = 512
GRID_DEV = 256
MESH_DEV = 256
BANDS = 16
MEMBERS = 2
NGRID = 4096
NMESH = 4096
ENC_CAP = 32
DEC_CAP = 32


def draw_weight_map(key, part):
    band = (jnp.arange(NGRID, dtype=jnp.int32) // GRID_DEV).astype(jnp.float32)
    steps = float(max(BANDS - 1, 1))
    rise = jnp.exp(math.log(100.0) * (band - steps) / steps)
    base = jnp.exp(jax.random.uniform(key, (CH, NGRID), jnp.float32, 0.0, math.log(10.0)))
    return jnp.clip(base * rise[None, :], 0.01, 10.0).astype(jnp.bfloat16)


def edge_tables(key, capacity, src_rows, dst_rows):
    keys = jax.random.split(key, 6)
    band_ids = jnp.arange(BANDS, dtype=jnp.int32)
    level = jax.random.randint(keys[0], (BANDS, BANDS), 0, 4)
    polar = ((band_ids < max(BANDS // 8, 1)) | (band_ids >= BANDS - max(BANDS // 8, 1))).astype(jnp.int32)
    level = jnp.minimum(level + polar[:, None], 3)
    coins = jax.random.randint(keys[1], (BANDS, BANDS, capacity), 0, 4)
    live = coins <= level[:, :, None]
    full_row = jax.random.randint(keys[2], (), 0, BANDS)
    full_col = jax.random.randint(keys[3], (), 0, BANDS)
    live = live | (band_ids[:, None, None] == full_row) | (band_ids[None, :, None] == full_col)
    source = jax.random.randint(keys[4], (BANDS, BANDS, capacity), 0, src_rows)
    target_ids = jax.random.randint(keys[5], (BANDS, BANDS, capacity), 0, dst_rows)
    sender = jnp.where(live, source, -1).astype(jnp.int32)
    receiver = jnp.transpose(jnp.where(live, target_ids, -1), (1, 0, 2)).astype(jnp.int32)
    return (sender, receiver)


def draw_enc_send(key, part):
    return edge_tables(jax.random.fold_in(key, 11), ENC_CAP, GRID_DEV, MESH_DEV)[0]


def draw_enc_recv(key, part):
    return edge_tables(jax.random.fold_in(key, 11), ENC_CAP, GRID_DEV, MESH_DEV)[1]


def draw_dec_send(key, part):
    return edge_tables(jax.random.fold_in(key, 12), DEC_CAP, MESH_DEV, GRID_DEV)[0]


def draw_dec_recv(key, part):
    return edge_tables(jax.random.fold_in(key, 12), DEC_CAP, MESH_DEV, GRID_DEV)[1]


def shard_levels(own_key, dims, cuts, smallest, high):
    loudness = 1.0
    for dim, parts in cuts:
        steps = jax.random.uniform(jax.random.fold_in(jax.random.fold_in(own_key, 6), dim), (parts,), jnp.float32, smallest / len(cuts), high / len(cuts))
        loudness = loudness * jnp.repeat(jnp.exp(steps), dims[dim] // parts).reshape((-1,) + (1,) * (len(dims) - 1 - dim))
    return loudness


def scatter_about(key, extent, deviation, limit, pieces=(), held_as=jnp.bfloat16):
    factor_of = shard_levels(key, extent, pieces, -0.22, 0.18) if pieces else 1.0
    entries = jax.random.normal(key, extent, jnp.float32) * deviation * factor_of
    return jnp.minimum(jnp.maximum(entries, -limit), limit).astype(held_as)


def setup_inputs(seed: int = 0) -> dict:
    streams_of = jax.random.split(jax.random.key(seed), 14)
    scaled_atmosphere_field = scatter_about(streams_of[0], (CH, NGRID), 1.0, 6.0, ((1, 16),), jnp.float32)
    perturbation = scatter_about(streams_of[1], (MEMBERS, CH, NGRID), 1.0, 6.0, ((0, 2), (2, 16)))
    target = scatter_about(streams_of[2], (MEMBERS, CH, NGRID), 1.0, 6.0, ((0, 2), (2, 16)))
    weight_map = draw_weight_map(jax.random.fold_in(streams_of[13], 71), 0)
    enc_send = draw_enc_send(jax.random.fold_in(streams_of[13], 71), 0)
    enc_recv = draw_enc_recv(jax.random.fold_in(streams_of[13], 71), 0)
    dec_send = draw_dec_send(jax.random.fold_in(streams_of[13], 71), 0)
    dec_recv = draw_dec_recv(jax.random.fold_in(streams_of[13], 71), 0)
    lattice_lift_matrix = scatter_about(streams_of[8], (CH, LAT), CH ** -0.5, 0.625)
    mixing_rescale_factor = jnp.clip(1.0 + 0.18 * jax.random.normal(streams_of[9], (LAT,), jnp.float32), 0.1, 1.9)
    expand_matrix = scatter_about(streams_of[10], (LAT, HID), LAT ** -0.5, 0.25)
    contract_matrix = scatter_about(streams_of[11], (HID, LAT), HID ** -0.5, 0.25)
    readout_matrix = scatter_about(streams_of[12], (LAT, CH), LAT ** -0.5, 0.25)
    return dict(scaled_atmosphere_field=scaled_atmosphere_field, perturbation=perturbation, target=target, weight_map=weight_map, enc_send=enc_send, enc_recv=enc_recv, dec_send=dec_send, dec_recv=dec_recv, lattice_lift_matrix=lattice_lift_matrix, mixing_rescale_factor=mixing_rescale_factor, expand_matrix=expand_matrix, contract_matrix=contract_matrix, readout_matrix=readout_matrix)


smooth_sq = 0.01
norm_eps = 1e-05

def flat_edges(send_table, recv_table, src_rows, dst_rows):
    band_total = send_table.shape[0]
    band_ids = jnp.arange(band_total, dtype=jnp.int32)
    incoming = jnp.transpose(recv_table, (1, 0, 2))
    source = band_ids[:, None, None] * src_rows + jnp.maximum(send_table, 0)
    target_ids = band_ids[None, :, None] * dst_rows + jnp.maximum(incoming, 0)
    live = (send_table >= 0).astype(jnp.float32)
    return (source.reshape(-1).astype(jnp.int32), target_ids.reshape(-1).astype(jnp.int32), live.reshape(-1))

def slope(diff):
    return diff * lax.rsqrt(diff * diff + smooth_sq)

def evaluate_sample_model(scaled_atmosphere_field, noise_one, lattice_lift_matrix, mixing_rescale_factor, expand_matrix, contract_matrix, readout_matrix, intake_link_pairs, readout_link_pairs):
    inputs_b = (scaled_atmosphere_field + noise_one.astype(jnp.float32)).astype(jnp.bfloat16)
    latent = jax.nn.silu(lax.dot_general(inputs_b, lattice_lift_matrix, (((0,), (0,)), ((), ())), preferred_element_type=jnp.float32)).astype(jnp.bfloat16)
    source, target_ids, live = intake_link_pairs
    carried = latent[source].astype(jnp.float32) * live[:, None]
    summed = jax.ops.segment_sum(carried, target_ids, num_segments=NMESH)
    edge_count = jax.ops.segment_sum(live, target_ids, num_segments=NMESH)
    mesh_state = summed / jnp.maximum(edge_count, 1.0)[:, None]
    recip = lax.rsqrt(lax.optimization_barrier(jnp.mean(mesh_state * mesh_state, axis=1, keepdims=True)) + norm_eps)
    normed_b = (mesh_state * recip * mixing_rescale_factor).astype(jnp.bfloat16)
    hidden_pre = jnp.dot(normed_b, expand_matrix, preferred_element_type=jnp.float32)
    hidden_b = jax.nn.silu(hidden_pre).astype(jnp.bfloat16)
    mesh_next = mesh_state + jnp.dot(hidden_b, contract_matrix, preferred_element_type=jnp.float32)
    next_b = mesh_next.astype(jnp.bfloat16)
    projected = jnp.dot(next_b, readout_matrix, preferred_element_type=jnp.float32).astype(jnp.bfloat16)
    dec_source, dec_target, dec_live = readout_link_pairs
    values = projected[dec_source].astype(jnp.float32) * dec_live[:, None]
    grid_sum = jax.ops.segment_sum(values, dec_target, num_segments=NGRID)
    grid_count = jax.ops.segment_sum(dec_live, dec_target, num_segments=NGRID)
    inverse = 1.0 / jnp.maximum(grid_count, 1.0)
    student_outputs = scaled_atmosphere_field + jnp.transpose(grid_sum * inverse[:, None])
    return (student_outputs, (mesh_state, recip, normed_b, hidden_pre, hidden_b, next_b, inverse))

def member_backward(pred_grad, retained_intermediates, mixing_rescale_factor, expand_matrix, contract_matrix, readout_matrix, readout_link_pairs):
    mesh_state, recip, normed_b, hidden_pre, hidden_b, next_b, inverse = retained_intermediates
    highest = lax.Precision.HIGHEST
    scaled = jnp.transpose(pred_grad * inverse[None, :])
    dec_source, dec_target, dec_live = readout_link_pairs
    per_slot = scaled[dec_target] * dec_live[:, None]
    node_grad = jax.ops.segment_sum(per_slot, dec_source, num_segments=NMESH)
    next_grad = jnp.dot(node_grad, jnp.transpose(readout_matrix.astype(jnp.float32)), precision=highest)
    dec_part = jnp.dot(jnp.transpose(next_b.astype(jnp.float32)), node_grad, precision=highest)
    down_part = jnp.dot(jnp.transpose(hidden_b.astype(jnp.float32)), next_grad, precision=highest)
    hidden_grad = jnp.dot(next_grad, jnp.transpose(contract_matrix.astype(jnp.float32)), precision=highest)
    sigma = jax.nn.sigmoid(hidden_pre)
    pre_grad = hidden_grad * sigma * (1.0 + hidden_pre * (1.0 - sigma))
    up_part = jnp.dot(jnp.transpose(normed_b.astype(jnp.float32)), pre_grad, precision=highest)
    normed_grad = jnp.dot(pre_grad, jnp.transpose(expand_matrix.astype(jnp.float32)), precision=highest)
    gain_part = lax.optimization_barrier(jnp.sum(normed_grad * mesh_state * recip, axis=0))
    gained = normed_grad * mixing_rescale_factor
    state_grad = next_grad + recip * gained - mesh_state * (recip * recip * recip) * lax.optimization_barrier(jnp.mean(gained * mesh_state, axis=1, keepdims=True))
    return (state_grad.astype(jnp.bfloat16), up_part, down_part, dec_part, gain_part)

def reference(scaled_atmosphere_field, perturbation, target, weight_map, enc_send, enc_recv, dec_send, dec_recv, lattice_lift_matrix, mixing_rescale_factor, expand_matrix, contract_matrix, readout_matrix):
    intake_link_pairs = flat_edges(enc_send, enc_recv, GRID_DEV, MESH_DEV)
    readout_link_pairs = flat_edges(dec_send, dec_recv, MESH_DEV, GRID_DEV)
    target_f = target.astype(jnp.float32)
    weight_f = weight_map.astype(jnp.float32)
    prediction_pile = []
    savings = []
    for sample_position in range(MEMBERS):
        sample_prediction, retained_intermediates = evaluate_sample_model(scaled_atmosphere_field, perturbation[sample_position], lattice_lift_matrix, mixing_rescale_factor, expand_matrix, contract_matrix, readout_matrix, intake_link_pairs, readout_link_pairs)
        prediction_pile.append(sample_prediction)
        savings.append(retained_intermediates)
    student_outputs = jnp.stack(prediction_pile)
    mesh_grads = []
    collected = ([], [], [], [])
    for sample_position in range(MEMBERS):
        teacher_terms = jnp.zeros_like(student_outputs[sample_position])
        own_terms = jnp.zeros_like(student_outputs[sample_position])
        for other in range(MEMBERS):
            teacher_terms = teacher_terms + slope(student_outputs[sample_position] - target_f[other])
            own_terms = own_terms + slope(student_outputs[sample_position] - student_outputs[other])
        pred_grad = weight_f * (teacher_terms - own_terms)
        state_b, up_part, down_part, dec_part, gain_part = member_backward(pred_grad, savings[sample_position], mixing_rescale_factor, expand_matrix, contract_matrix, readout_matrix, readout_link_pairs)
        mesh_grads.append(state_b)
        for holder, piece in zip(collected, (up_part, down_part, dec_part, gain_part)):
            holder.append(piece)
    factor = 1.0 / math.sqrt(NMESH)
    return (student_outputs, jnp.stack(mesh_grads), jnp.stack(collected[0]) * factor, jnp.stack(collected[1]) * factor, jnp.stack(collected[2]) * factor, jnp.stack(collected[3]) * factor)
```

```python
import math

import jax
import jax.numpy as jnp
from jax import lax
from jax.sharding import PartitionSpec as P

MESH_DEV = 256


smooth_sq = 0.01
norm_eps = 1e-05

bf16 = jnp.bfloat16
f32 = jnp.float32


def slope(diff):
    return diff * lax.rsqrt(diff * diff + smooth_sq)


def mm(a, b, ca, cb):
    return lax.dot_general(a, b, (((ca,), (cb,)), ((), ())), preferred_element_type=f32)


def split3(x):
    hi = x.astype(bf16)
    return hi, (x - hi.astype(f32)).astype(bf16)


def mm2(a, b, ca, cb):
    hi, lo = split3(a)
    return mm(hi, b, ca, cb) + mm(lo, b, ca, cb)


def exchange(x, band_count):
    rows, width = x.shape
    y = lax.all_to_all(
        x.reshape(band_count, rows // band_count, width), "band", split_axis=0, concat_axis=0, tiled=True
    )
    return y.reshape(rows, width)


def sum_over_bands(x, band_count):
    rows, width = x.shape
    parts = lax.all_to_all(
        x.astype(bf16).reshape(band_count, rows // band_count, width),
        "band",
        split_axis=0,
        concat_axis=0,
        tiled=True,
    )
    own = jnp.sum(parts.astype(f32), axis=0).astype(bf16)
    spread = jnp.broadcast_to(own[None], parts.shape)
    full = lax.all_to_all(spread, "band", split_axis=0, concat_axis=0, tiled=True)
    return full.reshape(rows, width).astype(f32)


def body(
    scaled_atmosphere_field,
    perturbation,
    target,
    weight_map,
    enc_send,
    enc_recv,
    dec_send,
    dec_recv,
    lattice_lift_matrix,
    mixing_rescale_factor,
    expand_matrix,
    contract_matrix,
    readout_matrix,
):
    band_count = lax.axis_size("band")
    channels, grid_rows = scaled_atmosphere_field.shape
    node_rows = MESH_DEV
    cell_ids = jnp.arange(grid_rows, dtype=jnp.int32)
    node_ids = jnp.arange(node_rows, dtype=jnp.int32)
    inputs_b = (scaled_atmosphere_field + perturbation[0].astype(f32)).astype(bf16)
    picker = (enc_send[0].reshape(-1)[:, None] == cell_ids[None, :]).astype(bf16)
    outgoing = mm(picker, inputs_b, 1, 1).astype(bf16)
    arrived = exchange(outgoing, band_count)
    slot_rows = jax.nn.silu(mm(arrived, lattice_lift_matrix, 1, 0)).astype(bf16)
    landing = (node_ids[:, None] == enc_recv[0].reshape(-1)[None, :]).astype(bf16)
    edge_count = jnp.sum(landing.astype(f32), axis=1, keepdims=True)
    mesh_state = mm(landing, slot_rows, 1, 0) / jnp.maximum(edge_count, 1.0)
    recip = lax.rsqrt(jnp.mean(mesh_state * mesh_state, axis=1, keepdims=True) + norm_eps)
    normed_b = (mesh_state * recip * mixing_rescale_factor).astype(bf16)
    hidden_pre = mm(normed_b, expand_matrix, 1, 0)
    hidden_b = jax.nn.silu(hidden_pre).astype(bf16)
    next_b = (mesh_state + mm(hidden_b, contract_matrix, 1, 0)).astype(bf16)
    mesh_picker = (dec_send[0].reshape(-1)[:, None] == node_ids[None, :]).astype(bf16)
    fill_map = (cell_ids[:, None] == dec_recv[0].reshape(-1)[None, :]).astype(bf16)
    inverse = 1.0 / jnp.maximum(jnp.sum(fill_map.astype(f32), axis=1), 1.0)
    projected = mm(next_b, readout_matrix, 1, 0).astype(bf16)
    chosen = mm(mesh_picker, projected, 1, 0).astype(bf16)
    slot_values = exchange(chosen, band_count)
    grid_sum = mm(slot_values, fill_map, 0, 1)
    student_outputs = scaled_atmosphere_field + grid_sum * inverse[None, :]
    all_pred, all_target = (
        lax.all_gather(student_outputs[None], "member", axis=0, tiled=True),
        lax.all_gather(target, "member", axis=0, tiled=True),
    )
    teacher_terms = jnp.sum(slope(student_outputs[None] - all_target.astype(f32)), axis=0)
    own_terms = jnp.sum(slope(student_outputs[None] - all_pred), axis=0)
    pred_grad = weight_map.astype(f32) * (teacher_terms - own_terms)
    scaled = (pred_grad * inverse[None, :]).astype(bf16)
    slot_grad = mm(fill_map, scaled, 0, 1).astype(bf16)
    returned = exchange(slot_grad, band_count)
    node_grad = mm(mesh_picker, returned, 0, 0)
    next_grad = mm2(node_grad, readout_matrix, 1, 1)
    grad_hi, grad_lo = split3(node_grad)
    states = jnp.concatenate([next_b, hidden_b], axis=1)
    small = mm(states, grad_hi, 0, 0) + mm(states, grad_lo, 0, 0)
    hidden_grad = mm2(next_grad, contract_matrix, 1, 1)
    sigma = jax.nn.sigmoid(hidden_pre)
    pre_grad = hidden_grad * sigma * (1.0 + hidden_pre * (1.0 - sigma))
    pre_hi, pre_lo = split3(pre_grad)
    up_part = mm(normed_b, pre_hi, 0, 0) + mm(normed_b, pre_lo, 0, 0)
    normed_grad = mm(pre_hi, expand_matrix, 1, 1) + mm(pre_lo, expand_matrix, 1, 1)
    gain_part = jnp.sum(normed_grad * mesh_state * recip, axis=0)
    gained = normed_grad * mixing_rescale_factor
    state_grad = (
        next_grad
        + recip * gained
        - mesh_state
        * (recip * recip * recip)
        * jnp.mean(gained * mesh_state, axis=1, keepdims=True)
    )
    width = up_part.shape[0]
    factor = 1.0 / math.sqrt(band_count * node_rows)
    packed = jnp.concatenate(
        [up_part, small[:width], small[width:], gain_part[:, None]], axis=1
    )
    pad = -packed.shape[1] % 16
    packed = jnp.pad(packed, ((0, 0), (0, pad)))
    total = sum_over_bands(packed, band_count) * factor
    hid = up_part.shape[1]
    grad_up = total[:, :hid]
    grad_dec = total[:, hid : hid + channels]
    hid_sum = total[:, hid + channels : hid + 2 * channels]
    grad_gain = total[:, hid + 2 * channels]
    grad_down = mm2(hid_sum, readout_matrix, 1, 1)
    return (
        student_outputs[None],
        state_grad.astype(bf16)[None],
        grad_up[None],
        grad_down[None],
        grad_dec[None],
        grad_gain[None],
    )


def solution(mesh):
    return jax.shard_map(
        body,
        mesh=mesh,
        in_specs=(
            P(None, "band"),
            P("member", None, "band"),
            P("member", None, "band"),
            P(None, "band"),
            P("band", None, None),
            P("band", None, None),
            P("band", None, None),
            P("band", None, None),
            P(),
            P(),
            P(),
            P(),
            P(),
        ),
        out_specs=(
            P("member", None, "band"),
            P("member", "band", None),
            P("member", None, None),
            P("member", None, None),
            P("member", None, None),
            P("member", None),
        ),
        check_vma=False,
    )
```

```python
import functools
import math

import jax
import jax.numpy as jnp
from jax import lax
from jax.experimental import pallas as pl
from jax.experimental.pallas import tpu as pltpu
from jax.sharding import PartitionSpec as P

MESH_DEV = 256


smooth_sq = 0.01
norm_eps = 1e-05

bf16 = jnp.bfloat16
f32 = jnp.float32


def slope(diff):
    return diff * lax.rsqrt(diff * diff + smooth_sq)


def mm(a, b, ca, cb):
    return lax.dot_general(a, b, (((ca,), (cb,)), ((), ())), preferred_element_type=f32)


def split3(x):
    hi = x.astype(bf16)
    return hi, (x - hi.astype(f32)).astype(bf16)


def mm2(a, b, ca, cb):
    hi, lo = split3(a)
    return mm(hi, b, ca, cb) + mm(lo, b, ca, cb)


def exchange(x, band_count):
    rows, width = x.shape
    y = lax.all_to_all(
        x.reshape(band_count, rows // band_count, width), "band", split_axis=0, concat_axis=0, tiled=True
    )
    return y.reshape(rows, width)


def sum_over_bands(x, band_count):
    rows, width = x.shape
    parts = lax.all_to_all(
        x.astype(bf16).reshape(band_count, rows // band_count, width),
        "band",
        split_axis=0,
        concat_axis=0,
        tiled=True,
    )
    own = jnp.sum(parts.astype(f32), axis=0).astype(bf16)
    spread = jnp.broadcast_to(own[None], parts.shape)
    full = lax.all_to_all(spread, "band", split_axis=0, concat_axis=0, tiled=True)
    return full.reshape(rows, width).astype(f32)


TABLE_ROWS = 16
LANES = 128


def one_hot(a, b):
    return jnp.where(a == b, 1.0, 0.0).astype(bf16)


def sigmoid(v):
    return 0.5 + 0.5 * jnp.tanh(0.5 * v)


def table_rows(all_ref, bands, group, xy, s, table_at):
    mate = s * (bands // group) + xy
    return all_ref[mate, table_at : table_at + TABLE_ROWS, :].astype(f32)


def forward_kernel(
    group,
    channels,
    me_ref,
    all_ref,
    lift_ref,
    scale_ref,
    expand_ref,
    contract_ref,
    readout_ref,
    normed_ref,
    slope_ref,
    state_ref,
    own_ref,
    own_pre_ref,
    chosen_ref,
    slot_ref,
):
    bands = all_ref.shape[0]
    node_rows, width = normed_ref.shape[1], normed_ref.shape[2]
    slots = slot_ref.shape[1]
    cap = slots // bands
    z, xy = me_ref[0], me_ref[1]
    subs = lax.broadcasted_iota(jnp.int32, (node_rows, LANES), 0).astype(f32)

    def embed(b, carry):
        latent = mm(all_ref[b, 0:channels, :], lift_ref[...], 0, 0)
        latent = (latent * sigmoid(latent)).astype(bf16)
        slot_ref[:, pl.ds(pl.multiple_of(b * cap, cap), cap), :] = latent.reshape(group, cap, width)
        return carry

    lax.fori_loop(0, bands, embed, 0)

    def nodes(s, carry):
        table = table_rows(all_ref, bands, group, xy, s, channels)
        parts = slots // LANES
        hot = [jnp.where(subs == table[j : j + 1, :], 1.0, 0.0) for j in range(parts)]
        count = sum(jnp.sum(h, axis=1, keepdims=True) for h in hot)
        landing = jnp.concatenate(hot, axis=1).astype(bf16)
        state = mm(landing, slot_ref[s], 1, 0) / jnp.maximum(count, 1.0)
        recip = lax.rsqrt(jnp.mean(state * state, axis=1, keepdims=True) + norm_eps)
        normed = (state * recip * scale_ref[...]).astype(bf16)
        normed_ref[s] = normed
        pre = mm(normed, expand_ref[...], 1, 0)
        gate = sigmoid(pre)
        hidden = pre * gate
        slope_ref[s] = (gate + hidden * (1.0 - gate)).astype(bf16)
        hidden = hidden.astype(bf16)
        following = (state + mm(hidden, contract_ref[...], 1, 0)).astype(bf16)
        state_ref[s, :, 0:width] = following
        state_ref[s, :, width:] = hidden

        @pl.when(s == z)
        def _():
            own_ref[...] = state
            own_pre_ref[...] = pre
            projected = mm(following, readout_ref[...], 1, 0).astype(bf16)
            for j in range(parts):
                pick = one_hot(subs, table[parts + j : parts + j + 1, :])
                chosen_ref[j * LANES : (j + 1) * LANES, :] = mm(pick, projected, 0, 0).astype(bf16)

        return carry

    lax.fori_loop(0, group, nodes, 0)


def backward_kernel(
    group,
    channels,
    me_ref,
    grad_ref,
    all_ref,
    chain_ref,
    normed_ref,
    slope_ref,
    state_ref,
    own_ref,
    *rest,
):
    piece_refs, (value_ref, up_ref, small_ref) = rest[:-3], rest[-3:]
    bands = grad_ref.shape[0]
    slots = value_ref.shape[1]
    node_rows, width = normed_ref.shape[1], normed_ref.shape[2]
    cap = slots // bands
    z, xy = me_ref[0], me_ref[1]
    subs = lax.broadcasted_iota(jnp.int32, (node_rows, LANES), 0).astype(f32)

    def turn(b, carry):
        values = grad_ref[b].astype(f32).T.astype(bf16)
        value_ref[:, pl.ds(pl.multiple_of(b * cap, cap), cap), :] = values.reshape(group, cap, channels)
        return carry

    lax.fori_loop(0, bands, turn, 0)
    up_ref[...] = jnp.zeros_like(up_ref)
    small_ref[...] = jnp.zeros_like(small_ref)

    def nodes(s, carry):
        table = table_rows(all_ref, bands, group, xy, s, channels)
        parts = slots // LANES
        pick = jnp.concatenate(
            [one_hot(subs, table[parts + j : parts + j + 1, :]) for j in range(parts)], axis=1
        )
        node_grad = mm(pick, value_ref[s], 1, 0)

        @pl.when(s == z)
        def _():
            own_ref[...] = node_grad

        node_b = node_grad.astype(bf16)
        pre = (mm(node_b, chain_ref[...], 1, 1) * slope_ref[s].astype(f32)).astype(bf16)
        up_ref[...] += mm(normed_ref[s], pre, 0, 0)
        small_ref[...] += mm(node_b, state_ref[s], 0, 0)
        return carry

    lax.fori_loop(0, group, nodes, 0)
    count = len(piece_refs)
    rows = up_ref.shape[0] // count
    half = up_ref.shape[1] // 2
    lanes = small_ref.shape[1] // count
    for p, piece_ref in enumerate(piece_refs):
        to = xy ^ p
        at = pl.ds(pl.multiple_of(to * rows, rows), rows)
        piece_ref[0:rows, :] = up_ref[at, 0:half].astype(bf16)
        piece_ref[rows : 2 * rows, :] = up_ref[at, half:].astype(bf16)
        piece_ref[2 * rows :, :] = small_ref[:, pl.ds(pl.multiple_of(to * lanes, lanes), lanes)].astype(bf16)


def finish_kernel(factor, channels, me_ref, scale_ref, expand_ref, readout_ref, *rest):
    count = len(rest) - 5
    piece_refs, (up_ref, down_ref, dec_ref, gain_ref, small_ref) = rest[:count], rest[count:]
    rows = up_ref.shape[0] // count
    half = up_ref.shape[1] // 2
    lanes = small_ref.shape[1] // count
    for p, piece_ref in enumerate(piece_refs):
        to = me_ref[1] ^ p
        at = pl.ds(pl.multiple_of(to * rows, rows), rows)
        left = piece_ref[0:rows, :].astype(f32) * factor
        right = piece_ref[rows : 2 * rows, :].astype(f32) * factor
        up_ref[at, 0:half] = left
        up_ref[at, half:] = right
        small_ref[:, pl.ds(pl.multiple_of(to * lanes, lanes), lanes)] = piece_ref[2 * rows :, :].astype(f32) * factor
        gain = jnp.sum(left * expand_ref[at, 0:half].astype(f32), axis=1, keepdims=True)
        gain = gain + jnp.sum(right * expand_ref[at, half:].astype(f32), axis=1, keepdims=True)
        gain_ref[at, :] = gain / scale_ref[at, :]
    width = up_ref.shape[0]
    dec_ref[...] = small_ref[:, 0:width].T
    hidden = small_ref[:, width:]
    high = hidden.astype(bf16)
    low = (hidden - high.astype(f32)).astype(bf16)
    down_ref[...] = mm(high, readout_ref[...], 0, 1) + mm(low, readout_ref[...], 0, 1)


def vmem_call(kernel, outs, name, scratch=(), budget=16):
    vmem = pl.BlockSpec(memory_space=pltpu.VMEM)
    smem = pl.BlockSpec(memory_space=pltpu.SMEM)

    def call(scalars, *operands):
        return pl.pallas_call(
            kernel,
            out_shape=[jax.ShapeDtypeStruct(s, d) for s, d in outs],
            in_specs=[smem] + [vmem] * len(operands),
            out_specs=[vmem] * len(outs),
            scratch_shapes=[pltpu.VMEM(s, d) for s, d in scratch],
            compiler_params=pltpu.CompilerParams(vmem_limit_bytes=budget * 2**20),
            name=name,
        )(scalars, *operands)

    return call


def to_column(x, bands, group):
    channels = x.shape[0]
    blocks = x.reshape(channels, bands // group, -1).transpose(1, 0, 2)
    return jnp.broadcast_to(blocks[None], (group,) + blocks.shape).reshape(bands, channels, -1)


def by_column(table, group):
    bands, cap = table.shape
    return table.reshape(group, bands // group, cap).transpose(1, 0, 2).reshape(-1)


def all_to_all(x):
    return lax.all_to_all(x, "band", split_axis=0, concat_axis=0, tiled=True)


def member_terms(student_outputs, target, weight_map):
    all_pred, all_target = (
        lax.all_gather(student_outputs[None], "member", axis=0, tiled=True),
        lax.all_gather(target, "member", axis=0, tiled=True),
    )
    teacher_terms = jnp.sum(slope(student_outputs[None] - all_target.astype(f32)), axis=0)
    own_terms = jnp.sum(slope(student_outputs[None] - all_pred), axis=0)
    return weight_map.astype(f32) * (teacher_terms - own_terms)


def state_gradient(node_grad, mesh_state, hidden_pre, scale, expand, contract, readout):
    recip = lax.rsqrt(jnp.mean(mesh_state * mesh_state, axis=1, keepdims=True) + norm_eps)
    next_grad = mm2(node_grad, readout, 1, 1)
    hidden_grad = mm2(next_grad, contract, 1, 1)
    sigma = jax.nn.sigmoid(hidden_pre)
    pre_grad = hidden_grad * sigma * (1.0 + hidden_pre * (1.0 - sigma))
    normed_grad = mm2(pre_grad, expand, 1, 1)
    gained = normed_grad * scale
    return (
        next_grad
        + recip * gained
        - mesh_state * (recip * recip * recip) * jnp.mean(gained * mesh_state, axis=1, keepdims=True)
    ).astype(bf16)


def column_body(
    group,
    scaled_atmosphere_field,
    perturbation,
    target,
    weight_map,
    enc_send,
    enc_recv,
    dec_send,
    dec_recv,
    lattice_lift_matrix,
    mixing_rescale_factor,
    expand_matrix,
    contract_matrix,
    readout_matrix,
):
    bands = lax.axis_size("band")
    channels, grid_rows = scaled_atmosphere_field.shape
    node_rows = MESH_DEV
    width, hid = expand_matrix.shape
    slots = bands * enc_send.shape[2]
    crew = bands // group
    band = lax.axis_index("band").astype(jnp.int32)
    me = jnp.stack([band // crew, band % crew])
    cell_ids = jnp.arange(grid_rows, dtype=jnp.int32)
    inputs_b = (scaled_atmosphere_field + perturbation[0].astype(f32)).astype(bf16)
    picker = (cell_ids[:, None] == by_column(enc_send[0], group)[None, :]).astype(bf16)
    outgoing = to_column(mm(inputs_b, picker, 1, 0).astype(bf16), bands, group)
    tables = jnp.concatenate([enc_recv[0].reshape(-1, LANES), dec_send[0].reshape(-1, LANES)]).astype(bf16)
    tables = jnp.pad(tables, ((0, TABLE_ROWS - tables.shape[0]), (0, 0)))
    tables = jnp.broadcast_to(tables[None], (bands,) + tables.shape)
    arrived = all_to_all(jnp.concatenate([outgoing, tables], axis=1))
    normed, slopes, states, mesh_state, hidden_pre, chosen = vmem_call(
        functools.partial(forward_kernel, group, channels),
        [
            ((group, node_rows, width), bf16),
            ((group, node_rows, hid), bf16),
            ((group, node_rows, width + hid), bf16),
            ((node_rows, width), f32),
            ((node_rows, hid), f32),
            ((slots, channels), bf16),
        ],
        "forward",
        scratch=[((group, slots, width), bf16)],
    )(
        me,
        arrived,
        lattice_lift_matrix,
        mixing_rescale_factor[None, :],
        expand_matrix,
        contract_matrix,
        readout_matrix,
    )
    chain = mm(contract_matrix, readout_matrix, 1, 0).astype(bf16)
    slot_values = exchange(chosen, bands)
    fill_map = (cell_ids[:, None] == dec_recv[0].reshape(-1)[None, :]).astype(bf16)
    inverse = 1.0 / jnp.maximum(jnp.sum(fill_map.astype(f32), axis=1), 1.0)
    student_outputs = scaled_atmosphere_field + mm(slot_values, fill_map, 0, 1) * inverse[None, :]
    pred_grad = member_terms(student_outputs, target, weight_map)
    scaled = (pred_grad * inverse[None, :]).astype(bf16)
    spread_map = (cell_ids[:, None] == by_column(dec_recv[0], group)[None, :]).astype(bf16)
    returned = all_to_all(to_column(mm(scaled, spread_map, 1, 0).astype(bf16), bands, group))
    piece_rows = 2 * (width // crew) + channels
    node_grad, *pieces = vmem_call(
        functools.partial(backward_kernel, group, channels),
        [((node_rows, channels), f32)] + [((piece_rows, hid // 2), bf16)] * crew,
        "backward",
        scratch=[
            ((group, slots, channels), bf16),
            ((width, hid), f32),
            ((channels, width + hid), f32),
        ],
    )(me, returned, arrived, chain, normed, slopes, states)
    swaps = [[(i, i ^ p) for i in range(bands)] for p in range(1, crew)]
    others = [lax.ppermute(piece, "band", swap) for piece, swap in zip(pieces[1:], swaps)]
    total = sum(x.astype(f32) for x in [pieces[0]] + others).astype(bf16)
    totals = [total] + [lax.ppermute(total, "band", swap) for swap in swaps]
    state_grad = state_gradient(
        node_grad, mesh_state, hidden_pre, mixing_rescale_factor, expand_matrix, contract_matrix, readout_matrix
    )
    factor = 1.0 / math.sqrt(bands * node_rows)
    grad_up, grad_down, grad_dec, grad_gain = vmem_call(
        functools.partial(finish_kernel, factor, channels),
        [((width, hid), f32), ((hid, width), f32), ((width, channels), f32), ((width, 1), f32)],
        "finish",
        scratch=[((channels, width + hid), f32)],
    )(me, mixing_rescale_factor[:, None], expand_matrix, readout_matrix, *totals)
    return (
        student_outputs[None],
        state_grad[None],
        grad_up[None],
        grad_down[None],
        grad_dec[None],
        grad_gain[:, 0][None],
    )


def band_body(
    scaled_atmosphere_field,
    perturbation,
    target,
    weight_map,
    enc_send,
    enc_recv,
    dec_send,
    dec_recv,
    lattice_lift_matrix,
    mixing_rescale_factor,
    expand_matrix,
    contract_matrix,
    readout_matrix,
):
    band_count = lax.axis_size("band")
    channels, grid_rows = scaled_atmosphere_field.shape
    node_rows = MESH_DEV
    cell_ids = jnp.arange(grid_rows, dtype=jnp.int32)
    node_ids = jnp.arange(node_rows, dtype=jnp.int32)
    inputs_b = (scaled_atmosphere_field + perturbation[0].astype(f32)).astype(bf16)
    picker = (enc_send[0].reshape(-1)[:, None] == cell_ids[None, :]).astype(bf16)
    outgoing = mm(picker, inputs_b, 1, 1).astype(bf16)
    arrived = exchange(outgoing, band_count)
    slot_rows = jax.nn.silu(mm(arrived, lattice_lift_matrix, 1, 0)).astype(bf16)
    landing = (node_ids[:, None] == enc_recv[0].reshape(-1)[None, :]).astype(bf16)
    edge_count = jnp.sum(landing.astype(f32), axis=1, keepdims=True)
    mesh_state = mm(landing, slot_rows, 1, 0) / jnp.maximum(edge_count, 1.0)
    recip = lax.rsqrt(jnp.mean(mesh_state * mesh_state, axis=1, keepdims=True) + norm_eps)
    normed_b = (mesh_state * recip * mixing_rescale_factor).astype(bf16)
    hidden_pre = mm(normed_b, expand_matrix, 1, 0)
    hidden_b = jax.nn.silu(hidden_pre).astype(bf16)
    next_b = (mesh_state + mm(hidden_b, contract_matrix, 1, 0)).astype(bf16)
    mesh_picker = (dec_send[0].reshape(-1)[:, None] == node_ids[None, :]).astype(bf16)
    fill_map = (cell_ids[:, None] == dec_recv[0].reshape(-1)[None, :]).astype(bf16)
    inverse = 1.0 / jnp.maximum(jnp.sum(fill_map.astype(f32), axis=1), 1.0)
    projected = mm(next_b, readout_matrix, 1, 0).astype(bf16)
    chosen = mm(mesh_picker, projected, 1, 0).astype(bf16)
    slot_values = exchange(chosen, band_count)
    grid_sum = mm(slot_values, fill_map, 0, 1)
    student_outputs = scaled_atmosphere_field + grid_sum * inverse[None, :]
    pred_grad = member_terms(student_outputs, target, weight_map)
    scaled = (pred_grad * inverse[None, :]).astype(bf16)
    slot_grad = mm(fill_map, scaled, 0, 1).astype(bf16)
    returned = exchange(slot_grad, band_count)
    node_grad = mm(mesh_picker, returned, 0, 0)
    grad_hi, grad_lo = split3(node_grad)
    states = jnp.concatenate([next_b, hidden_b], axis=1)
    small = mm(states, grad_hi, 0, 0) + mm(states, grad_lo, 0, 0)
    hidden_grad = mm2(mm2(node_grad, readout_matrix, 1, 1), contract_matrix, 1, 1)
    sigma = jax.nn.sigmoid(hidden_pre)
    pre_hi, pre_lo = split3(hidden_grad * sigma * (1.0 + hidden_pre * (1.0 - sigma)))
    up_part = mm(normed_b, pre_hi, 0, 0) + mm(normed_b, pre_lo, 0, 0)
    state_grad = state_gradient(
        node_grad, mesh_state, hidden_pre, mixing_rescale_factor, expand_matrix, contract_matrix, readout_matrix
    )
    width, hid = up_part.shape
    factor = 1.0 / math.sqrt(band_count * node_rows)
    packed = jnp.concatenate([up_part, small[:width], small[width:]], axis=1)
    packed = jnp.pad(packed, ((0, 0), (0, -packed.shape[1] % 16)))
    total = sum_over_bands(packed, band_count) * factor
    grad_up = total[:, :hid]
    grad_dec = total[:, hid : hid + channels]
    grad_down = mm2(total[:, hid + channels : hid + 2 * channels], readout_matrix, 1, 1)
    grad_gain = jnp.sum(grad_up * expand_matrix.astype(f32), axis=1) / mixing_rescale_factor
    return (
        student_outputs[None],
        state_grad[None],
        grad_up[None],
        grad_down[None],
        grad_dec[None],
        grad_gain[None],
    )


def body(*args):
    field, enc_send, dec_send, expand = args[0], args[4], args[6], args[10]
    bands, cap = enc_send.shape[1:]
    channels, grid_rows = field.shape
    group = LANES // cap
    column = (
        dec_send.shape[2] == cap
        and LANES % cap == 0
        and cap % 16 == 0
        and group * group == bands
        and channels % 16 == 0
        and max(grid_rows, MESH_DEV) <= 256
        and bands * cap * 2 <= TABLE_ROWS * LANES
        and expand.shape[0] == expand.shape[1]
    )
    return column_body(group, *args) if column else band_body(*args)


def solution(mesh):
    return jax.shard_map(
        body,
        mesh=mesh,
        in_specs=(
            P(None, "band"),
            P("member", None, "band"),
            P("member", None, "band"),
            P(None, "band"),
            P("band", None, None),
            P("band", None, None),
            P("band", None, None),
            P("band", None, None),
            P(),
            P(),
            P(),
            P(),
            P(),
        ),
        out_specs=(
            P("member", None, "band"),
            P("member", "band", None),
            P("member", None, None),
            P("member", None, None),
            P("member", None, None),
            P("member", None),
        ),
        check_vma=False,
    )
```

```python
import functools
import math

import jax
import jax.numpy as jnp
from jax import lax
from jax.experimental import pallas as pl
from jax.experimental.pallas import tpu as pltpu
from jax.sharding import PartitionSpec as P

MESH_DEV = 256


smooth_sq = 0.01
norm_eps = 1e-05

bf16 = jnp.bfloat16
f32 = jnp.float32


def slope(diff):
    return diff * lax.rsqrt(diff * diff + smooth_sq)


def mm(a, b, ca, cb):
    return lax.dot_general(a, b, (((ca,), (cb,)), ((), ())), preferred_element_type=f32)


def split3(x):
    hi = x.astype(bf16)
    return hi, (x - hi.astype(f32)).astype(bf16)


def mm2(a, b, ca, cb):
    hi, lo = split3(a)
    return mm(hi, b, ca, cb) + mm(lo, b, ca, cb)


def exchange(x, band_count):
    rows, width = x.shape
    y = lax.all_to_all(
        x.reshape(band_count, rows // band_count, width), "band", split_axis=0, concat_axis=0, tiled=True
    )
    return y.reshape(rows, width)


def sum_over_bands(x, band_count):
    rows, width = x.shape
    parts = lax.all_to_all(
        x.astype(bf16).reshape(band_count, rows // band_count, width),
        "band",
        split_axis=0,
        concat_axis=0,
        tiled=True,
    )
    own = jnp.sum(parts.astype(f32), axis=0).astype(bf16)
    spread = jnp.broadcast_to(own[None], parts.shape)
    full = lax.all_to_all(spread, "band", split_axis=0, concat_axis=0, tiled=True)
    return full.reshape(rows, width).astype(f32)


TABLE_ROWS = 16
LANES = 128


def one_hot(a, b):
    return jnp.where(a == b, 1.0, 0.0).astype(bf16)


def sigmoid(v):
    return 0.5 + 0.5 * jnp.tanh(0.5 * v)


def table_rows(all_ref, bands, group, xy, s, table_at):
    mate = s * (bands // group) + xy
    return all_ref[mate, table_at : table_at + TABLE_ROWS, :].astype(f32)


def lane_blocks(table, group, rows, row_of):
    bands, cap = table.shape
    r = lax.broadcasted_iota(jnp.int32, (rows, bands), 0)
    b = lax.broadcasted_iota(jnp.int32, (rows, bands), 1)
    slot = lax.broadcasted_iota(jnp.int32, (cap, LANES), 0)
    lane = lax.broadcasted_iota(jnp.int32, (cap, LANES), 1)
    out = jnp.zeros((rows, LANES), f32)
    for j in range(group):
        rows_j = mm(jnp.where(row_of(r, j) == b, 1.0, 0.0).astype(bf16), table, 1, 0).astype(bf16)
        out = out + mm(rows_j, one_hot(lane, slot + j * cap), 1, 0)
    return out


def column_order(table_ref, group):
    table = table_ref[0].astype(f32).astype(bf16)
    crew = table.shape[0] // group
    return lane_blocks(table, group, 8, lambda r, j: jnp.where(r < crew, j * crew + r, -1)), crew


def send_copies(group, crew, block_ref, out_ref, sems):
    return [
        pltpu.make_async_copy(block_ref, out_ref.at[j * crew : (j + 1) * crew], sems.at[j]) for j in range(group)
    ]


def encode_kernel(group, ready, field_ref, noise_ref, send_ref, recv_ref, mesh_ref, out_ref, block_ref, sems):
    channels, grid_rows = field_ref.shape
    ready(0, 1, 2, 3, 4)
    inputs = (field_ref[...] + noise_ref[0].astype(f32)).astype(bf16) * 0.5
    order, crew = column_order(send_ref, group)
    subs = lax.broadcasted_iota(jnp.int32, (grid_rows, LANES), 0).astype(f32)
    bands = recv_ref.shape[1]
    rows = bands // group
    recv = recv_ref[0].astype(f32).astype(bf16)
    mesh = mesh_ref[0].astype(f32).astype(bf16)
    table = lane_blocks(recv, group, TABLE_ROWS, lambda r, j: jnp.where(r < rows, r * group + j, -1))
    table = table + lane_blocks(
        mesh,
        group,
        TABLE_ROWS,
        lambda r, j: jnp.where((r >= rows) & (r < 2 * rows), (r - rows) * group + j, -1),
    )
    for c in range(crew):
        pick = one_hot(subs, order[c : c + 1, :])
        block_ref[c, 0:channels, :] = mm(inputs, pick, 1, 0).astype(bf16)
        block_ref[c, channels:, :] = table.astype(bf16)
    copies = send_copies(group, crew, block_ref, out_ref, sems)
    for copy in copies:
        copy.start()
    for copy in copies:
        copy.wait()


def loss_kernel(
    group, student_ref, pred_ref, target_ref, weight_ref, inverse_ref, recv_ref, out_ref, block_ref, sems
):
    grid_rows = student_ref.shape[1]
    student = student_ref[...]
    terms = jnp.zeros_like(student)
    for j in range(pred_ref.shape[0]):
        terms = terms + slope(student - target_ref[j].astype(f32)) - slope(student - pred_ref[j])
    scaled = (weight_ref[...].astype(f32) * terms * inverse_ref[...]).astype(bf16)
    order, crew = column_order(recv_ref, group)
    subs = lax.broadcasted_iota(jnp.int32, (grid_rows, LANES), 0).astype(f32)
    for c in range(crew):
        block_ref[c] = mm(scaled, one_hot(subs, order[c : c + 1, :]), 1, 0).astype(bf16)
    copies = send_copies(group, crew, block_ref, out_ref, sems)
    for copy in copies:
        copy.start()
    for copy in copies:
        copy.wait()


def forward_kernel(
    group,
    channels,
    ready,
    me_ref,
    all_ref,
    lift_ref,
    scale_ref,
    expand_ref,
    contract_ref,
    readout_ref,
    normed_ref,
    slope_ref,
    state_ref,
    own_ref,
    own_pre_ref,
    chosen_ref,
    table_ref,
    slot_ref,
    normed_buf,
    slope_buf,
    state_buf,
    own_buf,
    own_pre_buf,
    sems,
    own_sems,
):
    bands = all_ref.shape[0]
    node_rows, width = normed_ref.shape[1], normed_ref.shape[2]
    slots = slot_ref.shape[1]
    cap = slots // bands
    z, xy = me_ref[0], me_ref[1]
    subs = lax.broadcasted_iota(jnp.int32, (node_rows, LANES), 0).astype(f32)

    def embed(b, carry):
        latent = mm(all_ref[b, 0:channels, :], lift_ref[...], 0, 0)
        latent = (latent + latent * jnp.tanh(latent)).astype(bf16)
        slot_ref[:, pl.ds(pl.multiple_of(b * cap, cap), cap), :] = latent.reshape(group, cap, width)
        return carry

    lax.fori_loop(0, bands, embed, 0, unroll=4)
    ready(2, 3, 4, 5)
    kept = [(normed_buf, normed_ref), (slope_buf, slope_ref), (state_buf, state_ref)]
    own_copies = [
        pltpu.make_async_copy(own_buf, own_ref, own_sems.at[0]),
        pltpu.make_async_copy(own_pre_buf, own_pre_ref, own_sems.at[1]),
    ]

    def copies(s):
        return [pltpu.make_async_copy(a.at[s], b.at[s], sems.at[i, s]) for i, (a, b) in enumerate(kept)]

    def nodes(i, carry):
        s = lax.rem(z + i, group)
        table = table_rows(all_ref, bands, group, xy, s, channels)
        table_ref[s] = table
        parts = slots // LANES
        landing = jnp.concatenate([one_hot(subs, table[j : j + 1, :]) for j in range(parts)], axis=1)
        count = mm(landing, jnp.ones((slots, LANES), bf16), 1, 0)[:, 0:1]
        state = mm(landing, slot_ref[s], 1, 0) * (1.0 / jnp.maximum(count, 1.0))
        recip = lax.rsqrt(jnp.mean(state * state, axis=1, keepdims=True) + norm_eps)
        normed = (state * recip * scale_ref[...]).astype(bf16)
        normed_buf[s] = normed
        pre = mm(normed, expand_ref[...], 1, 0)
        bent = jnp.tanh(pre)
        above = 1.0 + bent
        slope_buf[s] = (above * (1.0 + pre * (1.0 - bent))).astype(bf16)
        hidden = (pre * above).astype(bf16)
        following = (state + mm(hidden, contract_ref[...], 1, 0)).astype(bf16)
        state_buf[s, :, 0:width] = following
        state_buf[s, :, width:] = hidden
        for copy in copies(s):
            copy.start()

        @pl.when(i == 0)
        def _():
            own_buf[...] = state
            own_pre_buf[...] = pre
            for copy in own_copies:
                copy.start()
            projected = mm(following, readout_ref[...], 1, 1).astype(bf16)
            for j in range(parts):
                pick = one_hot(subs, table[parts + j : parts + j + 1, :])
                chosen_ref[j * LANES : (j + 1) * LANES, :] = mm(pick, projected, 0, 0).astype(bf16)

        return carry

    lax.fori_loop(0, group, nodes, 0)
    for copy in own_copies:
        copy.wait()
    for s in range(group):
        for copy in copies(s):
            copy.wait()


def backward_kernel(
    group,
    channels,
    me_ref,
    grad_ref,
    table_ref,
    chain_ref,
    normed_ref,
    slope_ref,
    state_ref,
    own_ref,
    *rest,
):
    piece_refs, (value_ref, node_ref, up_ref, small_ref, normed_buf, slope_buf, state_buf, sems) = rest[:-8], rest[-8:]
    bands = grad_ref.shape[0]
    slots = value_ref.shape[1]
    node_rows, width = normed_ref.shape[1], normed_ref.shape[2]
    cap = slots // bands
    z, xy = me_ref[0], me_ref[1]
    subs = lax.broadcasted_iota(jnp.int32, (node_rows, LANES), 0).astype(f32)
    kept = [(slope_ref, slope_buf), (normed_ref, normed_buf), (state_ref, state_buf)]

    def copies(s):
        return [pltpu.make_async_copy(a.at[s], b.at[s], sems.at[i, s]) for i, (a, b) in enumerate(kept)]

    for s in range(group):
        for copy in copies(s):
            copy.start()

    def turn(b, carry):
        values = grad_ref[b].astype(f32).T.astype(bf16)
        value_ref[:, pl.ds(pl.multiple_of(b * cap, cap), cap), :] = values.reshape(group, cap, channels)
        return carry

    lax.fori_loop(0, bands, turn, 0, unroll=4)

    def nodes(s, carry):
        table = table_ref[s]
        parts = slots // LANES
        pick = jnp.concatenate(
            [one_hot(subs, table[parts + j : parts + j + 1, :]) for j in range(parts)], axis=1
        )
        node_grad = mm(pick, value_ref[s], 1, 0)

        @pl.when(s == z)
        def _():
            own_ref[...] = node_grad

        node_b = node_grad.astype(bf16)
        at = pl.ds(pl.multiple_of(s * node_rows, node_rows), node_rows)
        node_ref[at, :] = node_b
        copies(s)[0].wait()
        pre = mm(node_b, chain_ref[...], 1, 0)
        slope_buf[s] = (pre * slope_buf[s].astype(f32)).astype(bf16)
        return carry

    lax.fori_loop(0, group, nodes, 0)
    for s in range(group):
        for copy in copies(s)[1:]:
            copy.wait()
    everything = (group * node_rows, -1)
    up_ref[...] = 2.0 * mm(normed_buf[...].reshape(everything), slope_buf[...].reshape(everything), 0, 0)
    small_ref[...] = mm(node_ref[...], state_buf[...].reshape(everything), 0, 0)
    count = len(piece_refs)
    rows = up_ref.shape[0] // count
    half = up_ref.shape[1] // 2
    lanes = small_ref.shape[1] // count
    for p, piece_ref in enumerate(piece_refs):
        to = xy ^ p
        at = pl.ds(pl.multiple_of(to * rows, rows), rows)
        piece_ref[0:rows, :] = up_ref[at, 0:half].astype(bf16)
        piece_ref[rows : 2 * rows, :] = up_ref[at, half:].astype(bf16)
        piece_ref[2 * rows :, :] = small_ref[:, pl.ds(pl.multiple_of(to * lanes, lanes), lanes)].astype(bf16)


def finish_kernel(factor, channels, me_ref, scale_ref, expand_ref, readout_ref, *rest):
    count = len(rest) - 8
    piece_refs = rest[:count]
    up_out, down_out, dec_ref, gain_ref, small_ref, up_ref, down_ref, sems = rest[count:]
    rows = up_ref.shape[0] // count
    half = up_ref.shape[1] // 2
    lanes = small_ref.shape[1] // count
    width = up_ref.shape[0]
    places = [pl.ds(pl.multiple_of((me_ref[1] ^ p) * rows, rows), rows) for p in range(count)]
    up_copies = [pltpu.make_async_copy(up_ref.at[at], up_out.at[at], sems.at[0, p]) for p, at in enumerate(places)]
    down_copies = [
        pltpu.make_async_copy(down_ref.at[at], down_out.at[at], sems.at[1, p])
        for p, at in enumerate(pl.ds(p * rows, rows) for p in range(count))
    ]
    for p, piece_ref in enumerate(piece_refs):
        up_ref[places[p], 0:half] = piece_ref[0:rows, :].astype(f32) * factor
        up_ref[places[p], half:] = piece_ref[rows : 2 * rows, :].astype(f32) * factor
        up_copies[p].start()
        at = pl.ds(pl.multiple_of((me_ref[1] ^ p) * lanes, lanes), lanes)
        small_ref[:, at] = piece_ref[2 * rows :, :].astype(f32) * factor
    high = small_ref[:, width:].astype(bf16)
    low = (small_ref[:, width:] - high.astype(f32)).astype(bf16)
    for p in range(count):
        at = slice(p * rows, (p + 1) * rows)
        down_ref[at, :] = mm(high[:, at], readout_ref[...], 0, 0) + mm(low[:, at], readout_ref[...], 0, 0)
        down_copies[p].start()
    dec_ref[...] = small_ref[:, 0:width]
    for at in places:
        gain = up_ref[at, :] * expand_ref[at, :].astype(f32)
        gain = sum(gain[:, j : j + LANES] for j in range(0, 2 * half, LANES))
        gain_ref[:, at] = jnp.sum(gain.T, axis=0, keepdims=True) / scale_ref[:, at]
    for copy in up_copies + down_copies:
        copy.wait()


def vmem_call(kernel, outs, name, scratch=(), sems=(), budget=24, left_in=(), left_out=(), fetched=()):
    vmem = pl.BlockSpec(memory_space=pltpu.VMEM)
    smem = pl.BlockSpec(memory_space=pltpu.SMEM)
    left = pl.BlockSpec(memory_space=pltpu.HBM)
    fetched = list(fetched)

    def call(scalars, *operands):
        first = 0 if scalars is None else 1
        outside = set(left_in) | set(fetched)

        def run(*refs):
            refs = list(refs)
            if fetched:
                bufs, sem = refs[-1 - len(fetched) : -1], refs[-1]
                refs = refs[: -1 - len(fetched)]
                copies = {
                    at: pltpu.make_async_copy(refs[first + at], buf, sem.at[i])
                    for i, (at, buf) in enumerate(zip(fetched, bufs))
                }
                for at, buf in zip(fetched, bufs):
                    copies[at].start()
                    refs[first + at] = buf

                def ready(*which):
                    for at in which:
                        copies[at].wait()

                kernel(ready, *refs)
            else:
                kernel(*refs)

        return pl.pallas_call(
            run,
            out_shape=[(pltpu.HBM if i in left_out else jax.ShapeDtypeStruct)(s, d) for i, (s, d) in enumerate(outs)],
            in_specs=[smem] * first + [left if i in outside else vmem for i in range(len(operands))],
            out_specs=[left if i in left_out else vmem for i in range(len(outs))],
            scratch_shapes=[pltpu.VMEM(s, d) for s, d in scratch]
            + [pltpu.SemaphoreType.DMA(s) for s in sems]
            + [pltpu.VMEM(operands[i].shape, operands[i].dtype) for i in fetched]
            + ([pltpu.SemaphoreType.DMA((len(fetched),))] if fetched else []),
            compiler_params=pltpu.CompilerParams(vmem_limit_bytes=budget * 2**20),
            name=name,
        )(
            *([] if scalars is None else [scalars]),
            *[pltpu.with_memory_space_constraint(x, pltpu.HBM) if i in outside else x for i, x in enumerate(operands)],
        )

    return call


def all_to_all(x):
    return lax.all_to_all(x, "band", split_axis=0, concat_axis=0, tiled=True)


def member_terms(student_outputs, target, weight_map):
    all_pred, all_target = (
        lax.all_gather(student_outputs[None], "member", axis=0, tiled=True),
        lax.all_gather(target, "member", axis=0, tiled=True),
    )
    teacher_terms = jnp.sum(slope(student_outputs[None] - all_target.astype(f32)), axis=0)
    own_terms = jnp.sum(slope(student_outputs[None] - all_pred), axis=0)
    return weight_map.astype(f32) * (teacher_terms - own_terms)


def state_gradient(node_grad, mesh_state, hidden_pre, scale, expand, contract, readout):
    recip = lax.rsqrt(jnp.mean(mesh_state * mesh_state, axis=1, keepdims=True) + norm_eps)
    next_grad = mm2(node_grad, readout, 1, 1)
    hidden_grad = mm2(next_grad, contract, 1, 1)
    sigma = jax.nn.sigmoid(hidden_pre)
    pre_grad = hidden_grad * sigma * (1.0 + hidden_pre * (1.0 - sigma))
    normed_grad = mm2(pre_grad, expand, 1, 1)
    gained = normed_grad * scale
    return (
        next_grad
        + recip * gained
        - mesh_state * (recip * recip * recip) * jnp.mean(gained * mesh_state, axis=1, keepdims=True)
    ).astype(bf16)


def column_body(
    group,
    scaled_atmosphere_field,
    perturbation,
    target,
    weight_map,
    enc_send,
    enc_recv,
    dec_send,
    dec_recv,
    lattice_lift_matrix,
    mixing_rescale_factor,
    expand_matrix,
    contract_matrix,
    readout_matrix,
):
    bands = lax.axis_size("band")
    channels, grid_rows = scaled_atmosphere_field.shape
    node_rows = MESH_DEV
    width, hid = expand_matrix.shape
    slots = bands * enc_send.shape[2]
    crew = bands // group
    band = lax.axis_index("band").astype(jnp.int32)
    me = jnp.stack([band // crew, band % crew])
    cell_ids = jnp.arange(grid_rows, dtype=jnp.int32)
    block = (crew, channels + TABLE_ROWS, LANES)
    outgoing = vmem_call(
        functools.partial(encode_kernel, group),
        [((bands, channels + TABLE_ROWS, LANES), bf16)],
        "encode",
        scratch=[(block, bf16)],
        sems=[(group,)],
        left_out=(0,),
        fetched=range(5),
    )(None, scaled_atmosphere_field, perturbation, enc_send, enc_recv, dec_send)[0]
    arrived = all_to_all(outgoing)
    kept = [
        ((group, node_rows, width), bf16),
        ((group, node_rows, hid), bf16),
        ((group, node_rows, width + hid), bf16),
    ]
    own = [((node_rows, width), f32), ((node_rows, hid), f32)]
    normed, slopes, states, mesh_state, half_pre, chosen, column_tables = vmem_call(
        functools.partial(forward_kernel, group, channels),
        kept + own + [((slots, channels), bf16), ((group, TABLE_ROWS, LANES), f32)],
        "forward",
        scratch=[((group, slots, width), bf16)] + kept + own,
        sems=[(3, group), (2,)],
        left_out=range(5),
        fetched=(2, 3, 4, 5),
    )(
        me,
        arrived,
        lattice_lift_matrix,
        0.5 * mixing_rescale_factor[None, :],
        expand_matrix,
        contract_matrix,
        readout_matrix.T,
    )
    chain = (0.5 * mm(readout_matrix, contract_matrix, 0, 1)).astype(bf16)
    slot_values = exchange(chosen, bands)
    fill_map = (cell_ids[:, None] == dec_recv[0].reshape(-1)[None, :]).astype(bf16)
    inverse = 1.0 / jnp.maximum(jnp.sum(fill_map.astype(f32), axis=1), 1.0)
    student_outputs = scaled_atmosphere_field + mm(slot_values, fill_map, 0, 1) * inverse[None, :]
    all_pred = lax.all_gather(student_outputs, "member", axis=0)
    all_target = lax.all_gather(target[0], "member", axis=0)
    outgoing = vmem_call(
        functools.partial(loss_kernel, group),
        [((bands, channels, LANES), bf16)],
        "loss",
        scratch=[((crew, channels, LANES), bf16)],
        sems=[(group,)],
        left_out=(0,),
    )(None, student_outputs, all_pred, all_target, weight_map, inverse[None, :], dec_recv)[0]
    returned = all_to_all(outgoing)
    piece_rows = 2 * (width // crew) + channels
    node_grad, *pieces = vmem_call(
        functools.partial(backward_kernel, group, channels),
        [((node_rows, channels), f32)] + [((piece_rows, hid // 2), bf16)] * crew,
        "backward",
        scratch=[
            ((group, slots, channels), bf16),
            ((group * node_rows, channels), bf16),
            ((width, hid), f32),
            ((channels, width + hid), f32),
            kept[0],
            kept[1],
            kept[2],
        ],
        sems=[(3, group)],
        left_in=(3, 4, 5),
    )(me, returned, column_tables, chain, normed, slopes, states)
    swaps = [[(i, i ^ p) for i in range(bands)] for p in range(1, crew)]
    others = [lax.ppermute(piece, "band", swap) for piece, swap in zip(pieces[1:], swaps)]
    total = sum(x.astype(f32) for x in [pieces[0]] + others).astype(bf16)
    totals = [total] + [lax.ppermute(total, "band", swap) for swap in swaps]
    state_grad = state_gradient(
        node_grad,
        mesh_state,
        2.0 * half_pre,
        mixing_rescale_factor,
        expand_matrix,
        contract_matrix,
        readout_matrix,
    )
    factor = 1.0 / math.sqrt(bands * node_rows)
    grad_up, grad_down, grad_dec, grad_gain = vmem_call(
        functools.partial(finish_kernel, factor, channels),
        [((width, hid), f32), ((hid, width), f32), ((channels, width), f32), ((1, width), f32)],
        "finish",
        scratch=[((channels, width + hid), f32), ((width, hid), f32), ((hid, width), f32)],
        sems=[(2, crew)],
        left_out=(0, 1),
    )(me, mixing_rescale_factor[None, :], expand_matrix, readout_matrix.T, *totals)
    return (
        student_outputs[None],
        state_grad[None],
        grad_up[None],
        grad_down[None],
        grad_dec.T[None],
        grad_gain,
    )


def band_body(
    scaled_atmosphere_field,
    perturbation,
    target,
    weight_map,
    enc_send,
    enc_recv,
    dec_send,
    dec_recv,
    lattice_lift_matrix,
    mixing_rescale_factor,
    expand_matrix,
    contract_matrix,
    readout_matrix,
):
    band_count = lax.axis_size("band")
    channels, grid_rows = scaled_atmosphere_field.shape
    node_rows = MESH_DEV
    cell_ids = jnp.arange(grid_rows, dtype=jnp.int32)
    node_ids = jnp.arange(node_rows, dtype=jnp.int32)
    inputs_b = (scaled_atmosphere_field + perturbation[0].astype(f32)).astype(bf16)
    picker = (enc_send[0].reshape(-1)[:, None] == cell_ids[None, :]).astype(bf16)
    outgoing = mm(picker, inputs_b, 1, 1).astype(bf16)
    arrived = exchange(outgoing, band_count)
    slot_rows = jax.nn.silu(mm(arrived, lattice_lift_matrix, 1, 0)).astype(bf16)
    landing = (node_ids[:, None] == enc_recv[0].reshape(-1)[None, :]).astype(bf16)
    edge_count = jnp.sum(landing.astype(f32), axis=1, keepdims=True)
    mesh_state = mm(landing, slot_rows, 1, 0) / jnp.maximum(edge_count, 1.0)
    recip = lax.rsqrt(jnp.mean(mesh_state * mesh_state, axis=1, keepdims=True) + norm_eps)
    normed_b = (mesh_state * recip * mixing_rescale_factor).astype(bf16)
    hidden_pre = mm(normed_b, expand_matrix, 1, 0)
    hidden_b = jax.nn.silu(hidden_pre).astype(bf16)
    next_b = (mesh_state + mm(hidden_b, contract_matrix, 1, 0)).astype(bf16)
    mesh_picker = (dec_send[0].reshape(-1)[:, None] == node_ids[None, :]).astype(bf16)
    fill_map = (cell_ids[:, None] == dec_recv[0].reshape(-1)[None, :]).astype(bf16)
    inverse = 1.0 / jnp.maximum(jnp.sum(fill_map.astype(f32), axis=1), 1.0)
    projected = mm(next_b, readout_matrix, 1, 0).astype(bf16)
    chosen = mm(mesh_picker, projected, 1, 0).astype(bf16)
    slot_values = exchange(chosen, band_count)
    grid_sum = mm(slot_values, fill_map, 0, 1)
    student_outputs = scaled_atmosphere_field + grid_sum * inverse[None, :]
    pred_grad = member_terms(student_outputs, target, weight_map)
    scaled = (pred_grad * inverse[None, :]).astype(bf16)
    slot_grad = mm(fill_map, scaled, 0, 1).astype(bf16)
    returned = exchange(slot_grad, band_count)
    node_grad = mm(mesh_picker, returned, 0, 0)
    grad_hi, grad_lo = split3(node_grad)
    states = jnp.concatenate([next_b, hidden_b], axis=1)
    small = mm(states, grad_hi, 0, 0) + mm(states, grad_lo, 0, 0)
    hidden_grad = mm2(mm2(node_grad, readout_matrix, 1, 1), contract_matrix, 1, 1)
    sigma = jax.nn.sigmoid(hidden_pre)
    pre_hi, pre_lo = split3(hidden_grad * sigma * (1.0 + hidden_pre * (1.0 - sigma)))
    up_part = mm(normed_b, pre_hi, 0, 0) + mm(normed_b, pre_lo, 0, 0)
    state_grad = state_gradient(
        node_grad, mesh_state, hidden_pre, mixing_rescale_factor, expand_matrix, contract_matrix, readout_matrix
    )
    width, hid = up_part.shape
    factor = 1.0 / math.sqrt(band_count * node_rows)
    packed = jnp.concatenate([up_part, small[:width], small[width:]], axis=1)
    packed = jnp.pad(packed, ((0, 0), (0, -packed.shape[1] % 16)))
    total = sum_over_bands(packed, band_count) * factor
    grad_up = total[:, :hid]
    grad_dec = total[:, hid : hid + channels]
    grad_down = mm2(total[:, hid + channels : hid + 2 * channels], readout_matrix, 1, 1)
    grad_gain = jnp.sum(grad_up * expand_matrix.astype(f32), axis=1) / mixing_rescale_factor
    return (
        student_outputs[None],
        state_grad[None],
        grad_up[None],
        grad_down[None],
        grad_dec[None],
        grad_gain[None],
    )


def body(*args):
    field, enc_send, dec_send, expand = args[0], args[4], args[6], args[10]
    bands, cap = enc_send.shape[1:]
    channels, grid_rows = field.shape
    group = LANES // cap
    column = (
        dec_send.shape[2] == cap
        and LANES % cap == 0
        and cap % 16 == 0
        and group * group == bands
        and channels % 16 == 0
        and max(grid_rows, MESH_DEV) <= 256
        and bands * cap * 2 <= TABLE_ROWS * LANES
        and expand.shape[0] == expand.shape[1]
    )
    return column_body(group, *args) if column else band_body(*args)


def solution(mesh):
    return jax.shard_map(
        body,
        mesh=mesh,
        in_specs=(
            P(None, "band"),
            P("member", None, "band"),
            P("member", None, "band"),
            P(None, "band"),
            P("band", None, None),
            P("band", None, None),
            P("band", None, None),
            P("band", None, None),
            P(),
            P(),
            P(),
            P(),
            P(),
        ),
        out_specs=(
            P("member", None, "band"),
            P("member", "band", None),
            P("member", None, None),
            P("member", None, None),
            P("member", None, None),
            P("member", None),
        ),
        check_vma=False,
    )
```

```python
import functools
import math

import jax
import jax.numpy as jnp
from jax import lax
from jax.experimental import pallas as pl
from jax.experimental.pallas import tpu as pltpu
from jax.sharding import PartitionSpec as P


MESH_DEV = 256


smooth_sq = 0.01
norm_eps = 1e-05

bf16 = jnp.bfloat16
f32 = jnp.float32


def slope(diff):
    return diff * lax.rsqrt(diff * diff + smooth_sq)


def mm(a, b, ca, cb):
    return lax.dot_general(a, b, (((ca,), (cb,)), ((), ())), preferred_element_type=f32)


def split3(x):
    hi = x.astype(bf16)
    return hi, (x - hi.astype(f32)).astype(bf16)


def mm2(a, b, ca, cb):
    hi, lo = split3(a)
    return mm(hi, b, ca, cb) + mm(lo, b, ca, cb)


def exchange(x, band_count):
    rows, width = x.shape
    y = lax.all_to_all(
        x.reshape(band_count, rows // band_count, width), "band", split_axis=0, concat_axis=0, tiled=True
    )
    return y.reshape(rows, width)


def sum_over_bands(x, band_count):
    rows, width = x.shape
    parts = lax.all_to_all(
        x.astype(bf16).reshape(band_count, rows // band_count, width),
        "band",
        split_axis=0,
        concat_axis=0,
        tiled=True,
    )
    own = jnp.sum(parts.astype(f32), axis=0).astype(bf16)
    spread = jnp.broadcast_to(own[None], parts.shape)
    full = lax.all_to_all(spread, "band", split_axis=0, concat_axis=0, tiled=True)
    return full.reshape(rows, width).astype(f32)


TABLE_ROWS = 16
LANES = 128


def one_hot(a, b):
    return jnp.where(a == b, 1.0, 0.0).astype(bf16)


def lane_blocks(table, group, rows, row_of):
    bands, cap = table.shape
    r = lax.broadcasted_iota(jnp.int32, (rows, bands), 0)
    b = lax.broadcasted_iota(jnp.int32, (rows, bands), 1)
    slot = lax.broadcasted_iota(jnp.int32, (cap, LANES), 0)
    lane = lax.broadcasted_iota(jnp.int32, (cap, LANES), 1)
    out = jnp.zeros((rows, LANES), f32)
    for j in range(group):
        rows_j = mm(jnp.where(row_of(r, j) == b, 1.0, 0.0).astype(bf16), table, 1, 0).astype(bf16)
        out = out + mm(rows_j, one_hot(lane, slot + j * cap), 1, 0)
    return out


def column_order(table_ref, group):
    table = table_ref[0].astype(f32).astype(bf16)
    crew = table.shape[0] // group
    return lane_blocks(table, group, 8, lambda r, j: jnp.where(r < crew, j * crew + r, -1)), crew


def send_copies(group, crew, block_ref, out_ref, sems):
    return [
        pltpu.make_async_copy(block_ref, out_ref.at[j * crew : (j + 1) * crew], sems.at[j]) for j in range(group)
    ]


def encode_kernel(
    group, ready, field_ref, noise_ref, send_ref, recv_ref, mesh_ref, out_ref, table_ref, block_ref, sems
):
    grid_rows = field_ref.shape[1]
    bands, _ = send_ref.shape[1:]
    rows = bands // group
    ready(0, 1, 2, 3, 4)
    inputs = (field_ref[...] + noise_ref[0].astype(f32)).astype(bf16) * 0.5

    def in_rows(ref, first):
        table = ref[0].astype(f32).astype(bf16)
        return lane_blocks(
            table,
            group,
            TABLE_ROWS,
            lambda r, j: jnp.where((r >= first) & (r < first + rows), (r - first) * group + j, -1),
        )

    order = in_rows(send_ref, 0)
    table_ref[...] = in_rows(recv_ref, 0) + in_rows(mesh_ref, rows)
    subs = lax.broadcasted_iota(jnp.int32, (grid_rows, LANES), 0).astype(f32)
    pick = jnp.concatenate([one_hot(subs, order[r : r + 1, :]) for r in range(rows)], axis=1)
    block_ref[...] = mm(inputs, pick, 1, 0).T.astype(bf16).reshape(block_ref.shape)
    copy = pltpu.make_async_copy(block_ref, out_ref, sems.at[0])
    copy.start()
    copy.wait()


def loss_kernel(
    group, student_ref, pred_ref, target_ref, weight_ref, inverse_ref, recv_ref, out_ref, block_ref, sems
):
    grid_rows = student_ref.shape[1]
    student = student_ref[...]
    terms = jnp.zeros_like(student)
    for j in range(pred_ref.shape[0]):
        terms = terms + slope(student - target_ref[j].astype(f32)) - slope(student - pred_ref[j])
    scaled = (weight_ref[...].astype(f32) * terms * inverse_ref[...]).astype(bf16)
    order, crew = column_order(recv_ref, group)
    subs = lax.broadcasted_iota(jnp.int32, (grid_rows, LANES), 0).astype(f32)
    for c in range(crew):
        block_ref[c] = mm(scaled, one_hot(subs, order[c : c + 1, :]), 1, 0).astype(bf16)
    copies = send_copies(group, crew, block_ref, out_ref, sems)
    for copy in copies:
        copy.start()
    for copy in copies:
        copy.wait()


def node_forward(cells, channel_dim, table, scale_ref, expand_ref, contract_ref, lift_ref, ready):
    node_rows = MESH_DEV
    slots = cells.shape[1 - channel_dim]
    subs = lax.broadcasted_iota(jnp.int32, (node_rows, LANES), 0).astype(f32)
    latent = mm(cells, lift_ref[...], channel_dim, 0)
    latent = (latent + latent * jnp.tanh(latent)).astype(bf16)
    parts = slots // LANES
    landing = jnp.concatenate([one_hot(subs, table[j : j + 1, :]) for j in range(parts)], axis=1)
    count = mm(landing, jnp.ones((slots, LANES), bf16), 1, 0)[:, 0:1]
    state = mm(landing, latent, 1, 0) * (1.0 / jnp.maximum(count, 1.0))
    recip = lax.rsqrt(jnp.mean(state * state, axis=1, keepdims=True) + norm_eps)
    ready()
    normed = (state * recip * scale_ref[...]).astype(bf16)
    pre = mm(normed, expand_ref[...], 1, 0)
    bent = jnp.tanh(pre)
    above = 1.0 + bent
    bend = (above * (1.0 + pre * (1.0 - bent))).astype(bf16)
    hidden = (pre * above).astype(bf16)
    following = (state + mm(hidden, contract_ref[...], 1, 0)).astype(bf16)
    return state, pre, normed, bend, following, hidden


def own_kernel(
    channels,
    ready,
    cells_ref,
    table_ref,
    lift_ref,
    scale_ref,
    expand_ref,
    contract_ref,
    readout_ref,
    chosen_ref,
    *rest,
):
    count = (len(rest) - 1) // 2
    out_refs, bufs, sems = rest[:count], rest[count:-1], rest[-1]
    copies = [pltpu.make_async_copy(a, b, sems.at[i]) for i, (a, b) in enumerate(zip(bufs, out_refs))]
    parcel_buf, state_buf, pre_buf, normed_buf, bend_buf, both_buf = bufs
    slots = cells_ref.shape[0]
    width = both_buf.shape[1] // 2
    parts = slots // LANES
    table = table_ref[...]
    parcel_buf[0:channels, :] = cells_ref[...].astype(f32).T.astype(bf16)
    parcel_buf[channels:, :] = jnp.concatenate([table] * parts, axis=1).astype(bf16)
    copies[0].start()
    state, pre, normed, bend, following, hidden = node_forward(
        cells_ref[...], 1, table, scale_ref, expand_ref, contract_ref, lift_ref, lambda: ready(3, 4, 5, 6)
    )
    both_buf[:, 0:width] = following
    projected = mm(following, readout_ref[...], 1, 1).astype(bf16)
    subs = lax.broadcasted_iota(jnp.int32, (state.shape[0], LANES), 0).astype(f32)
    for j in range(parts):
        pick = one_hot(subs, table[parts + j : parts + j + 1, :])
        chosen_ref[j * LANES : (j + 1) * LANES, :] = mm(pick, projected, 0, 0).astype(bf16)
    state_buf[...] = state
    pre_buf[...] = pre
    normed_buf[...] = normed
    bend_buf[...] = bend
    both_buf[:, width:] = hidden
    for copy in copies[1:]:
        copy.start()
    for copy in copies:
        copy.wait()


def mates_kernel(channels, ready, lift_ref, scale_ref, expand_ref, contract_ref, *rest):
    mates = len(rest) - 8
    parcel_refs = rest[:mates]
    normed_out, bend_out, both_out, table_ref, normed_buf, bend_buf, both_buf, sems = rest[mates:]
    width = both_buf.shape[2] // 2
    ready(*range(4 + mates))
    pairs = [(normed_buf, normed_out), (bend_buf, bend_out), (both_buf, both_out)]
    copies = [
        [pltpu.make_async_copy(a.at[m], b.at[m], sems.at[i, m]) for i, (a, b) in enumerate(pairs)]
        for m in range(mates)
    ]
    for m, parcel_ref in enumerate(parcel_refs):
        table = parcel_ref[channels:, 0:LANES].astype(f32)
        table_ref[m] = table
        _, _, normed, bend, following, hidden = node_forward(
            parcel_ref[0:channels, :], 0, table, scale_ref, expand_ref, contract_ref, lift_ref, lambda: None
        )
        normed_buf[m] = normed
        bend_buf[m] = bend
        both_buf[m, :, 0:width] = following
        both_buf[m, :, width:] = hidden
        for copy in copies[m]:
            copy.start()
    for line in copies:
        for copy in line:
            copy.wait()


def backward_kernel(
    group,
    channels,
    me_ref,
    grad_ref,
    table_ref,
    mate_table_ref,
    chain_ref,
    normed_ref,
    bend_ref,
    both_ref,
    mate_normed_ref,
    mate_bend_ref,
    mate_both_ref,
    own_ref,
    *rest,
):
    piece_refs, (value_ref, node_ref, up_ref, small_ref, normed_buf, bend_buf, both_buf, sems) = rest[:-8], rest[-8:]
    bands = grad_ref.shape[0]
    slots = value_ref.shape[1]
    node_rows = normed_ref.shape[0]
    cap = slots // bands
    z, xy = me_ref[0], me_ref[1]
    subs = lax.broadcasted_iota(jnp.int32, (node_rows, LANES), 0).astype(f32)
    kept = [
        (bend_ref, mate_bend_ref, bend_buf),
        (normed_ref, mate_normed_ref, normed_buf),
        (both_ref, mate_both_ref, both_buf),
    ]
    copies = [
        [
            pltpu.make_async_copy(mate.at[s - 1] if s else own, buf.at[s], sems.at[i, s])
            for i, (own, mate, buf) in enumerate(kept)
        ]
        for s in range(group)
    ]
    for line in copies:
        for copy in line:
            copy.start()

    def turn(b, carry):
        values = grad_ref[b].astype(f32).T.astype(bf16)
        value_ref[:, pl.ds(pl.multiple_of(b * cap, cap), cap), :] = values.reshape(group, cap, channels)
        return carry

    lax.fori_loop(0, bands, turn, 0, unroll=4)
    parts = slots // LANES
    for s in range(group):
        table = mate_table_ref[s - 1] if s else table_ref[...]
        pick = jnp.concatenate(
            [one_hot(subs, table[parts + j : parts + j + 1, :]) for j in range(parts)], axis=1
        )
        node_grad = mm(pick, value_ref[z ^ s], 1, 0)
        if s == 0:
            own_ref[...] = node_grad
        node_b = node_grad.astype(bf16)
        node_ref[s * node_rows : (s + 1) * node_rows, :] = node_b
        copies[s][0].wait()
        pre = mm(node_b, chain_ref[...], 1, 0)
        bend_buf[s] = (pre * bend_buf[s].astype(f32)).astype(bf16)
    for line in copies:
        for copy in line[1:]:
            copy.wait()
    everything = (group * node_rows, -1)
    up_ref[...] = 2.0 * mm(normed_buf[...].reshape(everything), bend_buf[...].reshape(everything), 0, 0)
    small_ref[...] = mm(node_ref[...], both_buf[...].reshape(everything), 0, 0)
    count = len(piece_refs)
    rows = up_ref.shape[0] // count
    half = up_ref.shape[1] // 2
    lanes = small_ref.shape[1] // count
    for p, piece_ref in enumerate(piece_refs):
        to = xy ^ p
        at = pl.ds(pl.multiple_of(to * rows, rows), rows)
        piece_ref[0:rows, :] = up_ref[at, 0:half].astype(bf16)
        piece_ref[rows : 2 * rows, :] = up_ref[at, half:].astype(bf16)
        piece_ref[2 * rows :, :] = small_ref[:, pl.ds(pl.multiple_of(to * lanes, lanes), lanes)].astype(bf16)


def finish_kernel(factor, me_ref, scale_ref, expand_ref, readout_ref, *rest):
    count = len(rest) - 8
    piece_refs = rest[:count]
    up_out, down_out, dec_ref, gain_ref, small_ref, up_ref, down_ref, sems = rest[count:]
    rows = up_ref.shape[0] // count
    half = up_ref.shape[1] // 2
    lanes = small_ref.shape[1] // count
    width = up_ref.shape[0]
    places = [pl.ds(pl.multiple_of((me_ref[1] ^ p) * rows, rows), rows) for p in range(count)]
    up_copies = [pltpu.make_async_copy(up_ref.at[at], up_out.at[at], sems.at[0, p]) for p, at in enumerate(places)]
    down_copies = [
        pltpu.make_async_copy(down_ref.at[at], down_out.at[at], sems.at[1, p])
        for p, at in enumerate(pl.ds(p * rows, rows) for p in range(count))
    ]
    for p, piece_ref in enumerate(piece_refs):
        up_ref[places[p], 0:half] = piece_ref[0:rows, :].astype(f32) * factor
        up_ref[places[p], half:] = piece_ref[rows : 2 * rows, :].astype(f32) * factor
        up_copies[p].start()
        at = pl.ds(pl.multiple_of((me_ref[1] ^ p) * lanes, lanes), lanes)
        small_ref[:, at] = piece_ref[2 * rows :, :].astype(f32) * factor
    high = small_ref[:, width:].astype(bf16)
    low = (small_ref[:, width:] - high.astype(f32)).astype(bf16)
    for p in range(count):
        at = slice(p * rows, (p + 1) * rows)
        down_ref[at, :] = mm(high[:, at], readout_ref[...], 0, 0) + mm(low[:, at], readout_ref[...], 0, 0)
        down_copies[p].start()
    dec_ref[...] = small_ref[:, 0:width]
    for at in places:
        gain = up_ref[at, :] * expand_ref[at, :].astype(f32)
        gain = sum(gain[:, j : j + LANES] for j in range(0, 2 * half, LANES))
        gain_ref[:, at] = jnp.sum(gain.T, axis=0, keepdims=True) / scale_ref[:, at]
    for copy in up_copies + down_copies:
        copy.wait()


def vmem_call(kernel, outs, scratch=(), sems=(), budget=24, left_in=(), left_out=(), fetched=()):
    vmem = pl.BlockSpec(memory_space=pltpu.VMEM)
    smem = pl.BlockSpec(memory_space=pltpu.SMEM)
    left = pl.BlockSpec(memory_space=pltpu.HBM)
    fetched = list(fetched)

    def call(scalars, *operands):
        first = 0 if scalars is None else 1
        outside = set(left_in) | set(fetched)

        def run(*refs):
            refs = list(refs)
            if fetched:
                bufs, sem = refs[-1 - len(fetched) : -1], refs[-1]
                refs = refs[: -1 - len(fetched)]
                copies = {
                    at: pltpu.make_async_copy(refs[first + at], buf, sem.at[i])
                    for i, (at, buf) in enumerate(zip(fetched, bufs))
                }
                for at, buf in zip(fetched, bufs):
                    copies[at].start()
                    refs[first + at] = buf

                def ready(*which):
                    for at in which:
                        copies[at].wait()

                kernel(ready, *refs)
            else:
                kernel(*refs)

        return pl.pallas_call(
            run,
            out_shape=[(pltpu.HBM if i in left_out else jax.ShapeDtypeStruct)(s, d) for i, (s, d) in enumerate(outs)],
            in_specs=[smem] * first + [left if i in outside else vmem for i in range(len(operands))],
            out_specs=[left if i in left_out else vmem for i in range(len(outs))],
            scratch_shapes=[pltpu.VMEM(s, d) for s, d in scratch]
            + [pltpu.SemaphoreType.DMA(s) for s in sems]
            + [pltpu.VMEM(operands[i].shape, operands[i].dtype) for i in fetched]
            + ([pltpu.SemaphoreType.DMA((len(fetched),))] if fetched else []),
            compiler_params=pltpu.CompilerParams(vmem_limit_bytes=budget * 2**20),
        )(
            *([] if scalars is None else [scalars]),
            *[pltpu.with_memory_space_constraint(x, pltpu.HBM) if i in outside else x for i, x in enumerate(operands)],
        )

    return call


def all_to_all(x):
    return lax.all_to_all(x, "band", split_axis=0, concat_axis=0, tiled=True)


def member_terms(student_outputs, target, weight_map):
    all_pred, all_target = (
        lax.all_gather(student_outputs[None], "member", axis=0, tiled=True),
        lax.all_gather(target, "member", axis=0, tiled=True),
    )
    teacher_terms = jnp.sum(slope(student_outputs[None] - all_target.astype(f32)), axis=0)
    own_terms = jnp.sum(slope(student_outputs[None] - all_pred), axis=0)
    return weight_map.astype(f32) * (teacher_terms - own_terms)


def state_gradient(node_grad, mesh_state, hidden_pre, scale, expand, contract, readout):
    recip = lax.rsqrt(jnp.mean(mesh_state * mesh_state, axis=1, keepdims=True) + norm_eps)
    next_grad = mm2(node_grad, readout, 1, 1)
    hidden_grad = mm2(next_grad, contract, 1, 1)
    sigma = jax.nn.sigmoid(hidden_pre)
    pre_grad = hidden_grad * sigma * (1.0 + hidden_pre * (1.0 - sigma))
    normed_grad = mm2(pre_grad, expand, 1, 1)
    gained = normed_grad * scale
    return (
        next_grad
        + recip * gained
        - mesh_state * (recip * recip * recip) * jnp.mean(gained * mesh_state, axis=1, keepdims=True)
    ).astype(bf16)


def column_body(
    group,
    scaled_atmosphere_field,
    perturbation,
    target,
    weight_map,
    enc_send,
    enc_recv,
    dec_send,
    dec_recv,
    lattice_lift_matrix,
    mixing_rescale_factor,
    expand_matrix,
    contract_matrix,
    readout_matrix,
):
    bands = lax.axis_size("band")
    channels, grid_rows = scaled_atmosphere_field.shape
    node_rows = MESH_DEV
    width, hid = expand_matrix.shape
    slots = bands * enc_send.shape[2]
    crew = bands // group
    band = lax.axis_index("band").astype(jnp.int32)
    me = jnp.stack([band // crew, band % crew])
    cell_ids = jnp.arange(grid_rows, dtype=jnp.int32)
    cap = enc_send.shape[2]
    block = ((bands, cap, channels), bf16)
    outgoing, table = vmem_call(
        functools.partial(encode_kernel, group),
        [block, ((TABLE_ROWS, LANES), f32)],
        scratch=[block],
        sems=[(1,)],
        left_out=(0,),
        fetched=range(5),
    )(None, scaled_atmosphere_field, perturbation, enc_send, enc_recv, dec_send)
    arrived = all_to_all(outgoing).reshape(slots, channels)
    half_scale = 0.5 * mixing_rescale_factor[None, :]
    kept = [((node_rows, width), bf16), ((node_rows, hid), bf16), ((node_rows, width + hid), bf16)]
    sent = [((channels + TABLE_ROWS, slots), bf16), ((node_rows, width), f32), ((node_rows, hid), f32)] + kept
    chosen, parcel, mesh_state, half_pre, normed, bend, both = vmem_call(
        functools.partial(own_kernel, channels),
        [((slots, channels), bf16)] + sent,
        scratch=sent,
        sems=[(len(sent),)],
        left_out=range(1, 1 + len(sent)),
        fetched=(3, 4, 5, 6),
    )(
        None,
        arrived,
        table,
        lattice_lift_matrix,
        half_scale,
        expand_matrix,
        contract_matrix,
        readout_matrix.T,
    )
    parcels = [
        lax.ppermute(parcel, "band", [(i, i ^ (m * crew)) for i in range(bands)]) for m in range(1, group)
    ]
    mate_kept = [((group - 1,) + shape, dtype) for shape, dtype in kept]
    mate_normed, mate_bend, mate_both, mate_table = vmem_call(
        functools.partial(mates_kernel, channels),
        mate_kept + [((group - 1, TABLE_ROWS, LANES), f32)],
        scratch=mate_kept,
        sems=[(3, group - 1)],
        left_out=(0, 1, 2),
        fetched=range(4 + len(parcels)),
    )(None, lattice_lift_matrix, half_scale, expand_matrix, contract_matrix, *parcels)
    chain = (0.5 * mm(readout_matrix, contract_matrix, 0, 1)).astype(bf16)
    slot_values = exchange(chosen, bands)
    fill_map = (cell_ids[:, None] == dec_recv[0].reshape(-1)[None, :]).astype(bf16)
    inverse = 1.0 / jnp.maximum(jnp.sum(fill_map.astype(f32), axis=1), 1.0)
    student_outputs = scaled_atmosphere_field + mm(slot_values, fill_map, 0, 1) * inverse[None, :]
    all_pred = lax.all_gather(student_outputs, "member", axis=0)
    all_target = lax.all_gather(target[0], "member", axis=0)
    outgoing = vmem_call(
        functools.partial(loss_kernel, group),
        [((bands, channels, LANES), bf16)],
        scratch=[((crew, channels, LANES), bf16)],
        sems=[(group,)],
        left_out=(0,),
    )(None, student_outputs, all_pred, all_target, weight_map, inverse[None, :], dec_recv)[0]
    returned = all_to_all(outgoing)
    piece_rows = 2 * (width // crew) + channels
    node_grad, *pieces = vmem_call(
        functools.partial(backward_kernel, group, channels),
        [((node_rows, channels), f32)] + [((piece_rows, hid // 2), bf16)] * crew,
        scratch=[
            ((group, slots, channels), bf16),
            ((group * node_rows, channels), bf16),
            ((width, hid), f32),
            ((channels, width + hid), f32),
        ]
        + [((group,) + shape, dtype) for shape, dtype in kept],
        sems=[(3, group)],
        left_in=range(4, 10),
    )(me, returned, table, mate_table, chain, normed, bend, both, mate_normed, mate_bend, mate_both)
    swaps = [[(i, i ^ p) for i in range(bands)] for p in range(1, crew)]
    others = [lax.ppermute(piece, "band", swap) for piece, swap in zip(pieces[1:], swaps)]
    total = sum(x.astype(f32) for x in [pieces[0]] + others).astype(bf16)
    totals = [total] + [lax.ppermute(total, "band", swap) for swap in swaps]
    state_grad = state_gradient(
        node_grad,
        mesh_state,
        2.0 * half_pre,
        mixing_rescale_factor,
        expand_matrix,
        contract_matrix,
        readout_matrix,
    )
    factor = 1.0 / math.sqrt(bands * node_rows)
    grad_up, grad_down, grad_dec, grad_gain = vmem_call(
        functools.partial(finish_kernel, factor),
        [((width, hid), f32), ((hid, width), f32), ((channels, width), f32), ((1, width), f32)],
        scratch=[((channels, width + hid), f32), ((width, hid), f32), ((hid, width), f32)],
        sems=[(2, crew)],
        left_out=(0, 1),
    )(me, mixing_rescale_factor[None, :], expand_matrix, readout_matrix.T, *totals)
    return (
        student_outputs[None],
        state_grad[None],
        grad_up[None],
        grad_down[None],
        grad_dec.T[None],
        grad_gain,
    )


def band_body(
    scaled_atmosphere_field,
    perturbation,
    target,
    weight_map,
    enc_send,
    enc_recv,
    dec_send,
    dec_recv,
    lattice_lift_matrix,
    mixing_rescale_factor,
    expand_matrix,
    contract_matrix,
    readout_matrix,
):
    band_count = lax.axis_size("band")
    channels, grid_rows = scaled_atmosphere_field.shape
    node_rows = MESH_DEV
    cell_ids = jnp.arange(grid_rows, dtype=jnp.int32)
    node_ids = jnp.arange(node_rows, dtype=jnp.int32)
    inputs_b = (scaled_atmosphere_field + perturbation[0].astype(f32)).astype(bf16)
    picker = (enc_send[0].reshape(-1)[:, None] == cell_ids[None, :]).astype(bf16)
    outgoing = mm(picker, inputs_b, 1, 1).astype(bf16)
    arrived = exchange(outgoing, band_count)
    slot_rows = jax.nn.silu(mm(arrived, lattice_lift_matrix, 1, 0)).astype(bf16)
    landing = (node_ids[:, None] == enc_recv[0].reshape(-1)[None, :]).astype(bf16)
    edge_count = jnp.sum(landing.astype(f32), axis=1, keepdims=True)
    mesh_state = mm(landing, slot_rows, 1, 0) / jnp.maximum(edge_count, 1.0)
    recip = lax.rsqrt(jnp.mean(mesh_state * mesh_state, axis=1, keepdims=True) + norm_eps)
    normed_b = (mesh_state * recip * mixing_rescale_factor).astype(bf16)
    hidden_pre = mm(normed_b, expand_matrix, 1, 0)
    hidden_b = jax.nn.silu(hidden_pre).astype(bf16)
    next_b = (mesh_state + mm(hidden_b, contract_matrix, 1, 0)).astype(bf16)
    mesh_picker = (dec_send[0].reshape(-1)[:, None] == node_ids[None, :]).astype(bf16)
    fill_map = (cell_ids[:, None] == dec_recv[0].reshape(-1)[None, :]).astype(bf16)
    inverse = 1.0 / jnp.maximum(jnp.sum(fill_map.astype(f32), axis=1), 1.0)
    projected = mm(next_b, readout_matrix, 1, 0).astype(bf16)
    chosen = mm(mesh_picker, projected, 1, 0).astype(bf16)
    slot_values = exchange(chosen, band_count)
    grid_sum = mm(slot_values, fill_map, 0, 1)
    student_outputs = scaled_atmosphere_field + grid_sum * inverse[None, :]
    pred_grad = member_terms(student_outputs, target, weight_map)
    scaled = (pred_grad * inverse[None, :]).astype(bf16)
    slot_grad = mm(fill_map, scaled, 0, 1).astype(bf16)
    returned = exchange(slot_grad, band_count)
    node_grad = mm(mesh_picker, returned, 0, 0)
    grad_hi, grad_lo = split3(node_grad)
    states = jnp.concatenate([next_b, hidden_b], axis=1)
    small = mm(states, grad_hi, 0, 0) + mm(states, grad_lo, 0, 0)
    hidden_grad = mm2(mm2(node_grad, readout_matrix, 1, 1), contract_matrix, 1, 1)
    sigma = jax.nn.sigmoid(hidden_pre)
    pre_hi, pre_lo = split3(hidden_grad * sigma * (1.0 + hidden_pre * (1.0 - sigma)))
    up_part = mm(normed_b, pre_hi, 0, 0) + mm(normed_b, pre_lo, 0, 0)
    state_grad = state_gradient(
        node_grad, mesh_state, hidden_pre, mixing_rescale_factor, expand_matrix, contract_matrix, readout_matrix
    )
    width, hid = up_part.shape
    factor = 1.0 / math.sqrt(band_count * node_rows)
    packed = jnp.concatenate([up_part, small[:width], small[width:]], axis=1)
    packed = jnp.pad(packed, ((0, 0), (0, -packed.shape[1] % 16)))
    total = sum_over_bands(packed, band_count) * factor
    grad_up = total[:, :hid]
    grad_dec = total[:, hid : hid + channels]
    grad_down = mm2(total[:, hid + channels : hid + 2 * channels], readout_matrix, 1, 1)
    grad_gain = jnp.sum(grad_up * expand_matrix.astype(f32), axis=1) / mixing_rescale_factor
    return (
        student_outputs[None],
        state_grad[None],
        grad_up[None],
        grad_down[None],
        grad_dec[None],
        grad_gain[None],
    )


def body(*args):
    field, enc_send, dec_send, expand = args[0], args[4], args[6], args[10]
    bands, cap = enc_send.shape[1:]
    channels, grid_rows = field.shape
    group = LANES // cap
    column = (
        dec_send.shape[2] == cap
        and LANES % cap == 0
        and cap % 16 == 0
        and group * group == bands
        and channels % 16 == 0
        and max(grid_rows, MESH_DEV) <= 256
        and bands * cap * 2 <= TABLE_ROWS * LANES
        and expand.shape[0] == expand.shape[1]
    )
    return column_body(group, *args) if column else band_body(*args)


def solution(mesh):
    return jax.shard_map(
        body,
        mesh=mesh,
        in_specs=(
            P(None, "band"),
            P("member", None, "band"),
            P("member", None, "band"),
            P(None, "band"),
            P("band", None, None),
            P("band", None, None),
            P("band", None, None),
            P("band", None, None),
            P(),
            P(),
            P(),
            P(),
            P(),
        ),
        out_specs=(
            P("member", None, "band"),
            P("member", "band", None),
            P("member", None, None),
            P("member", None, None),
            P("member", None, None),
            P("member", None),
        ),
        check_vma=False,
    )
```

```python
import functools
import math

import jax
import jax.numpy as jnp
from jax import lax
from jax.experimental import pallas as pl
from jax.experimental.pallas import tpu as pltpu
from jax.sharding import PartitionSpec as P


MESH_DEV = 256


smooth_sq = 0.01
norm_eps = 1e-05

bf16 = jnp.bfloat16
f32 = jnp.float32


def slope(diff):
    return diff * lax.rsqrt(diff * diff + smooth_sq)


def mm(a, b, ca, cb):
    return lax.dot_general(a, b, (((ca,), (cb,)), ((), ())), preferred_element_type=f32)


def split3(x):
    hi = x.astype(bf16)
    return hi, (x - hi.astype(f32)).astype(bf16)


def mm2(a, b, ca, cb):
    hi, lo = split3(a)
    return mm(hi, b, ca, cb) + mm(lo, b, ca, cb)


def exchange(x, band_count):
    rows, width = x.shape
    y = lax.all_to_all(
        x.reshape(band_count, rows // band_count, width), "band", split_axis=0, concat_axis=0, tiled=True
    )
    return y.reshape(rows, width)


def sum_over_bands(x, band_count):
    rows, width = x.shape
    parts = lax.all_to_all(
        x.astype(bf16).reshape(band_count, rows // band_count, width),
        "band",
        split_axis=0,
        concat_axis=0,
        tiled=True,
    )
    own = jnp.sum(parts.astype(f32), axis=0).astype(bf16)
    spread = jnp.broadcast_to(own[None], parts.shape)
    full = lax.all_to_all(spread, "band", split_axis=0, concat_axis=0, tiled=True)
    return full.reshape(rows, width).astype(f32)


TABLE_ROWS = 8
LANES = 128


def one_hot(a, b):
    return jnp.where(a == b, 1.0, 0.0).astype(bf16)


def lane_blocks(table, group, rows, row_of):
    bands, cap = table.shape
    r = lax.broadcasted_iota(jnp.int32, (rows, bands), 0)
    b = lax.broadcasted_iota(jnp.int32, (rows, bands), 1)
    slot = lax.broadcasted_iota(jnp.int32, (cap, LANES), 0)
    lane = lax.broadcasted_iota(jnp.int32, (cap, LANES), 1)
    out = jnp.zeros((rows, LANES), f32)
    for j in range(group):
        rows_j = mm(jnp.where(row_of(r, j) == b, 1.0, 0.0).astype(bf16), table, 1, 0).astype(bf16)
        out = out + mm(rows_j, one_hot(lane, slot + j * cap), 1, 0)
    return out


def column_order(table_ref, group):
    table = table_ref[0].astype(f32).astype(bf16)
    crew = table.shape[0] // group
    return lane_blocks(table, group, 8, lambda r, j: jnp.where(r < crew, j * crew + r, -1)), crew


def send_copies(group, crew, block_ref, out_ref, sems):
    return [
        pltpu.make_async_copy(block_ref, out_ref.at[j * crew : (j + 1) * crew], sems.at[j]) for j in range(group)
    ]


def encode_kernel(
    group, ready, field_ref, noise_ref, send_ref, recv_ref, mesh_ref, out_ref, table_ref, block_ref, sems
):
    grid_rows = field_ref.shape[1]
    bands, _ = send_ref.shape[1:]
    rows = bands // group
    ready(0, 1, 2, 3, 4)
    inputs = (field_ref[...] + noise_ref[0].astype(f32)).astype(bf16) * 0.5

    def in_rows(ref, first):
        table = ref[0].astype(f32).astype(bf16)
        return lane_blocks(
            table,
            group,
            TABLE_ROWS,
            lambda r, j: jnp.where((r >= first) & (r < first + rows), (r - first) * group + j, -1),
        )

    order = in_rows(send_ref, 0)
    table_ref[...] = in_rows(recv_ref, 0) + in_rows(mesh_ref, rows)
    subs = lax.broadcasted_iota(jnp.int32, (grid_rows, LANES), 0).astype(f32)
    pick = jnp.concatenate([one_hot(subs, order[r : r + 1, :]) for r in range(rows)], axis=1)
    block_ref[...] = mm(inputs, pick, 1, 0).T.astype(bf16).reshape(block_ref.shape)
    copy = pltpu.make_async_copy(block_ref, out_ref, sems.at[0])
    copy.start()
    copy.wait()


def loss_kernel(
    group, student_ref, pred_ref, target_ref, weight_ref, inverse_ref, recv_ref, out_ref, block_ref, sems
):
    grid_rows = student_ref.shape[1]
    student = student_ref[...]
    terms = jnp.zeros_like(student)
    for j in range(pred_ref.shape[0]):
        terms = terms + slope(student - target_ref[j].astype(f32)) - slope(student - pred_ref[j])
    scaled = (weight_ref[...].astype(f32) * terms * inverse_ref[...]).astype(bf16)
    order, crew = column_order(recv_ref, group)
    subs = lax.broadcasted_iota(jnp.int32, (grid_rows, LANES), 0).astype(f32)
    for c in range(crew):
        block_ref[c] = mm(scaled, one_hot(subs, order[c : c + 1, :]), 1, 0).astype(bf16)
    copies = send_copies(group, crew, block_ref, out_ref, sems)
    for copy in copies:
        copy.start()
    for copy in copies:
        copy.wait()


def node_forward(cells, channel_dim, table, scale_ref, expand_ref, contract_ref, lift_ref, ready, keep=None):
    node_rows = MESH_DEV
    slots = cells.shape[1 - channel_dim]
    subs = lax.broadcasted_iota(jnp.int32, (node_rows, LANES), 0).astype(f32)
    latent = mm(cells, lift_ref[...], channel_dim, 0)
    latent = (latent + latent * jnp.tanh(latent)).astype(bf16)
    parts = slots // LANES
    landing = jnp.concatenate([one_hot(subs, table[j : j + 1, :]) for j in range(parts)], axis=1)
    count = mm(landing, jnp.ones((slots, LANES), bf16), 1, 0)[:, 0:1]
    state = mm(landing, latent, 1, 0) * (1.0 / jnp.maximum(count, 1.0))
    recip = lax.rsqrt(jnp.mean(state * state, axis=1, keepdims=True) + norm_eps)
    if keep:
        keep(2, state)
    ready()
    normed = (state * recip * scale_ref[...]).astype(bf16)
    if keep:
        keep(4, normed)
    pre = mm(normed, expand_ref[...], 1, 0)
    if keep:
        keep(3, pre)
    bent = jnp.tanh(pre)
    above = 1.0 + bent
    bend = (above * (1.0 + pre * (1.0 - bent))).astype(bf16)
    if keep:
        keep(5, bend)
    hidden = (pre * above).astype(bf16)
    following = (state + mm(hidden, contract_ref[...], 1, 0)).astype(bf16)
    return state, pre, normed, bend, following, hidden


def own_kernel(
    channels,
    ready,
    cells_ref,
    table_ref,
    lift_ref,
    scale_ref,
    expand_ref,
    contract_ref,
    readout_ref,
    chosen_ref,
    *rest,
):
    count = len(rest) // 2
    out_refs, bufs, sems = (chosen_ref,) + rest[: count - 1], rest[count - 1 : -1], rest[-1]
    copies = [pltpu.make_async_copy(a, b, sems.at[i]) for i, (a, b) in enumerate(zip(bufs, out_refs))]
    chosen_buf, parcel_buf, _, _, _, _, both_buf = bufs
    slots = cells_ref.shape[0]
    width = both_buf.shape[1] // 2
    parts = slots // LANES
    table = table_ref[...]
    parcel_buf[0:channels, :] = cells_ref[...].astype(f32).T.astype(bf16)
    parcel_buf[channels:, :] = jnp.concatenate([table] * parts, axis=1).astype(bf16)
    copies[1].start()

    def keep(at, value):
        bufs[at][...] = value
        copies[at].start()

    ready(2)
    state, _, _, _, following, hidden = node_forward(
        cells_ref[...],
        1,
        table,
        scale_ref,
        expand_ref,
        contract_ref,
        lift_ref,
        lambda: ready(3, 4, 5, 6),
        keep,
    )
    both_buf[:, 0:width] = following
    both_buf[:, width:] = hidden
    copies[6].start()
    projected = mm(following, readout_ref[...], 1, 1).astype(bf16)
    subs = lax.broadcasted_iota(jnp.int32, (state.shape[0], LANES), 0).astype(f32)
    for j in range(parts):
        pick = one_hot(subs, table[parts + j : parts + j + 1, :])
        chosen_buf[j * LANES : (j + 1) * LANES, :] = mm(pick, projected, 0, 0).astype(bf16)
    copies[0].start()
    for copy in copies:
        copy.wait()


def mates_kernel(
    channels,
    ready,
    lift_ref,
    scale_ref,
    expand_ref,
    contract_ref,
    parcel_ref,
    normed_out,
    bend_out,
    both_out,
    table_ref,
    normed_buf,
    bend_buf,
    both_buf,
    sems,
):
    mates = table_ref.shape[0]
    width = both_buf.shape[2] // 2
    ready(*range(5))
    pairs = [(normed_buf, normed_out), (bend_buf, bend_out), (both_buf, both_out)]
    copies = [
        [pltpu.make_async_copy(a.at[m], b.at[m], sems.at[i, m]) for i, (a, b) in enumerate(pairs)]
        for m in range(mates)
    ]
    for m in range(mates):
        table = parcel_ref[m, channels:, 0:LANES].astype(f32)
        table_ref[m] = table
        _, _, normed, bend, following, hidden = node_forward(
            parcel_ref[m, 0:channels, :], 0, table, scale_ref, expand_ref, contract_ref, lift_ref, lambda: None
        )
        normed_buf[m] = normed
        bend_buf[m] = bend
        both_buf[m, :, 0:width] = following
        both_buf[m, :, width:] = hidden
        for copy in copies[m]:
            copy.start()
    for line in copies:
        for copy in line:
            copy.wait()


def backward_kernel(
    group,
    channels,
    mate_count,
    me_ref,
    grad_ref,
    chain_ref,
    table_ref,
    normed_ref,
    bend_ref,
    both_ref,
    *rest,
):
    mate_refs, own_ref, piece_refs = rest[:mate_count], rest[mate_count], rest[mate_count + 1 : -8]
    value_ref, node_ref, up_ref, small_ref, normed_buf, bend_buf, both_buf, sems = rest[-8:]
    bands = grad_ref.shape[0]
    slots = value_ref.shape[1]
    node_rows = normed_ref.shape[0]
    cap = slots // bands
    z, xy = me_ref[0], me_ref[1]
    subs = lax.broadcasted_iota(jnp.int32, (node_rows, LANES), 0).astype(f32)
    held = [(table_ref[...], bend_ref, normed_ref, both_ref)]
    for at in range(0, mate_count, 4):
        mate_normed, mate_bend, mate_both, mate_table = mate_refs[at : at + 4]
        held += [
            (mate_table[m], mate_bend.at[m], mate_normed.at[m], mate_both.at[m]) for m in range(mate_table.shape[0])
        ]
    copies = [
        [
            pltpu.make_async_copy(ref, buf.at[s], sems.at[i, s])
            for i, (ref, buf) in enumerate(zip(held[s][1:], (bend_buf, normed_buf, both_buf)))
        ]
        for s in range(group)
    ]
    for line in copies:
        for copy in line:
            copy.start()

    def turn(b, carry):
        values = grad_ref[b].astype(f32).T.astype(bf16)
        value_ref[:, pl.ds(pl.multiple_of(b * cap, cap), cap), :] = values.reshape(group, cap, channels)
        return carry

    lax.fori_loop(0, bands, turn, 0, unroll=4)
    parts = slots // LANES
    for s in range(group):
        table = held[s][0]
        pick = jnp.concatenate(
            [one_hot(subs, table[parts + j : parts + j + 1, :]) for j in range(parts)], axis=1
        )
        node_grad = mm(pick, value_ref[z ^ s], 1, 0)
        if s == 0:
            own_ref[...] = node_grad
        node_b = node_grad.astype(bf16)
        node_ref[s * node_rows : (s + 1) * node_rows, :] = node_b
        copies[s][0].wait()
        pre = mm(node_b, chain_ref[...], 1, 0)
        bend_buf[s] = (pre * bend_buf[s].astype(f32)).astype(bf16)
    for line in copies:
        for copy in line[1:]:
            copy.wait()
    everything = (group * node_rows, -1)
    up_ref[...] = 2.0 * mm(normed_buf[...].reshape(everything), bend_buf[...].reshape(everything), 0, 0)
    small_ref[...] = mm(node_ref[...], both_buf[...].reshape(everything), 0, 0)
    count = len(piece_refs)
    rows = up_ref.shape[0] // count
    half = up_ref.shape[1] // 2
    lanes = small_ref.shape[1] // count
    for p, piece_ref in enumerate(piece_refs):
        to = xy ^ p
        at = pl.ds(pl.multiple_of(to * rows, rows), rows)
        piece_ref[0:rows, :] = up_ref[at, 0:half].astype(bf16)
        piece_ref[rows : 2 * rows, :] = up_ref[at, half:].astype(bf16)
        piece_ref[2 * rows :, :] = small_ref[:, pl.ds(pl.multiple_of(to * lanes, lanes), lanes)].astype(bf16)


def finish_kernel(factor, me_ref, scale_ref, expand_ref, readout_ref, *rest):
    count = len(rest) - 11
    piece_refs = rest[:count]
    up_out, down_out, dec_out, gain_out, small_ref, up_ref, down_ref, dec_ref, gain_ref, sems, last_sems = rest[count:]
    rows = up_ref.shape[0] // count
    half = up_ref.shape[1] // 2
    lanes = small_ref.shape[1] // count
    width = up_ref.shape[0]
    places = [pl.ds(pl.multiple_of((me_ref[1] ^ p) * rows, rows), rows) for p in range(count)]
    up_copies = [pltpu.make_async_copy(up_ref.at[at], up_out.at[at], sems.at[0, p]) for p, at in enumerate(places)]
    down_copies = [
        pltpu.make_async_copy(down_ref.at[at], down_out.at[at], sems.at[1, p])
        for p, at in enumerate(pl.ds(p * rows, rows) for p in range(count))
    ]
    for p, piece_ref in enumerate(piece_refs):
        up_ref[places[p], 0:half] = piece_ref[0:rows, :].astype(f32) * factor
        up_ref[places[p], half:] = piece_ref[rows : 2 * rows, :].astype(f32) * factor
        up_copies[p].start()
        at = pl.ds(pl.multiple_of((me_ref[1] ^ p) * lanes, lanes), lanes)
        small_ref[:, at] = piece_ref[2 * rows :, :].astype(f32) * factor
    dec_ref[...] = small_ref[:, 0:width]
    last_copies = [
        pltpu.make_async_copy(dec_ref, dec_out, last_sems.at[0]),
        pltpu.make_async_copy(gain_ref, gain_out, last_sems.at[1]),
    ]
    last_copies[0].start()
    high = small_ref[:, width:].astype(bf16)
    low = (small_ref[:, width:] - high.astype(f32)).astype(bf16)
    for p in range(count):
        at = slice(p * rows, (p + 1) * rows)
        down_ref[at, :] = mm(high[:, at], readout_ref[...], 0, 0) + mm(low[:, at], readout_ref[...], 0, 0)
        down_copies[p].start()
    for at in places:
        gain = up_ref[at, :] * expand_ref[at, :].astype(f32)
        gain = sum(gain[:, j : j + LANES] for j in range(0, 2 * half, LANES))
        gain_ref[:, at] = jnp.sum(gain.T, axis=0, keepdims=True) / scale_ref[:, at]
    last_copies[1].start()
    for copy in up_copies + down_copies + last_copies:
        copy.wait()


def vmem_call(kernel, outs, scratch=(), sems=(), budget=24, left_in=(), left_out=(), fetched=()):
    vmem = pl.BlockSpec(memory_space=pltpu.VMEM)
    smem = pl.BlockSpec(memory_space=pltpu.SMEM)
    left = pl.BlockSpec(memory_space=pltpu.HBM)
    fetched = list(fetched)

    def call(scalars, *operands):
        first = 0 if scalars is None else 1
        outside = set(left_in) | set(fetched)

        def run(*refs):
            refs = list(refs)
            if fetched:
                bufs, sem = refs[-1 - len(fetched) : -1], refs[-1]
                refs = refs[: -1 - len(fetched)]
                copies = {
                    at: pltpu.make_async_copy(refs[first + at], buf, sem.at[i])
                    for i, (at, buf) in enumerate(zip(fetched, bufs))
                }
                for at, buf in zip(fetched, bufs):
                    copies[at].start()
                    refs[first + at] = buf

                def ready(*which):
                    for at in which:
                        copies[at].wait()

                kernel(ready, *refs)
            else:
                kernel(*refs)

        return pl.pallas_call(
            run,
            out_shape=[(pltpu.HBM if i in left_out else jax.ShapeDtypeStruct)(s, d) for i, (s, d) in enumerate(outs)],
            in_specs=[smem] * first + [left if i in outside else vmem for i in range(len(operands))],
            out_specs=[left if i in left_out else vmem for i in range(len(outs))],
            scratch_shapes=[pltpu.VMEM(s, d) for s, d in scratch]
            + [pltpu.SemaphoreType.DMA(s) for s in sems]
            + [pltpu.VMEM(operands[i].shape, operands[i].dtype) for i in fetched]
            + ([pltpu.SemaphoreType.DMA((len(fetched),))] if fetched else []),
            compiler_params=pltpu.CompilerParams(vmem_limit_bytes=budget * 2**20),
        )(
            *([] if scalars is None else [scalars]),
            *[pltpu.with_memory_space_constraint(x, pltpu.HBM) if i in outside else x for i, x in enumerate(operands)],
        )

    return call


def all_to_all(x):
    return lax.all_to_all(x, "band", split_axis=0, concat_axis=0, tiled=True)


def member_terms(student_outputs, target, weight_map):
    all_pred, all_target = (
        lax.all_gather(student_outputs[None], "member", axis=0, tiled=True),
        lax.all_gather(target, "member", axis=0, tiled=True),
    )
    teacher_terms = jnp.sum(slope(student_outputs[None] - all_target.astype(f32)), axis=0)
    own_terms = jnp.sum(slope(student_outputs[None] - all_pred), axis=0)
    return weight_map.astype(f32) * (teacher_terms - own_terms)


def state_gradient(node_grad, mesh_state, hidden_pre, scale, expand, contract, readout):
    recip = lax.rsqrt(jnp.mean(mesh_state * mesh_state, axis=1, keepdims=True) + norm_eps)
    next_grad = mm2(node_grad, readout, 1, 1)
    hidden_grad = mm2(next_grad, contract, 1, 1)
    sigma = jax.nn.sigmoid(hidden_pre)
    pre_grad = hidden_grad * sigma * (1.0 + hidden_pre * (1.0 - sigma))
    normed_grad = mm2(pre_grad, expand, 1, 1)
    gained = normed_grad * scale
    return (
        next_grad
        + recip * gained
        - mesh_state * (recip * recip * recip) * jnp.mean(gained * mesh_state, axis=1, keepdims=True)
    ).astype(bf16)


def column_body(
    group,
    scaled_atmosphere_field,
    perturbation,
    target,
    weight_map,
    enc_send,
    enc_recv,
    dec_send,
    dec_recv,
    lattice_lift_matrix,
    mixing_rescale_factor,
    expand_matrix,
    contract_matrix,
    readout_matrix,
):
    bands = lax.axis_size("band")
    channels, grid_rows = scaled_atmosphere_field.shape
    node_rows = MESH_DEV
    width, hid = expand_matrix.shape
    slots = bands * enc_send.shape[2]
    crew = bands // group
    band = lax.axis_index("band").astype(jnp.int32)
    me = jnp.stack([band // crew, band % crew])
    cell_ids = jnp.arange(grid_rows, dtype=jnp.int32)
    cap = enc_send.shape[2]
    block = ((bands, cap, channels), bf16)
    outgoing, table = vmem_call(
        functools.partial(encode_kernel, group),
        [block, ((TABLE_ROWS, LANES), f32)],
        scratch=[block],
        sems=[(1,)],
        left_out=(0,),
        fetched=range(5),
    )(None, scaled_atmosphere_field, perturbation, enc_send, enc_recv, dec_send)
    arrived = all_to_all(outgoing).reshape(slots, channels)
    half_scale = 0.5 * mixing_rescale_factor[None, :]
    kept = [((node_rows, width), bf16), ((node_rows, hid), bf16), ((node_rows, width + hid), bf16)]
    sent = [((slots, channels), bf16), ((channels + TABLE_ROWS, slots), bf16), ((node_rows, width), f32), ((node_rows, hid), f32)] + kept
    chosen, parcel, mesh_state, half_pre, normed, bend, both = vmem_call(
        functools.partial(own_kernel, channels),
        sent,
        scratch=sent,
        sems=[(len(sent),)],
        left_out=range(len(sent)),
        fetched=(2, 3, 4, 5, 6),
    )(
        None,
        arrived,
        table,
        lattice_lift_matrix,
        half_scale,
        expand_matrix,
        contract_matrix,
        readout_matrix.T,
    )
    parcels, mates = parcel[None], []
    while parcels.shape[0] < group:
        held = parcels.shape[0]
        more = lax.ppermute(parcels, "band", [(i, i ^ (held * crew)) for i in range(bands)])
        parcels = jnp.concatenate([parcels, more])
        mate_kept = [((held,) + shape, dtype) for shape, dtype in kept]
        mates += vmem_call(
            functools.partial(mates_kernel, channels),
            mate_kept + [((held, TABLE_ROWS, LANES), f32)],
            scratch=mate_kept,
            sems=[(3, held)],
            left_out=(0, 1, 2),
            fetched=range(5),
        )(None, lattice_lift_matrix, half_scale, expand_matrix, contract_matrix, more)
    chain = (0.5 * mm(readout_matrix, contract_matrix, 0, 1)).astype(bf16)
    slot_values = exchange(chosen, bands)
    fill_map = (cell_ids[:, None] == dec_recv[0].reshape(-1)[None, :]).astype(bf16)
    inverse = 1.0 / jnp.maximum(jnp.sum(fill_map.astype(f32), axis=1), 1.0)
    student_outputs = scaled_atmosphere_field + mm(slot_values, fill_map, 0, 1) * inverse[None, :]
    all_pred = lax.all_gather(student_outputs, "member", axis=0)
    all_target = lax.all_gather(target[0], "member", axis=0)
    outgoing = vmem_call(
        functools.partial(loss_kernel, group),
        [((bands, channels, LANES), bf16)],
        scratch=[((crew, channels, LANES), bf16)],
        sems=[(group,)],
        left_out=(0,),
    )(None, student_outputs, all_pred, all_target, weight_map, inverse[None, :], dec_recv)[0]
    returned = all_to_all(outgoing)
    piece_rows = 2 * (width // crew) + channels
    node_grad, *pieces = vmem_call(
        functools.partial(backward_kernel, group, channels, len(mates)),
        [((node_rows, channels), f32)] + [((piece_rows, hid // 2), bf16)] * crew,
        scratch=[
            ((group, slots, channels), bf16),
            ((group * node_rows, channels), bf16),
            ((width, hid), f32),
            ((channels, width + hid), f32),
        ]
        + [((group,) + shape, dtype) for shape, dtype in kept],
        sems=[(3, group)],
        left_in=[3, 4, 5] + [6 + i for i in range(len(mates)) if i % 4 < 3],
    )(me, returned, chain, table, normed, bend, both, *mates)
    swaps = [[(i, i ^ p) for i in range(bands)] for p in range(1, crew)]
    others = [lax.ppermute(piece, "band", swap) for piece, swap in zip(pieces[1:], swaps)]
    total = sum(x.astype(f32) for x in [pieces[0]] + others).astype(bf16)
    totals = [total] + [lax.ppermute(total, "band", swap) for swap in swaps]
    state_grad = state_gradient(
        node_grad,
        mesh_state,
        2.0 * half_pre,
        mixing_rescale_factor,
        expand_matrix,
        contract_matrix,
        readout_matrix,
    )
    factor = 1.0 / math.sqrt(bands * node_rows)
    whole = [((width, hid), f32), ((hid, width), f32), ((channels, width), f32), ((1, width), f32)]
    grad_up, grad_down, grad_dec, grad_gain = vmem_call(
        functools.partial(finish_kernel, factor),
        whole,
        scratch=[((channels, width + hid), f32)] + whole,
        sems=[(2, crew), (2,)],
        left_out=range(4),
    )(me, mixing_rescale_factor[None, :], expand_matrix, readout_matrix.T, *totals)
    return (
        student_outputs[None],
        state_grad[None],
        grad_up[None],
        grad_down[None],
        grad_dec.T[None],
        grad_gain,
    )


def band_body(
    scaled_atmosphere_field,
    perturbation,
    target,
    weight_map,
    enc_send,
    enc_recv,
    dec_send,
    dec_recv,
    lattice_lift_matrix,
    mixing_rescale_factor,
    expand_matrix,
    contract_matrix,
    readout_matrix,
):
    band_count = lax.axis_size("band")
    channels, grid_rows = scaled_atmosphere_field.shape
    node_rows = MESH_DEV
    cell_ids = jnp.arange(grid_rows, dtype=jnp.int32)
    node_ids = jnp.arange(node_rows, dtype=jnp.int32)
    inputs_b = (scaled_atmosphere_field + perturbation[0].astype(f32)).astype(bf16)
    picker = (enc_send[0].reshape(-1)[:, None] == cell_ids[None, :]).astype(bf16)
    outgoing = mm(picker, inputs_b, 1, 1).astype(bf16)
    arrived = exchange(outgoing, band_count)
    slot_rows = jax.nn.silu(mm(arrived, lattice_lift_matrix, 1, 0)).astype(bf16)
    landing = (node_ids[:, None] == enc_recv[0].reshape(-1)[None, :]).astype(bf16)
    edge_count = jnp.sum(landing.astype(f32), axis=1, keepdims=True)
    mesh_state = mm(landing, slot_rows, 1, 0) / jnp.maximum(edge_count, 1.0)
    recip = lax.rsqrt(jnp.mean(mesh_state * mesh_state, axis=1, keepdims=True) + norm_eps)
    normed_b = (mesh_state * recip * mixing_rescale_factor).astype(bf16)
    hidden_pre = mm(normed_b, expand_matrix, 1, 0)
    hidden_b = jax.nn.silu(hidden_pre).astype(bf16)
    next_b = (mesh_state + mm(hidden_b, contract_matrix, 1, 0)).astype(bf16)
    mesh_picker = (dec_send[0].reshape(-1)[:, None] == node_ids[None, :]).astype(bf16)
    fill_map = (cell_ids[:, None] == dec_recv[0].reshape(-1)[None, :]).astype(bf16)
    inverse = 1.0 / jnp.maximum(jnp.sum(fill_map.astype(f32), axis=1), 1.0)
    projected = mm(next_b, readout_matrix, 1, 0).astype(bf16)
    chosen = mm(mesh_picker, projected, 1, 0).astype(bf16)
    slot_values = exchange(chosen, band_count)
    grid_sum = mm(slot_values, fill_map, 0, 1)
    student_outputs = scaled_atmosphere_field + grid_sum * inverse[None, :]
    pred_grad = member_terms(student_outputs, target, weight_map)
    scaled = (pred_grad * inverse[None, :]).astype(bf16)
    slot_grad = mm(fill_map, scaled, 0, 1).astype(bf16)
    returned = exchange(slot_grad, band_count)
    node_grad = mm(mesh_picker, returned, 0, 0)
    grad_hi, grad_lo = split3(node_grad)
    states = jnp.concatenate([next_b, hidden_b], axis=1)
    small = mm(states, grad_hi, 0, 0) + mm(states, grad_lo, 0, 0)
    hidden_grad = mm2(mm2(node_grad, readout_matrix, 1, 1), contract_matrix, 1, 1)
    sigma = jax.nn.sigmoid(hidden_pre)
    pre_hi, pre_lo = split3(hidden_grad * sigma * (1.0 + hidden_pre * (1.0 - sigma)))
    up_part = mm(normed_b, pre_hi, 0, 0) + mm(normed_b, pre_lo, 0, 0)
    state_grad = state_gradient(
        node_grad, mesh_state, hidden_pre, mixing_rescale_factor, expand_matrix, contract_matrix, readout_matrix
    )
    width, hid = up_part.shape
    factor = 1.0 / math.sqrt(band_count * node_rows)
    packed = jnp.concatenate([up_part, small[:width], small[width:]], axis=1)
    packed = jnp.pad(packed, ((0, 0), (0, -packed.shape[1] % 16)))
    total = sum_over_bands(packed, band_count) * factor
    grad_up = total[:, :hid]
    grad_dec = total[:, hid : hid + channels]
    grad_down = mm2(total[:, hid + channels : hid + 2 * channels], readout_matrix, 1, 1)
    grad_gain = jnp.sum(grad_up * expand_matrix.astype(f32), axis=1) / mixing_rescale_factor
    return (
        student_outputs[None],
        state_grad[None],
        grad_up[None],
        grad_down[None],
        grad_dec[None],
        grad_gain[None],
    )


def body(*args):
    field, enc_send, dec_send, expand = args[0], args[4], args[6], args[10]
    bands, cap = enc_send.shape[1:]
    channels, grid_rows = field.shape
    group = LANES // cap
    column = (
        dec_send.shape[2] == cap
        and LANES % cap == 0
        and cap % 16 == 0
        and group * group == bands
        and channels % 16 == 0
        and max(grid_rows, MESH_DEV) <= 256
        and bands * cap * 2 <= TABLE_ROWS * LANES
        and expand.shape[0] == expand.shape[1]
    )
    return column_body(group, *args) if column else band_body(*args)


def solution(mesh):
    return jax.shard_map(
        body,
        mesh=mesh,
        in_specs=(
            P(None, "band"),
            P("member", None, "band"),
            P("member", None, "band"),
            P(None, "band"),
            P("band", None, None),
            P("band", None, None),
            P("band", None, None),
            P("band", None, None),
            P(),
            P(),
            P(),
            P(),
            P(),
        ),
        out_specs=(
            P("member", None, "band"),
            P("member", "band", None),
            P("member", None, None),
            P("member", None, None),
            P("member", None, None),
            P("member", None),
        ),
        check_vma=False,
    )
```

```python
import functools
import math

import jax
import jax.numpy as jnp
from jax import lax
from jax.experimental import pallas as pl
from jax.experimental.pallas import tpu as pltpu
from jax.sharding import PartitionSpec as P


MESH_DEV = 256


smooth_sq = 0.01
norm_eps = 1e-05

bf16 = jnp.bfloat16
f32 = jnp.float32


def slope(diff):
    return diff * lax.rsqrt(diff * diff + smooth_sq)


def mm(a, b, ca, cb):
    return lax.dot_general(a, b, (((ca,), (cb,)), ((), ())), preferred_element_type=f32)


def split3(x):
    hi = x.astype(bf16)
    return hi, (x - hi.astype(f32)).astype(bf16)


def mm2(a, b, ca, cb):
    hi, lo = split3(a)
    return mm(hi, b, ca, cb) + mm(lo, b, ca, cb)


def exchange(x, band_count):
    rows, width = x.shape
    y = lax.all_to_all(
        x.reshape(band_count, rows // band_count, width), "band", split_axis=0, concat_axis=0, tiled=True
    )
    return y.reshape(rows, width)


def sum_over_bands(x, band_count):
    rows, width = x.shape
    parts = lax.all_to_all(
        x.astype(bf16).reshape(band_count, rows // band_count, width),
        "band",
        split_axis=0,
        concat_axis=0,
        tiled=True,
    )
    own = jnp.sum(parts.astype(f32), axis=0).astype(bf16)
    spread = jnp.broadcast_to(own[None], parts.shape)
    full = lax.all_to_all(spread, "band", split_axis=0, concat_axis=0, tiled=True)
    return full.reshape(rows, width).astype(f32)


TABLE_ROWS = 8
LANES = 128


def one_hot(a, b):
    return jnp.where(a == b, 1.0, 0.0).astype(bf16)


def lane_blocks(table, group, rows, row_of):
    bands, cap = table.shape
    r = lax.broadcasted_iota(jnp.int32, (rows, bands), 0)
    b = lax.broadcasted_iota(jnp.int32, (rows, bands), 1)
    slot = lax.broadcasted_iota(jnp.int32, (cap, LANES), 0)
    lane = lax.broadcasted_iota(jnp.int32, (cap, LANES), 1)
    out = jnp.zeros((rows, LANES), f32)
    for j in range(group):
        rows_j = mm(jnp.where(row_of(r, j) == b, 1.0, 0.0).astype(bf16), table, 1, 0).astype(bf16)
        out = out + mm(rows_j, one_hot(lane, slot + j * cap), 1, 0)
    return out


def column_order(table_ref, group):
    table = table_ref[0].astype(f32).astype(bf16)
    crew = table.shape[0] // group
    return lane_blocks(table, group, 8, lambda r, j: jnp.where(r < crew, j * crew + r, -1)), crew


def send_copies(group, crew, block_ref, out_ref, sems):
    return [
        pltpu.make_async_copy(block_ref, out_ref.at[j * crew : (j + 1) * crew], sems.at[j]) for j in range(group)
    ]


def encode_kernel(
    group,
    ready,
    field_ref,
    noise_ref,
    send_ref,
    recv_ref,
    mesh_ref,
    lift_in,
    expand_in,
    contract_in,
    readout_in,
    out_ref,
    table_ref,
    lift_ref,
    expand_ref,
    contract_ref,
    readout_ref,
    block_ref,
    sems,
):
    grid_rows = field_ref.shape[1]
    bands, _ = send_ref.shape[1:]
    rows = bands // group
    pairs = [(lift_in, lift_ref), (expand_in, expand_ref), (contract_in, contract_ref), (readout_in, readout_ref)]
    weights = [pltpu.make_async_copy(a, b, sems.at[i + 1]) for i, (a, b) in enumerate(pairs)]
    for copy in weights:
        copy.start()
    ready(0, 1, 2, 3, 4)
    inputs = (field_ref[...] + noise_ref[0].astype(f32)).astype(bf16) * 0.5

    def in_rows(ref, first):
        table = ref[0].astype(f32).astype(bf16)
        return lane_blocks(
            table,
            group,
            TABLE_ROWS,
            lambda r, j: jnp.where((r >= first) & (r < first + rows), (r - first) * group + j, -1),
        )

    order = in_rows(send_ref, 0)
    table_ref[...] = in_rows(recv_ref, 0) + in_rows(mesh_ref, rows)
    subs = lax.broadcasted_iota(jnp.int32, (grid_rows, LANES), 0).astype(f32)
    pick = jnp.concatenate([one_hot(subs, order[r : r + 1, :]) for r in range(rows)], axis=1)
    block_ref[...] = mm(inputs, pick, 1, 0).T.astype(bf16).reshape(block_ref.shape)
    copy = pltpu.make_async_copy(block_ref, out_ref, sems.at[0])
    copy.start()
    for copy in [copy] + weights:
        copy.wait()


def loss_kernel(
    group, student_ref, pred_ref, target_ref, weight_ref, inverse_ref, recv_ref, out_ref, block_ref, sems
):
    grid_rows = student_ref.shape[1]
    student = student_ref[...]
    terms = jnp.zeros_like(student)
    for j in range(pred_ref.shape[0]):
        terms = terms + slope(student - target_ref[j].astype(f32)) - slope(student - pred_ref[j])
    scaled = (weight_ref[...].astype(f32) * terms * inverse_ref[...]).astype(bf16)
    order, crew = column_order(recv_ref, group)
    subs = lax.broadcasted_iota(jnp.int32, (grid_rows, LANES), 0).astype(f32)
    for c in range(crew):
        block_ref[c] = mm(scaled, one_hot(subs, order[c : c + 1, :]), 1, 0).astype(bf16)
    copies = send_copies(group, crew, block_ref, out_ref, sems)
    for copy in copies:
        copy.start()
    for copy in copies:
        copy.wait()


def node_forward(cells, channel_dim, table, scale_ref, expand_ref, contract_ref, lift_ref, ready, keep=None):
    node_rows = MESH_DEV
    slots = cells.shape[1 - channel_dim]
    subs = lax.broadcasted_iota(jnp.int32, (node_rows, LANES), 0).astype(f32)
    latent = mm(cells, lift_ref[...], channel_dim, 0)
    latent = (latent + latent * jnp.tanh(latent)).astype(bf16)
    parts = slots // LANES
    landing = jnp.concatenate([one_hot(subs, table[j : j + 1, :]) for j in range(parts)], axis=1)
    count = mm(landing, jnp.ones((slots, LANES), bf16), 1, 0)[:, 0:1]
    state = mm(landing, latent, 1, 0) * (1.0 / jnp.maximum(count, 1.0))
    recip = lax.rsqrt(jnp.mean(state * state, axis=1, keepdims=True) + norm_eps)
    if keep:
        keep(2, state)
    ready()
    normed = (state * recip * scale_ref[...]).astype(bf16)
    if keep:
        keep(4, normed)
    pre = mm(normed, expand_ref[...], 1, 0)
    if keep:
        keep(3, pre)
    bent = jnp.tanh(pre)
    above = 1.0 + bent
    bend = (above * (1.0 + pre * (1.0 - bent))).astype(bf16)
    if keep:
        keep(5, bend)
    hidden = (pre * above).astype(bf16)
    following = (state + mm(hidden, contract_ref[...], 1, 0)).astype(bf16)
    return state, pre, normed, bend, following, hidden


def own_kernel(
    channels,
    ready,
    cells_ref,
    table_ref,
    lift_ref,
    expand_ref,
    contract_ref,
    readout_ref,
    scale_ref,
    chosen_ref,
    *rest,
):
    count = len(rest) // 2
    out_refs, bufs, sems = (chosen_ref,) + rest[: count - 1], rest[count - 1 : -1], rest[-1]
    copies = [pltpu.make_async_copy(a, b, sems.at[i]) for i, (a, b) in enumerate(zip(bufs, out_refs))]
    chosen_buf, parcel_buf, _, _, _, _, both_buf = bufs
    slots = cells_ref.shape[0]
    width = both_buf.shape[1] // 2
    parts = slots // LANES
    table = table_ref[...]
    parcel_buf[0:channels, :] = cells_ref[...].astype(f32).T.astype(bf16)
    parcel_buf[channels:, :] = jnp.concatenate([table] * parts, axis=1).astype(bf16)
    copies[1].start()

    def keep(at, value):
        bufs[at][...] = value
        copies[at].start()

    state, _, _, _, following, hidden = node_forward(
        cells_ref[...],
        1,
        table,
        scale_ref,
        expand_ref,
        contract_ref,
        lift_ref,
        lambda: ready(6),
        keep,
    )
    both_buf[:, 0:width] = following
    both_buf[:, width:] = hidden
    copies[6].start()
    projected = mm(following, readout_ref[...], 1, 1).astype(bf16)
    subs = lax.broadcasted_iota(jnp.int32, (state.shape[0], LANES), 0).astype(f32)
    for j in range(parts):
        pick = one_hot(subs, table[parts + j : parts + j + 1, :])
        chosen_buf[j * LANES : (j + 1) * LANES, :] = mm(pick, projected, 0, 0).astype(bf16)
    copies[0].start()
    for copy in copies:
        copy.wait()


def mates_kernel(
    channels,
    ready,
    lift_ref,
    scale_ref,
    expand_ref,
    contract_ref,
    parcel_ref,
    normed_ref,
    bend_ref,
    both_out,
    table_ref,
    both_buf,
    sems,
):
    mates = table_ref.shape[0]
    width = both_buf.shape[2] // 2
    ready(*range(5))
    copies = [pltpu.make_async_copy(both_buf.at[m], both_out.at[m], sems.at[m]) for m in range(mates)]
    for m in range(mates):
        table = parcel_ref[m, channels:, 0:LANES].astype(f32)
        table_ref[m] = table
        _, _, normed, bend, following, hidden = node_forward(
            parcel_ref[m, 0:channels, :], 0, table, scale_ref, expand_ref, contract_ref, lift_ref, lambda: None
        )
        normed_ref[m] = normed
        bend_ref[m] = bend
        both_buf[m, :, 0:width] = following
        both_buf[m, :, width:] = hidden
        copies[m].start()
    for copy in copies:
        copy.wait()


def backward_kernel(
    group,
    channels,
    mate_count,
    me_ref,
    grad_ref,
    chain_ref,
    table_ref,
    normed_ref,
    bend_ref,
    both_ref,
    *rest,
):
    mate_refs, own_ref, piece_refs = rest[:mate_count], rest[mate_count], rest[mate_count + 1 : -8]
    value_ref, node_ref, up_ref, small_ref, normed_buf, bend_buf, both_buf, sems = rest[-8:]
    bands = grad_ref.shape[0]
    slots = value_ref.shape[1]
    node_rows = normed_ref.shape[0]
    cap = slots // bands
    z, xy = me_ref[0], me_ref[1]
    subs = lax.broadcasted_iota(jnp.int32, (node_rows, LANES), 0).astype(f32)
    held = [(table_ref[...], bend_ref, normed_ref, both_ref)]
    for at in range(0, mate_count, 4):
        mate_normed, mate_bend, mate_both, mate_table = mate_refs[at : at + 4]
        held += [
            (mate_table[m], mate_bend.at[m], mate_normed.at[m], mate_both.at[m]) for m in range(mate_table.shape[0])
        ]
    copies = [
        [
            pltpu.make_async_copy(ref, buf.at[s], sems.at[i, s])
            for i, (ref, buf) in enumerate(zip(held[s][1:], (bend_buf, normed_buf, both_buf)))
        ]
        for s in range(group)
    ]
    for line in copies:
        for copy in line:
            copy.start()

    def turn(b, carry):
        values = grad_ref[b].astype(f32).T.astype(bf16)
        value_ref[:, pl.ds(pl.multiple_of(b * cap, cap), cap), :] = values.reshape(group, cap, channels)
        return carry

    lax.fori_loop(0, bands, turn, 0, unroll=4)
    parts = slots // LANES
    for s in range(group):
        table = held[s][0]
        pick = jnp.concatenate(
            [one_hot(subs, table[parts + j : parts + j + 1, :]) for j in range(parts)], axis=1
        )
        node_grad = mm(pick, value_ref[z ^ s], 1, 0)
        if s == 0:
            own_ref[...] = node_grad
        node_b = node_grad.astype(bf16)
        node_ref[s * node_rows : (s + 1) * node_rows, :] = node_b
        copies[s][0].wait()
        pre = mm(node_b, chain_ref[...], 1, 0)
        bend_buf[s] = (pre * bend_buf[s].astype(f32)).astype(bf16)
    for line in copies:
        for copy in line[1:]:
            copy.wait()
    everything = (group * node_rows, -1)
    up_ref[...] = 2.0 * mm(normed_buf[...].reshape(everything), bend_buf[...].reshape(everything), 0, 0)
    small_ref[...] = mm(node_ref[...], both_buf[...].reshape(everything), 0, 0)
    count = len(piece_refs)
    rows = up_ref.shape[0] // count
    half = up_ref.shape[1] // 2
    lanes = small_ref.shape[1] // count
    for p, piece_ref in enumerate(piece_refs):
        to = xy ^ p
        at = pl.ds(pl.multiple_of(to * rows, rows), rows)
        piece_ref[0:rows, :] = up_ref[at, 0:half].astype(bf16)
        piece_ref[rows : 2 * rows, :] = up_ref[at, half:].astype(bf16)
        piece_ref[2 * rows :, :] = small_ref[:, pl.ds(pl.multiple_of(to * lanes, lanes), lanes)].astype(bf16)


def finish_kernel(factor, me_ref, scale_ref, expand_ref, readout_ref, *rest):
    count = len(rest) - 11
    piece_refs = rest[:count]
    up_out, down_out, dec_out, gain_out, small_ref, up_ref, down_ref, dec_ref, gain_ref, sems, last_sems = rest[count:]
    rows = up_ref.shape[0] // count
    half = up_ref.shape[1] // 2
    lanes = small_ref.shape[1] // count
    width = up_ref.shape[0]
    places = [pl.ds(pl.multiple_of((me_ref[1] ^ p) * rows, rows), rows) for p in range(count)]
    up_copies = [pltpu.make_async_copy(up_ref.at[at], up_out.at[at], sems.at[0, p]) for p, at in enumerate(places)]
    down_copies = [
        pltpu.make_async_copy(down_ref.at[at], down_out.at[at], sems.at[1, p])
        for p, at in enumerate(pl.ds(p * rows, rows) for p in range(count))
    ]
    for p, piece_ref in enumerate(piece_refs):
        up_ref[places[p], 0:half] = piece_ref[0:rows, :].astype(f32) * factor
        up_ref[places[p], half:] = piece_ref[rows : 2 * rows, :].astype(f32) * factor
        up_copies[p].start()
        at = pl.ds(pl.multiple_of((me_ref[1] ^ p) * lanes, lanes), lanes)
        small_ref[:, at] = piece_ref[2 * rows :, :].astype(f32) * factor
    dec_ref[...] = small_ref[:, 0:width]
    last_copies = [
        pltpu.make_async_copy(dec_ref, dec_out, last_sems.at[0]),
        pltpu.make_async_copy(gain_ref, gain_out, last_sems.at[1]),
    ]
    last_copies[0].start()
    high = small_ref[:, width:].astype(bf16)
    low = (small_ref[:, width:] - high.astype(f32)).astype(bf16)
    for p in range(count):
        at = slice(p * rows, (p + 1) * rows)
        down_ref[at, :] = mm(high[:, at], readout_ref[...], 0, 0) + mm(low[:, at], readout_ref[...], 0, 0)
        down_copies[p].start()
    for at in places:
        gain = up_ref[at, :] * expand_ref[at, :].astype(f32)
        gain = sum(gain[:, j : j + LANES] for j in range(0, 2 * half, LANES))
        gain_ref[:, at] = jnp.sum(gain.T, axis=0, keepdims=True) / scale_ref[:, at]
    last_copies[1].start()
    for copy in up_copies + down_copies + last_copies:
        copy.wait()


def vmem_call(kernel, outs, scratch=(), sems=(), budget=24, left_in=(), left_out=(), fetched=(), vmem_in=(), vmem_out=()):
    vmem = pl.BlockSpec(memory_space=pltpu.VMEM)
    smem = pl.BlockSpec(memory_space=pltpu.SMEM)
    left = pl.BlockSpec(memory_space=pltpu.HBM)
    fetched = list(fetched)

    def call(scalars, *operands):
        first = 0 if scalars is None else 1
        outside = set(left_in) | set(fetched)

        def run(*refs):
            refs = list(refs)
            if fetched:
                bufs, sem = refs[-1 - len(fetched) : -1], refs[-1]
                refs = refs[: -1 - len(fetched)]
                copies = {
                    at: pltpu.make_async_copy(refs[first + at], buf, sem.at[i])
                    for i, (at, buf) in enumerate(zip(fetched, bufs))
                }
                for at, buf in zip(fetched, bufs):
                    copies[at].start()
                    refs[first + at] = buf

                def ready(*which):
                    for at in which:
                        copies[at].wait()

                kernel(ready, *refs)
            else:
                kernel(*refs)

        return pl.pallas_call(
            run,
            out_shape=[
                (pltpu.HBM if i in left_out else pltpu.VMEM if i in vmem_out else jax.ShapeDtypeStruct)(s, d)
                for i, (s, d) in enumerate(outs)
            ],
            in_specs=[smem] * first + [left if i in outside else vmem for i in range(len(operands))],
            out_specs=[left if i in left_out else vmem for i in range(len(outs))],
            scratch_shapes=[pltpu.VMEM(s, d) for s, d in scratch]
            + [pltpu.SemaphoreType.DMA(s) for s in sems]
            + [pltpu.VMEM(operands[i].shape, operands[i].dtype) for i in fetched]
            + ([pltpu.SemaphoreType.DMA((len(fetched),))] if fetched else []),
            compiler_params=pltpu.CompilerParams(vmem_limit_bytes=budget * 2**20),
        )(
            *([] if scalars is None else [scalars]),
            *[
                pltpu.with_memory_space_constraint(x, pltpu.HBM)
                if i in outside
                else pltpu.with_memory_space_constraint(x, pltpu.VMEM)
                if i in vmem_in
                else x
                for i, x in enumerate(operands)
            ],
        )

    return call


def all_to_all(x):
    return lax.all_to_all(x, "band", split_axis=0, concat_axis=0, tiled=True)


def member_terms(student_outputs, target, weight_map):
    all_pred, all_target = (
        lax.all_gather(student_outputs[None], "member", axis=0, tiled=True),
        lax.all_gather(target, "member", axis=0, tiled=True),
    )
    teacher_terms = jnp.sum(slope(student_outputs[None] - all_target.astype(f32)), axis=0)
    own_terms = jnp.sum(slope(student_outputs[None] - all_pred), axis=0)
    return weight_map.astype(f32) * (teacher_terms - own_terms)


def state_gradient(node_grad, mesh_state, hidden_pre, scale, expand, contract, readout):
    recip = lax.rsqrt(jnp.mean(mesh_state * mesh_state, axis=1, keepdims=True) + norm_eps)
    next_grad = mm2(node_grad, readout, 1, 1)
    hidden_grad = mm2(next_grad, contract, 1, 1)
    sigma = jax.nn.sigmoid(hidden_pre)
    pre_grad = hidden_grad * sigma * (1.0 + hidden_pre * (1.0 - sigma))
    normed_grad = mm2(pre_grad, expand, 1, 1)
    gained = normed_grad * scale
    return (
        next_grad
        + recip * gained
        - mesh_state * (recip * recip * recip) * jnp.mean(gained * mesh_state, axis=1, keepdims=True)
    ).astype(bf16)


def column_body(
    group,
    scaled_atmosphere_field,
    perturbation,
    target,
    weight_map,
    enc_send,
    enc_recv,
    dec_send,
    dec_recv,
    lattice_lift_matrix,
    mixing_rescale_factor,
    expand_matrix,
    contract_matrix,
    readout_matrix,
):
    bands = lax.axis_size("band")
    channels, grid_rows = scaled_atmosphere_field.shape
    node_rows = MESH_DEV
    width, hid = expand_matrix.shape
    slots = bands * enc_send.shape[2]
    crew = bands // group
    band = lax.axis_index("band").astype(jnp.int32)
    me = jnp.stack([band // crew, band % crew])
    cell_ids = jnp.arange(grid_rows, dtype=jnp.int32)
    cap = enc_send.shape[2]
    block = ((bands, cap, channels), bf16)
    weights = (lattice_lift_matrix, expand_matrix, contract_matrix, readout_matrix.T)
    outgoing, table, *near_weights = vmem_call(
        functools.partial(encode_kernel, group),
        [block, ((TABLE_ROWS, LANES), f32)] + [(w.shape, w.dtype) for w in weights],
        scratch=[block],
        sems=[(5,)],
        left_in=range(5, 9),
        left_out=(0,),
        vmem_out=range(2, 6),
        fetched=range(5),
    )(None, scaled_atmosphere_field, perturbation, enc_send, enc_recv, dec_send, *weights)
    arrived = all_to_all(outgoing).reshape(slots, channels)
    half_scale = 0.5 * mixing_rescale_factor[None, :]
    kept = [((node_rows, width), bf16), ((node_rows, hid), bf16), ((node_rows, width + hid), bf16)]
    sent = [((slots, channels), bf16), ((channels + TABLE_ROWS, slots), bf16), ((node_rows, width), f32), ((node_rows, hid), f32)] + kept
    chosen, parcel, mesh_state, half_pre, normed, bend, both = vmem_call(
        functools.partial(own_kernel, channels),
        sent,
        scratch=sent,
        sems=[(len(sent),)],
        left_out=range(len(sent)),
        fetched=(6,),
        vmem_in=(2, 3, 4, 5),
    )(None, arrived, table, *near_weights, half_scale)
    parcels, mates = parcel[None], []
    while parcels.shape[0] < group:
        held = parcels.shape[0]
        more = lax.ppermute(parcels, "band", [(i, i ^ (held * crew)) for i in range(bands)])
        parcels = jnp.concatenate([parcels, more])
        mate_kept = [((held,) + shape, dtype) for shape, dtype in kept]
        mates += vmem_call(
            functools.partial(mates_kernel, channels),
            mate_kept + [((held, TABLE_ROWS, LANES), f32)],
            scratch=mate_kept[2:],
            sems=[(held,)],
            left_out=(2,),
            vmem_out=(0, 1),
            fetched=range(5),
        )(None, lattice_lift_matrix, half_scale, expand_matrix, contract_matrix, more)
    chain = (0.5 * mm(readout_matrix, contract_matrix, 0, 1)).astype(bf16)
    slot_values = exchange(chosen, bands)
    fill_map = (cell_ids[:, None] == dec_recv[0].reshape(-1)[None, :]).astype(bf16)
    inverse = 1.0 / jnp.maximum(jnp.sum(fill_map.astype(f32), axis=1), 1.0)
    student_outputs = scaled_atmosphere_field + mm(slot_values, fill_map, 0, 1) * inverse[None, :]
    all_pred = lax.all_gather(student_outputs, "member", axis=0)
    all_target = lax.all_gather(target[0], "member", axis=0)
    outgoing = vmem_call(
        functools.partial(loss_kernel, group),
        [((bands, channels, LANES), bf16)],
        scratch=[((crew, channels, LANES), bf16)],
        sems=[(group,)],
        left_out=(0,),
    )(None, student_outputs, all_pred, all_target, weight_map, inverse[None, :], dec_recv)[0]
    returned = all_to_all(outgoing)
    piece_rows = 2 * (width // crew) + channels
    node_grad, *pieces = vmem_call(
        functools.partial(backward_kernel, group, channels, len(mates)),
        [((node_rows, channels), f32)] + [((piece_rows, hid // 2), bf16)] * crew,
        scratch=[
            ((group, slots, channels), bf16),
            ((group * node_rows, channels), bf16),
            ((width, hid), f32),
            ((channels, width + hid), f32),
        ]
        + [((group,) + shape, dtype) for shape, dtype in kept],
        sems=[(3, group)],
        left_in=[3, 4, 5] + [6 + i for i in range(len(mates)) if i % 4 == 2],
        vmem_in=[6 + i for i in range(len(mates)) if i % 4 < 2],
    )(me, returned, chain, table, normed, bend, both, *mates)
    swaps = [[(i, i ^ p) for i in range(bands)] for p in range(1, crew)]
    others = [lax.ppermute(piece, "band", swap) for piece, swap in zip(pieces[1:], swaps)]
    total = sum(x.astype(f32) for x in [pieces[0]] + others).astype(bf16)
    totals = [total] + [lax.ppermute(total, "band", swap) for swap in swaps]
    state_grad = state_gradient(
        node_grad,
        mesh_state,
        2.0 * half_pre,
        mixing_rescale_factor,
        expand_matrix,
        contract_matrix,
        readout_matrix,
    )
    factor = 1.0 / math.sqrt(bands * node_rows)
    whole = [((width, hid), f32), ((hid, width), f32), ((channels, width), f32), ((1, width), f32)]
    grad_up, grad_down, grad_dec, grad_gain = vmem_call(
        functools.partial(finish_kernel, factor),
        whole,
        scratch=[((channels, width + hid), f32)] + whole,
        sems=[(2, crew), (2,)],
        left_out=range(4),
    )(me, mixing_rescale_factor[None, :], expand_matrix, readout_matrix.T, *totals)
    return (
        student_outputs[None],
        state_grad[None],
        grad_up[None],
        grad_down[None],
        grad_dec.T[None],
        grad_gain,
    )


def band_body(
    scaled_atmosphere_field,
    perturbation,
    target,
    weight_map,
    enc_send,
    enc_recv,
    dec_send,
    dec_recv,
    lattice_lift_matrix,
    mixing_rescale_factor,
    expand_matrix,
    contract_matrix,
    readout_matrix,
):
    band_count = lax.axis_size("band")
    channels, grid_rows = scaled_atmosphere_field.shape
    node_rows = MESH_DEV
    cell_ids = jnp.arange(grid_rows, dtype=jnp.int32)
    node_ids = jnp.arange(node_rows, dtype=jnp.int32)
    inputs_b = (scaled_atmosphere_field + perturbation[0].astype(f32)).astype(bf16)
    picker = (enc_send[0].reshape(-1)[:, None] == cell_ids[None, :]).astype(bf16)
    outgoing = mm(picker, inputs_b, 1, 1).astype(bf16)
    arrived = exchange(outgoing, band_count)
    slot_rows = jax.nn.silu(mm(arrived, lattice_lift_matrix, 1, 0)).astype(bf16)
    landing = (node_ids[:, None] == enc_recv[0].reshape(-1)[None, :]).astype(bf16)
    edge_count = jnp.sum(landing.astype(f32), axis=1, keepdims=True)
    mesh_state = mm(landing, slot_rows, 1, 0) / jnp.maximum(edge_count, 1.0)
    recip = lax.rsqrt(jnp.mean(mesh_state * mesh_state, axis=1, keepdims=True) + norm_eps)
    normed_b = (mesh_state * recip * mixing_rescale_factor).astype(bf16)
    hidden_pre = mm(normed_b, expand_matrix, 1, 0)
    hidden_b = jax.nn.silu(hidden_pre).astype(bf16)
    next_b = (mesh_state + mm(hidden_b, contract_matrix, 1, 0)).astype(bf16)
    mesh_picker = (dec_send[0].reshape(-1)[:, None] == node_ids[None, :]).astype(bf16)
    fill_map = (cell_ids[:, None] == dec_recv[0].reshape(-1)[None, :]).astype(bf16)
    inverse = 1.0 / jnp.maximum(jnp.sum(fill_map.astype(f32), axis=1), 1.0)
    projected = mm(next_b, readout_matrix, 1, 0).astype(bf16)
    chosen = mm(mesh_picker, projected, 1, 0).astype(bf16)
    slot_values = exchange(chosen, band_count)
    grid_sum = mm(slot_values, fill_map, 0, 1)
    student_outputs = scaled_atmosphere_field + grid_sum * inverse[None, :]
    pred_grad = member_terms(student_outputs, target, weight_map)
    scaled = (pred_grad * inverse[None, :]).astype(bf16)
    slot_grad = mm(fill_map, scaled, 0, 1).astype(bf16)
    returned = exchange(slot_grad, band_count)
    node_grad = mm(mesh_picker, returned, 0, 0)
    grad_hi, grad_lo = split3(node_grad)
    states = jnp.concatenate([next_b, hidden_b], axis=1)
    small = mm(states, grad_hi, 0, 0) + mm(states, grad_lo, 0, 0)
    hidden_grad = mm2(mm2(node_grad, readout_matrix, 1, 1), contract_matrix, 1, 1)
    sigma = jax.nn.sigmoid(hidden_pre)
    pre_hi, pre_lo = split3(hidden_grad * sigma * (1.0 + hidden_pre * (1.0 - sigma)))
    up_part = mm(normed_b, pre_hi, 0, 0) + mm(normed_b, pre_lo, 0, 0)
    state_grad = state_gradient(
        node_grad, mesh_state, hidden_pre, mixing_rescale_factor, expand_matrix, contract_matrix, readout_matrix
    )
    width, hid = up_part.shape
    factor = 1.0 / math.sqrt(band_count * node_rows)
    packed = jnp.concatenate([up_part, small[:width], small[width:]], axis=1)
    packed = jnp.pad(packed, ((0, 0), (0, -packed.shape[1] % 16)))
    total = sum_over_bands(packed, band_count) * factor
    grad_up = total[:, :hid]
    grad_dec = total[:, hid : hid + channels]
    grad_down = mm2(total[:, hid + channels : hid + 2 * channels], readout_matrix, 1, 1)
    grad_gain = jnp.sum(grad_up * expand_matrix.astype(f32), axis=1) / mixing_rescale_factor
    return (
        student_outputs[None],
        state_grad[None],
        grad_up[None],
        grad_down[None],
        grad_dec[None],
        grad_gain[None],
    )


def body(*args):
    field, enc_send, dec_send, expand = args[0], args[4], args[6], args[10]
    bands, cap = enc_send.shape[1:]
    channels, grid_rows = field.shape
    group = LANES // cap
    column = (
        dec_send.shape[2] == cap
        and LANES % cap == 0
        and cap % 16 == 0
        and group * group == bands
        and channels % 16 == 0
        and max(grid_rows, MESH_DEV) <= 256
        and bands * cap * 2 <= TABLE_ROWS * LANES
        and expand.shape[0] == expand.shape[1]
    )
    return column_body(group, *args) if column else band_body(*args)


def solution(mesh):
    return jax.shard_map(
        body,
        mesh=mesh,
        in_specs=(
            P(None, "band"),
            P("member", None, "band"),
            P("member", None, "band"),
            P(None, "band"),
            P("band", None, None),
            P("band", None, None),
            P("band", None, None),
            P("band", None, None),
            P(),
            P(),
            P(),
            P(),
            P(),
        ),
        out_specs=(
            P("member", None, "band"),
            P("member", "band", None),
            P("member", None, None),
            P("member", None, None),
            P("member", None, None),
            P("member", None),
        ),
        check_vma=False,
    )
```

```python
import functools
import math

import jax
import jax.numpy as jnp
from jax import lax
from jax.experimental import pallas as pl
from jax.experimental.pallas import tpu as pltpu
from jax.sharding import PartitionSpec as P


MESH_DEV = 256


smooth_sq = 0.01
norm_eps = 1e-05

bf16 = jnp.bfloat16
f32 = jnp.float32


def slope(diff):
    return diff * lax.rsqrt(diff * diff + smooth_sq)


def mm(a, b, ca, cb):
    return lax.dot_general(a, b, (((ca,), (cb,)), ((), ())), preferred_element_type=f32)


def split3(x):
    hi = x.astype(bf16)
    return hi, (x - hi.astype(f32)).astype(bf16)


def mm2(a, b, ca, cb):
    hi, lo = split3(a)
    return mm(hi, b, ca, cb) + mm(lo, b, ca, cb)


def exchange(x, band_count):
    rows, width = x.shape
    y = lax.all_to_all(
        x.reshape(band_count, rows // band_count, width), "band", split_axis=0, concat_axis=0, tiled=True
    )
    return y.reshape(rows, width)


def sum_over_bands(x, band_count):
    rows, width = x.shape
    parts = lax.all_to_all(
        x.astype(bf16).reshape(band_count, rows // band_count, width),
        "band",
        split_axis=0,
        concat_axis=0,
        tiled=True,
    )
    own = jnp.sum(parts.astype(f32), axis=0).astype(bf16)
    spread = jnp.broadcast_to(own[None], parts.shape)
    full = lax.all_to_all(spread, "band", split_axis=0, concat_axis=0, tiled=True)
    return full.reshape(rows, width).astype(f32)


TABLE_ROWS = 8
LANES = 128


def one_hot(a, b):
    return jnp.where(a == b, 1.0, 0.0).astype(bf16)


def lane_blocks(table, group, rows, row_of):
    bands, cap = table.shape
    r = lax.broadcasted_iota(jnp.int32, (rows, bands), 0)
    b = lax.broadcasted_iota(jnp.int32, (rows, bands), 1)
    slot = lax.broadcasted_iota(jnp.int32, (cap, LANES), 0)
    lane = lax.broadcasted_iota(jnp.int32, (cap, LANES), 1)
    out = jnp.zeros((rows, LANES), f32)
    for j in range(group):
        rows_j = mm(jnp.where(row_of(r, j) == b, 1.0, 0.0).astype(bf16), table, 1, 0).astype(bf16)
        out = out + mm(rows_j, one_hot(lane, slot + j * cap), 1, 0)
    return out


def column_order(table_ref, group):
    table = table_ref[0].astype(f32).astype(bf16)
    crew = table.shape[0] // group
    return lane_blocks(table, group, 8, lambda r, j: jnp.where(r < crew, j * crew + r, -1)), crew


def send_copies(group, crew, block_ref, out_ref, sems):
    return [
        pltpu.make_async_copy(block_ref, out_ref.at[j * crew : (j + 1) * crew], sems.at[j]) for j in range(group)
    ]


def encode_kernel(
    group,
    ready,
    field_ref,
    noise_ref,
    send_ref,
    recv_ref,
    mesh_ref,
    lift_in,
    expand_in,
    contract_in,
    readout_in,
    out_ref,
    table_ref,
    lift_ref,
    expand_ref,
    contract_ref,
    readout_ref,
    block_ref,
    sems,
):
    grid_rows = field_ref.shape[1]
    bands, _ = send_ref.shape[1:]
    rows = bands // group
    pairs = [(lift_in, lift_ref), (expand_in, expand_ref), (contract_in, contract_ref), (readout_in, readout_ref)]
    weights = [pltpu.make_async_copy(a, b, sems.at[i + 1]) for i, (a, b) in enumerate(pairs)]
    for copy in weights:
        copy.start()
    ready(0, 1, 2, 3, 4)
    inputs = (field_ref[...] + noise_ref[0].astype(f32)).astype(bf16) * 0.5

    def in_rows(ref, first):
        table = ref[0].astype(f32).astype(bf16)
        return lane_blocks(
            table,
            group,
            TABLE_ROWS,
            lambda r, j: jnp.where((r >= first) & (r < first + rows), (r - first) * group + j, -1),
        )

    order = in_rows(send_ref, 0)
    table_ref[...] = in_rows(recv_ref, 0) + in_rows(mesh_ref, rows)
    subs = lax.broadcasted_iota(jnp.int32, (grid_rows, LANES), 0).astype(f32)
    pick = jnp.concatenate([one_hot(subs, order[r : r + 1, :]) for r in range(rows)], axis=1)
    block_ref[...] = mm(inputs, pick, 1, 0).T.astype(bf16).reshape(block_ref.shape)
    copy = pltpu.make_async_copy(block_ref, out_ref, sems.at[0])
    copy.start()
    for copy in [copy] + weights:
        copy.wait()


def loss_kernel(group, student_ref, target_ref, weight_ref, inverse_ref, recv_ref, *rest):
    other_refs, (out_ref, block_ref, sems) = rest[:-3], rest[-3:]
    grid_rows = student_ref.shape[1]
    student = student_ref[...]
    terms = jnp.zeros_like(student)
    for j in range(target_ref.shape[0]):
        terms = terms + slope(student - target_ref[j].astype(f32))
    for other_ref in (student_ref,) + other_refs:
        terms = terms - slope(student - other_ref[...])
    scaled = (weight_ref[...].astype(f32) * terms * inverse_ref[...]).astype(bf16)
    order, crew = column_order(recv_ref, group)
    subs = lax.broadcasted_iota(jnp.int32, (grid_rows, LANES), 0).astype(f32)
    for c in range(crew):
        block_ref[c] = mm(scaled, one_hot(subs, order[c : c + 1, :]), 1, 0).astype(bf16)
    copies = send_copies(group, crew, block_ref, out_ref, sems)
    for copy in copies:
        copy.start()
    for copy in copies:
        copy.wait()


def node_forward(cells, channel_dim, table, scale_ref, expand_ref, contract_ref, lift_ref, ready, keep=None):
    node_rows = MESH_DEV
    slots = cells.shape[1 - channel_dim]
    subs = lax.broadcasted_iota(jnp.int32, (node_rows, LANES), 0).astype(f32)
    latent = mm(cells, lift_ref[...], channel_dim, 0)
    latent = (latent + latent * jnp.tanh(latent)).astype(bf16)
    parts = slots // LANES
    landing = jnp.concatenate([one_hot(subs, table[j : j + 1, :]) for j in range(parts)], axis=1)
    count = mm(landing, jnp.ones((slots, LANES), bf16), 1, 0)[:, 0:1]
    state = mm(landing, latent, 1, 0) * (1.0 / jnp.maximum(count, 1.0))
    recip = lax.rsqrt(jnp.mean(state * state, axis=1, keepdims=True) + norm_eps)
    if keep:
        keep(2, state)
    ready()
    normed = (state * recip * scale_ref[...]).astype(bf16)
    if keep:
        keep(4, normed)
    pre = mm(normed, expand_ref[...], 1, 0)
    if keep:
        keep(3, pre)
    bent = jnp.tanh(pre)
    above = 1.0 + bent
    bend = (above * (1.0 + pre * (1.0 - bent))).astype(bf16)
    if keep:
        keep(5, bend)
    hidden = (pre * above).astype(bf16)
    following = (state + mm(hidden, contract_ref[...], 1, 0)).astype(bf16)
    return state, pre, normed, bend, following, hidden


def own_kernel(
    channels,
    ready,
    cells_ref,
    table_ref,
    lift_ref,
    expand_ref,
    contract_ref,
    readout_ref,
    scale_ref,
    chosen_ref,
    *rest,
):
    count = len(rest) // 2
    out_refs, bufs, sems = (chosen_ref,) + rest[: count - 1], rest[count - 1 : -1], rest[-1]
    copies = [pltpu.make_async_copy(a, b, sems.at[i]) for i, (a, b) in enumerate(zip(bufs, out_refs))]
    chosen_buf, parcel_buf, _, _, _, _, both_buf = bufs
    slots = cells_ref.shape[0]
    width = both_buf.shape[1] // 2
    parts = slots // LANES
    table = table_ref[...]
    parcel_buf[0:channels, :] = cells_ref[...].astype(f32).T.astype(bf16)
    parcel_buf[channels:, :] = jnp.concatenate([table] * parts, axis=1).astype(bf16)
    copies[1].start()

    def keep(at, value):
        bufs[at][...] = value
        copies[at].start()

    state, _, _, _, following, hidden = node_forward(
        cells_ref[...],
        1,
        table,
        scale_ref,
        expand_ref,
        contract_ref,
        lift_ref,
        lambda: ready(6),
        keep,
    )
    both_buf[:, 0:width] = following
    both_buf[:, width:] = hidden
    copies[6].start()
    projected = mm(following, readout_ref[...], 1, 1).astype(bf16)
    subs = lax.broadcasted_iota(jnp.int32, (state.shape[0], LANES), 0).astype(f32)
    for j in range(parts):
        pick = one_hot(subs, table[parts + j : parts + j + 1, :])
        chosen_buf[j * LANES : (j + 1) * LANES, :] = mm(pick, projected, 0, 0).astype(bf16)
    copies[0].start()
    for copy in copies:
        copy.wait()


def mates_kernel(
    channels,
    ready,
    lift_ref,
    scale_ref,
    expand_ref,
    contract_ref,
    parcel_ref,
    normed_ref,
    bend_ref,
    both_out,
    table_ref,
    both_buf,
    sems,
):
    mates = table_ref.shape[0]
    width = both_buf.shape[2] // 2
    ready(*range(5))
    copies = [pltpu.make_async_copy(both_buf.at[m], both_out.at[m], sems.at[m]) for m in range(mates)]
    for m in range(mates):
        table = parcel_ref[m, channels:, 0:LANES].astype(f32)
        table_ref[m] = table
        _, _, normed, bend, following, hidden = node_forward(
            parcel_ref[m, 0:channels, :], 0, table, scale_ref, expand_ref, contract_ref, lift_ref, lambda: None
        )
        normed_ref[m] = normed
        bend_ref[m] = bend
        both_buf[m, :, 0:width] = following
        both_buf[m, :, width:] = hidden
        copies[m].start()
    for copy in copies:
        copy.wait()


def backward_kernel(
    group,
    channels,
    mate_count,
    me_ref,
    grad_ref,
    chain_ref,
    table_ref,
    normed_ref,
    bend_ref,
    both_ref,
    *rest,
):
    mate_refs, own_ref, piece_refs = rest[:mate_count], rest[mate_count], rest[mate_count + 1 : -8]
    value_ref, node_ref, up_ref, small_ref, normed_buf, bend_buf, both_buf, sems = rest[-8:]
    bands = grad_ref.shape[0]
    slots = value_ref.shape[1]
    node_rows = normed_ref.shape[0]
    cap = slots // bands
    z, xy = me_ref[0], me_ref[1]
    subs = lax.broadcasted_iota(jnp.int32, (node_rows, LANES), 0).astype(f32)
    held = [(table_ref[...], bend_ref, normed_ref, both_ref)]
    for at in range(0, mate_count, 4):
        mate_normed, mate_bend, mate_both, mate_table = mate_refs[at : at + 4]
        held += [
            (mate_table[m], mate_bend.at[m], mate_normed.at[m], mate_both.at[m]) for m in range(mate_table.shape[0])
        ]
    copies = [
        [
            pltpu.make_async_copy(ref, buf.at[s], sems.at[i, s])
            for i, (ref, buf) in enumerate(zip(held[s][1:], (bend_buf, normed_buf, both_buf)))
        ]
        for s in range(group)
    ]
    for line in copies:
        for copy in line:
            copy.start()

    def turn(b, carry):
        values = grad_ref[b].astype(f32).T.astype(bf16)
        value_ref[:, pl.ds(pl.multiple_of(b * cap, cap), cap), :] = values.reshape(group, cap, channels)
        return carry

    lax.fori_loop(0, bands, turn, 0, unroll=4)
    parts = slots // LANES
    for s in range(group):
        table = held[s][0]
        pick = jnp.concatenate(
            [one_hot(subs, table[parts + j : parts + j + 1, :]) for j in range(parts)], axis=1
        )
        node_grad = mm(pick, value_ref[z ^ s], 1, 0)
        if s == 0:
            own_ref[...] = node_grad
        node_b = node_grad.astype(bf16)
        node_ref[s * node_rows : (s + 1) * node_rows, :] = node_b
        copies[s][0].wait()
        pre = mm(node_b, chain_ref[...], 1, 0)
        bend_buf[s] = (pre * bend_buf[s].astype(f32)).astype(bf16)
    for line in copies:
        for copy in line[1:]:
            copy.wait()
    everything = (group * node_rows, -1)
    up_ref[...] = 2.0 * mm(normed_buf[...].reshape(everything), bend_buf[...].reshape(everything), 0, 0)
    small_ref[...] = mm(node_ref[...], both_buf[...].reshape(everything), 0, 0)
    count = len(piece_refs)
    rows = up_ref.shape[0] // count
    half = up_ref.shape[1] // 2
    lanes = small_ref.shape[1] // count
    for p, piece_ref in enumerate(piece_refs):
        to = xy ^ p
        at = pl.ds(pl.multiple_of(to * rows, rows), rows)
        piece_ref[0:rows, :] = up_ref[at, 0:half].astype(bf16)
        piece_ref[rows : 2 * rows, :] = up_ref[at, half:].astype(bf16)
        piece_ref[2 * rows :, :] = small_ref[:, pl.ds(pl.multiple_of(to * lanes, lanes), lanes)].astype(bf16)


def finish_kernel(factor, me_ref, scale_ref, expand_ref, readout_ref, *rest):
    count = len(rest) - 11
    piece_refs = rest[:count]
    up_out, down_out, dec_out, gain_out, small_ref, up_ref, down_ref, dec_ref, gain_ref, sems, last_sems = rest[count:]
    rows = up_ref.shape[0] // count
    half = up_ref.shape[1] // 2
    lanes = small_ref.shape[1] // count
    width = up_ref.shape[0]
    places = [pl.ds(pl.multiple_of((me_ref[1] ^ p) * rows, rows), rows) for p in range(count)]
    up_copies = [pltpu.make_async_copy(up_ref.at[at], up_out.at[at], sems.at[0, p]) for p, at in enumerate(places)]
    down_copies = [
        pltpu.make_async_copy(down_ref.at[at], down_out.at[at], sems.at[1, p])
        for p, at in enumerate(pl.ds(p * rows, rows) for p in range(count))
    ]
    for p, piece_ref in enumerate(piece_refs):
        up_ref[places[p], 0:half] = piece_ref[0:rows, :].astype(f32) * factor
        up_ref[places[p], half:] = piece_ref[rows : 2 * rows, :].astype(f32) * factor
        up_copies[p].start()
        at = pl.ds(pl.multiple_of((me_ref[1] ^ p) * lanes, lanes), lanes)
        small_ref[:, at] = piece_ref[2 * rows :, :].astype(f32) * factor
    dec_ref[...] = small_ref[:, 0:width]
    last_copies = [
        pltpu.make_async_copy(dec_ref, dec_out, last_sems.at[0]),
        pltpu.make_async_copy(gain_ref, gain_out, last_sems.at[1]),
    ]
    last_copies[0].start()
    high = small_ref[:, width:].astype(bf16)
    low = (small_ref[:, width:] - high.astype(f32)).astype(bf16)
    for p in range(count):
        at = slice(p * rows, (p + 1) * rows)
        down_ref[at, :] = mm(high[:, at], readout_ref[...], 0, 0) + mm(low[:, at], readout_ref[...], 0, 0)
        down_copies[p].start()
    for at in places:
        gain = up_ref[at, :] * expand_ref[at, :].astype(f32)
        gain = sum(gain[:, j : j + LANES] for j in range(0, 2 * half, LANES))
        gain_ref[:, at] = jnp.sum(gain.T, axis=0, keepdims=True) / scale_ref[:, at]
    last_copies[1].start()
    for copy in up_copies + down_copies + last_copies:
        copy.wait()


def vmem_call(kernel, outs, scratch=(), sems=(), budget=24, left_in=(), left_out=(), fetched=(), vmem_in=(), vmem_out=()):
    vmem = pl.BlockSpec(memory_space=pltpu.VMEM)
    smem = pl.BlockSpec(memory_space=pltpu.SMEM)
    left = pl.BlockSpec(memory_space=pltpu.HBM)
    fetched = list(fetched)

    def call(scalars, *operands):
        first = 0 if scalars is None else 1
        outside = set(left_in) | set(fetched)

        def run(*refs):
            refs = list(refs)
            if fetched:
                bufs, sem = refs[-1 - len(fetched) : -1], refs[-1]
                refs = refs[: -1 - len(fetched)]
                copies = {
                    at: pltpu.make_async_copy(refs[first + at], buf, sem.at[i])
                    for i, (at, buf) in enumerate(zip(fetched, bufs))
                }
                for at, buf in zip(fetched, bufs):
                    copies[at].start()
                    refs[first + at] = buf

                def ready(*which):
                    for at in which:
                        copies[at].wait()

                kernel(ready, *refs)
            else:
                kernel(*refs)

        return pl.pallas_call(
            run,
            out_shape=[
                (pltpu.HBM if i in left_out else pltpu.VMEM if i in vmem_out else jax.ShapeDtypeStruct)(s, d)
                for i, (s, d) in enumerate(outs)
            ],
            in_specs=[smem] * first + [left if i in outside else vmem for i in range(len(operands))],
            out_specs=[left if i in left_out else vmem for i in range(len(outs))],
            scratch_shapes=[pltpu.VMEM(s, d) for s, d in scratch]
            + [pltpu.SemaphoreType.DMA(s) for s in sems]
            + [pltpu.VMEM(operands[i].shape, operands[i].dtype) for i in fetched]
            + ([pltpu.SemaphoreType.DMA((len(fetched),))] if fetched else []),
            compiler_params=pltpu.CompilerParams(vmem_limit_bytes=budget * 2**20),
        )(
            *([] if scalars is None else [scalars]),
            *[
                pltpu.with_memory_space_constraint(x, pltpu.HBM)
                if i in outside
                else pltpu.with_memory_space_constraint(x, pltpu.VMEM)
                if i in vmem_in
                else x
                for i, x in enumerate(operands)
            ],
        )

    return call


def all_to_all(x):
    return lax.all_to_all(x, "band", split_axis=0, concat_axis=0, tiled=True)


def member_terms(student_outputs, target, weight_map):
    all_pred, all_target = (
        lax.all_gather(student_outputs[None], "member", axis=0, tiled=True),
        lax.all_gather(target, "member", axis=0, tiled=True),
    )
    teacher_terms = jnp.sum(slope(student_outputs[None] - all_target.astype(f32)), axis=0)
    own_terms = jnp.sum(slope(student_outputs[None] - all_pred), axis=0)
    return weight_map.astype(f32) * (teacher_terms - own_terms)


def state_gradient(node_grad, mesh_state, hidden_pre, scale, expand, contract, readout):
    recip = lax.rsqrt(jnp.mean(mesh_state * mesh_state, axis=1, keepdims=True) + norm_eps)
    next_grad = mm2(node_grad, readout, 1, 1)
    hidden_grad = mm2(next_grad, contract, 1, 1)
    sigma = jax.nn.sigmoid(hidden_pre)
    pre_grad = hidden_grad * sigma * (1.0 + hidden_pre * (1.0 - sigma))
    normed_grad = mm2(pre_grad, expand, 1, 1)
    gained = normed_grad * scale
    return (
        next_grad
        + recip * gained
        - mesh_state * (recip * recip * recip) * jnp.mean(gained * mesh_state, axis=1, keepdims=True)
    ).astype(bf16)


def column_body(
    group,
    scaled_atmosphere_field,
    perturbation,
    target,
    weight_map,
    enc_send,
    enc_recv,
    dec_send,
    dec_recv,
    lattice_lift_matrix,
    mixing_rescale_factor,
    expand_matrix,
    contract_matrix,
    readout_matrix,
):
    bands = lax.axis_size("band")
    channels, grid_rows = scaled_atmosphere_field.shape
    node_rows = MESH_DEV
    width, hid = expand_matrix.shape
    slots = bands * enc_send.shape[2]
    crew = bands // group
    band = lax.axis_index("band").astype(jnp.int32)
    me = jnp.stack([band // crew, band % crew])
    cell_ids = jnp.arange(grid_rows, dtype=jnp.int32)
    cap = enc_send.shape[2]
    block = ((bands, cap, channels), bf16)
    weights = (lattice_lift_matrix, expand_matrix, contract_matrix, readout_matrix.T)
    outgoing, table, *near_weights = vmem_call(
        functools.partial(encode_kernel, group),
        [block, ((TABLE_ROWS, LANES), f32)] + [(w.shape, w.dtype) for w in weights],
        scratch=[block],
        sems=[(5,)],
        left_in=range(5, 9),
        left_out=(0,),
        vmem_out=range(2, 6),
        fetched=range(5),
    )(None, scaled_atmosphere_field, perturbation, enc_send, enc_recv, dec_send, *weights)
    arrived = all_to_all(outgoing).reshape(slots, channels)
    half_scale = 0.5 * mixing_rescale_factor[None, :]
    kept = [((node_rows, width), bf16), ((node_rows, hid), bf16), ((node_rows, width + hid), bf16)]
    sent = [((slots, channels), bf16), ((channels + TABLE_ROWS, slots), bf16), ((node_rows, width), f32), ((node_rows, hid), f32)] + kept
    chosen, parcel, mesh_state, half_pre, normed, bend, both = vmem_call(
        functools.partial(own_kernel, channels),
        sent,
        scratch=sent,
        sems=[(len(sent),)],
        left_out=range(len(sent)),
        fetched=(6,),
        vmem_in=(2, 3, 4, 5),
    )(None, arrived, table, *near_weights, half_scale)
    parcels, mates = parcel[None], []
    while parcels.shape[0] < group:
        held = parcels.shape[0]
        more = lax.ppermute(parcels, "band", [(i, i ^ (held * crew)) for i in range(bands)])
        parcels = jnp.concatenate([parcels, more])
        mate_kept = [((held,) + shape, dtype) for shape, dtype in kept]
        mates += vmem_call(
            functools.partial(mates_kernel, channels),
            mate_kept + [((held, TABLE_ROWS, LANES), f32)],
            scratch=mate_kept[2:],
            sems=[(held,)],
            left_out=(2,),
            vmem_out=(0, 1),
            fetched=range(5),
        )(None, lattice_lift_matrix, half_scale, expand_matrix, contract_matrix, more)
    chain = (0.5 * mm(readout_matrix, contract_matrix, 0, 1)).astype(bf16)
    slot_values = exchange(chosen, bands)
    fill_map = (cell_ids[:, None] == dec_recv[0].reshape(-1)[None, :]).astype(bf16)
    inverse = 1.0 / jnp.maximum(jnp.sum(fill_map.astype(f32), axis=1), 1.0)
    student_outputs = scaled_atmosphere_field + mm(slot_values, fill_map, 0, 1) * inverse[None, :]
    members = lax.axis_size("member")
    turns = [[(m, (m + t) % members) for m in range(members)] for t in range(1, members)]
    others = [lax.ppermute(student_outputs, "member", turn) for turn in turns]
    all_target = lax.all_gather(target[0], "member", axis=0)
    outgoing = vmem_call(
        functools.partial(loss_kernel, group),
        [((bands, channels, LANES), bf16)],
        scratch=[((crew, channels, LANES), bf16)],
        sems=[(group,)],
        left_out=(0,),
    )(None, student_outputs, all_target, weight_map, inverse[None, :], dec_recv, *others)[0]
    returned = all_to_all(outgoing)
    piece_rows = 2 * (width // crew) + channels
    node_grad, *pieces = vmem_call(
        functools.partial(backward_kernel, group, channels, len(mates)),
        [((node_rows, channels), f32)] + [((piece_rows, hid // 2), bf16)] * crew,
        scratch=[
            ((group, slots, channels), bf16),
            ((group * node_rows, channels), bf16),
            ((width, hid), f32),
            ((channels, width + hid), f32),
        ]
        + [((group,) + shape, dtype) for shape, dtype in kept],
        sems=[(3, group)],
        left_in=[3, 4, 5] + [6 + i for i in range(len(mates)) if i % 4 == 2],
        vmem_in=[6 + i for i in range(len(mates)) if i % 4 < 2],
    )(me, returned, chain, table, normed, bend, both, *mates)
    swaps = [[(i, i ^ p) for i in range(bands)] for p in range(1, crew)]
    others = [lax.ppermute(piece, "band", swap) for piece, swap in zip(pieces[1:], swaps)]
    total = sum(x.astype(f32) for x in [pieces[0]] + others).astype(bf16)
    totals = [total] + [lax.ppermute(total, "band", swap) for swap in swaps]
    state_grad = state_gradient(
        node_grad,
        mesh_state,
        2.0 * half_pre,
        mixing_rescale_factor,
        expand_matrix,
        contract_matrix,
        readout_matrix,
    )
    factor = 1.0 / math.sqrt(bands * node_rows)
    whole = [((width, hid), f32), ((hid, width), f32), ((channels, width), f32), ((1, width), f32)]
    grad_up, grad_down, grad_dec, grad_gain = vmem_call(
        functools.partial(finish_kernel, factor),
        whole,
        scratch=[((channels, width + hid), f32)] + whole,
        sems=[(2, crew), (2,)],
        left_out=range(4),
    )(me, mixing_rescale_factor[None, :], expand_matrix, readout_matrix.T, *totals)
    return (
        student_outputs[None],
        state_grad[None],
        grad_up[None],
        grad_down[None],
        grad_dec.T[None],
        grad_gain,
    )


def band_body(
    scaled_atmosphere_field,
    perturbation,
    target,
    weight_map,
    enc_send,
    enc_recv,
    dec_send,
    dec_recv,
    lattice_lift_matrix,
    mixing_rescale_factor,
    expand_matrix,
    contract_matrix,
    readout_matrix,
):
    band_count = lax.axis_size("band")
    channels, grid_rows = scaled_atmosphere_field.shape
    node_rows = MESH_DEV
    cell_ids = jnp.arange(grid_rows, dtype=jnp.int32)
    node_ids = jnp.arange(node_rows, dtype=jnp.int32)
    inputs_b = (scaled_atmosphere_field + perturbation[0].astype(f32)).astype(bf16)
    picker = (enc_send[0].reshape(-1)[:, None] == cell_ids[None, :]).astype(bf16)
    outgoing = mm(picker, inputs_b, 1, 1).astype(bf16)
    arrived = exchange(outgoing, band_count)
    slot_rows = jax.nn.silu(mm(arrived, lattice_lift_matrix, 1, 0)).astype(bf16)
    landing = (node_ids[:, None] == enc_recv[0].reshape(-1)[None, :]).astype(bf16)
    edge_count = jnp.sum(landing.astype(f32), axis=1, keepdims=True)
    mesh_state = mm(landing, slot_rows, 1, 0) / jnp.maximum(edge_count, 1.0)
    recip = lax.rsqrt(jnp.mean(mesh_state * mesh_state, axis=1, keepdims=True) + norm_eps)
    normed_b = (mesh_state * recip * mixing_rescale_factor).astype(bf16)
    hidden_pre = mm(normed_b, expand_matrix, 1, 0)
    hidden_b = jax.nn.silu(hidden_pre).astype(bf16)
    next_b = (mesh_state + mm(hidden_b, contract_matrix, 1, 0)).astype(bf16)
    mesh_picker = (dec_send[0].reshape(-1)[:, None] == node_ids[None, :]).astype(bf16)
    fill_map = (cell_ids[:, None] == dec_recv[0].reshape(-1)[None, :]).astype(bf16)
    inverse = 1.0 / jnp.maximum(jnp.sum(fill_map.astype(f32), axis=1), 1.0)
    projected = mm(next_b, readout_matrix, 1, 0).astype(bf16)
    chosen = mm(mesh_picker, projected, 1, 0).astype(bf16)
    slot_values = exchange(chosen, band_count)
    grid_sum = mm(slot_values, fill_map, 0, 1)
    student_outputs = scaled_atmosphere_field + grid_sum * inverse[None, :]
    pred_grad = member_terms(student_outputs, target, weight_map)
    scaled = (pred_grad * inverse[None, :]).astype(bf16)
    slot_grad = mm(fill_map, scaled, 0, 1).astype(bf16)
    returned = exchange(slot_grad, band_count)
    node_grad = mm(mesh_picker, returned, 0, 0)
    grad_hi, grad_lo = split3(node_grad)
    states = jnp.concatenate([next_b, hidden_b], axis=1)
    small = mm(states, grad_hi, 0, 0) + mm(states, grad_lo, 0, 0)
    hidden_grad = mm2(mm2(node_grad, readout_matrix, 1, 1), contract_matrix, 1, 1)
    sigma = jax.nn.sigmoid(hidden_pre)
    pre_hi, pre_lo = split3(hidden_grad * sigma * (1.0 + hidden_pre * (1.0 - sigma)))
    up_part = mm(normed_b, pre_hi, 0, 0) + mm(normed_b, pre_lo, 0, 0)
    state_grad = state_gradient(
        node_grad, mesh_state, hidden_pre, mixing_rescale_factor, expand_matrix, contract_matrix, readout_matrix
    )
    width, hid = up_part.shape
    factor = 1.0 / math.sqrt(band_count * node_rows)
    packed = jnp.concatenate([up_part, small[:width], small[width:]], axis=1)
    packed = jnp.pad(packed, ((0, 0), (0, -packed.shape[1] % 16)))
    total = sum_over_bands(packed, band_count) * factor
    grad_up = total[:, :hid]
    grad_dec = total[:, hid : hid + channels]
    grad_down = mm2(total[:, hid + channels : hid + 2 * channels], readout_matrix, 1, 1)
    grad_gain = jnp.sum(grad_up * expand_matrix.astype(f32), axis=1) / mixing_rescale_factor
    return (
        student_outputs[None],
        state_grad[None],
        grad_up[None],
        grad_down[None],
        grad_dec[None],
        grad_gain[None],
    )


def body(*args):
    field, enc_send, dec_send, expand = args[0], args[4], args[6], args[10]
    bands, cap = enc_send.shape[1:]
    channels, grid_rows = field.shape
    group = LANES // cap
    column = (
        dec_send.shape[2] == cap
        and LANES % cap == 0
        and cap % 16 == 0
        and group * group == bands
        and channels % 16 == 0
        and max(grid_rows, MESH_DEV) <= 256
        and bands * cap * 2 <= TABLE_ROWS * LANES
        and expand.shape[0] == expand.shape[1]
    )
    return column_body(group, *args) if column else band_body(*args)


def solution(mesh):
    return jax.shard_map(
        body,
        mesh=mesh,
        in_specs=(
            P(None, "band"),
            P("member", None, "band"),
            P("member", None, "band"),
            P(None, "band"),
            P("band", None, None),
            P("band", None, None),
            P("band", None, None),
            P("band", None, None),
            P(),
            P(),
            P(),
            P(),
            P(),
        ),
        out_specs=(
            P("member", None, "band"),
            P("member", "band", None),
            P("member", None, None),
            P("member", None, None),
            P("member", None, None),
            P("member", None),
        ),
        check_vma=False,
    )
```

```python
import functools
import math

import jax
import jax.numpy as jnp
from jax import lax
from jax.experimental import pallas as pl
from jax.experimental.pallas import tpu as pltpu
from jax.sharding import PartitionSpec as P


MESH_DEV = 256


smooth_sq = 0.01
norm_eps = 1e-05

bf16 = jnp.bfloat16
f32 = jnp.float32


def slope(diff):
    return diff * lax.rsqrt(diff * diff + smooth_sq)


def mm(a, b, ca, cb):
    return lax.dot_general(a, b, (((ca,), (cb,)), ((), ())), preferred_element_type=f32)


def split3(x):
    hi = x.astype(bf16)
    return hi, (x - hi.astype(f32)).astype(bf16)


def mm2(a, b, ca, cb):
    hi, lo = split3(a)
    return mm(hi, b, ca, cb) + mm(lo, b, ca, cb)


def exchange(x, band_count):
    rows, width = x.shape
    y = lax.all_to_all(
        x.reshape(band_count, rows // band_count, width), "band", split_axis=0, concat_axis=0, tiled=True
    )
    return y.reshape(rows, width)


def sum_over_bands(x, band_count):
    rows, width = x.shape
    parts = lax.all_to_all(
        x.astype(bf16).reshape(band_count, rows // band_count, width),
        "band",
        split_axis=0,
        concat_axis=0,
        tiled=True,
    )
    own = jnp.sum(parts.astype(f32), axis=0).astype(bf16)
    spread = jnp.broadcast_to(own[None], parts.shape)
    full = lax.all_to_all(spread, "band", split_axis=0, concat_axis=0, tiled=True)
    return full.reshape(rows, width).astype(f32)


TABLE_ROWS = 8
LANES = 128


def one_hot(a, b):
    return jnp.where(a == b, 1.0, 0.0).astype(bf16)


def lane_blocks(table, group, rows, row_of):
    bands, cap = table.shape
    r = lax.broadcasted_iota(jnp.int32, (rows, bands), 0)
    b = lax.broadcasted_iota(jnp.int32, (rows, bands), 1)
    slot = lax.broadcasted_iota(jnp.int32, (cap, LANES), 0)
    lane = lax.broadcasted_iota(jnp.int32, (cap, LANES), 1)
    out = jnp.zeros((rows, LANES), f32)
    for j in range(group):
        rows_j = mm(jnp.where(row_of(r, j) == b, 1.0, 0.0).astype(bf16), table, 1, 0).astype(bf16)
        out = out + mm(rows_j, one_hot(lane, slot + j * cap), 1, 0)
    return out


def column_order(table_ref, group):
    table = table_ref[0].astype(f32).astype(bf16)
    crew = table.shape[0] // group
    return lane_blocks(table, group, 8, lambda r, j: jnp.where(r < crew, j * crew + r, -1)), crew


def send_copies(group, crew, block_ref, out_ref, sems):
    return [
        pltpu.make_async_copy(block_ref, out_ref.at[j * crew : (j + 1) * crew], sems.at[j]) for j in range(group)
    ]


def encode_kernel(
    group,
    ready,
    field_ref,
    noise_ref,
    send_ref,
    recv_ref,
    mesh_ref,
    lift_in,
    expand_in,
    contract_in,
    readout_in,
    out_ref,
    table_ref,
    lift_ref,
    expand_ref,
    contract_ref,
    readout_ref,
    block_ref,
    sems,
):
    grid_rows = field_ref.shape[1]
    bands, _ = send_ref.shape[1:]
    rows = bands // group
    pairs = [(lift_in, lift_ref), (expand_in, expand_ref), (contract_in, contract_ref), (readout_in, readout_ref)]
    weights = [pltpu.make_async_copy(a, b, sems.at[i + 1]) for i, (a, b) in enumerate(pairs)]
    for copy in weights:
        copy.start()
    ready(0, 1, 2, 3, 4)
    inputs = (field_ref[...] + noise_ref[0].astype(f32)).astype(bf16) * 0.5

    def in_rows(ref, first):
        table = ref[0].astype(f32).astype(bf16)
        return lane_blocks(
            table,
            group,
            TABLE_ROWS,
            lambda r, j: jnp.where((r >= first) & (r < first + rows), (r - first) * group + j, -1),
        )

    order = in_rows(send_ref, 0)
    table_ref[...] = in_rows(recv_ref, 0) + in_rows(mesh_ref, rows)
    subs = lax.broadcasted_iota(jnp.int32, (grid_rows, LANES), 0).astype(f32)
    pick = jnp.concatenate([one_hot(subs, order[r : r + 1, :]) for r in range(rows)], axis=1)
    block_ref[...] = mm(inputs, pick, 1, 0).T.astype(bf16).reshape(block_ref.shape)
    copy = pltpu.make_async_copy(block_ref, out_ref, sems.at[0])
    copy.start()
    for copy in [copy] + weights:
        copy.wait()


def loss_kernel(group, student_ref, target_ref, weight_ref, inverse_ref, recv_ref, *rest):
    other_refs, (out_ref, block_ref, sems) = rest[:-3], rest[-3:]
    grid_rows = student_ref.shape[1]
    student = student_ref[...]
    terms = jnp.zeros_like(student)
    for j in range(target_ref.shape[0]):
        terms = terms + slope(student - target_ref[j].astype(f32))
    for other_ref in (student_ref,) + other_refs:
        terms = terms - slope(student - other_ref[...])
    scaled = (weight_ref[...].astype(f32) * terms * inverse_ref[...]).astype(bf16)
    order, crew = column_order(recv_ref, group)
    subs = lax.broadcasted_iota(jnp.int32, (grid_rows, LANES), 0).astype(f32)
    for c in range(crew):
        block_ref[c] = mm(scaled, one_hot(subs, order[c : c + 1, :]), 1, 0).astype(bf16)
    copies = send_copies(group, crew, block_ref, out_ref, sems)
    for copy in copies:
        copy.start()
    for copy in copies:
        copy.wait()


def node_forward(cells, channel_dim, table, scale_ref, expand_ref, contract_ref, lift_ref, ready, keep=None):
    node_rows = MESH_DEV
    slots = cells.shape[1 - channel_dim]
    subs = lax.broadcasted_iota(jnp.int32, (node_rows, LANES), 0).astype(f32)
    latent = mm(cells, lift_ref[...], channel_dim, 0)
    latent = (latent + latent * jnp.tanh(latent)).astype(bf16)
    parts = slots // LANES
    landing = jnp.concatenate([one_hot(subs, table[j : j + 1, :]) for j in range(parts)], axis=1)
    count = mm(landing, jnp.ones((slots, LANES), bf16), 1, 0)[:, 0:1]
    state = mm(landing, latent, 1, 0) * (1.0 / jnp.maximum(count, 1.0))
    recip = lax.rsqrt(jnp.mean(state * state, axis=1, keepdims=True) + norm_eps)
    if keep:
        keep(2, state)
    ready()
    normed = (state * recip * scale_ref[...]).astype(bf16)
    if keep:
        keep(4, normed)
    pre = mm(normed, expand_ref[...], 1, 0)
    if keep:
        keep(3, pre)
    bent = jnp.tanh(pre)
    above = 1.0 + bent
    bend = (above * (1.0 + pre * (1.0 - bent))).astype(bf16)
    if keep:
        keep(5, bend)
    hidden = (pre * above).astype(bf16)
    following = (state + mm(hidden, contract_ref[...], 1, 0)).astype(bf16)
    return state, pre, normed, bend, following, hidden


def own_kernel(
    channels,
    ready,
    cells_ref,
    table_ref,
    lift_ref,
    expand_ref,
    contract_ref,
    readout_ref,
    scale_ref,
    chosen_ref,
    *rest,
):
    count = len(rest) // 2
    out_refs, bufs, sems = (chosen_ref,) + rest[: count - 1], rest[count - 1 : -1], rest[-1]
    copies = [pltpu.make_async_copy(a, b, sems.at[i]) for i, (a, b) in enumerate(zip(bufs, out_refs))]
    chosen_buf, parcel_buf, _, _, _, _, both_buf = bufs
    slots = cells_ref.shape[0]
    width = both_buf.shape[1] // 2
    parts = slots // LANES
    table = table_ref[...]
    parcel_buf[0:channels, :] = cells_ref[...].astype(f32).T.astype(bf16)
    parcel_buf[channels:, :] = jnp.concatenate([table] * parts, axis=1).astype(bf16)
    copies[1].start()

    def keep(at, value):
        bufs[at][...] = value
        copies[at].start()

    state, _, _, _, following, hidden = node_forward(
        cells_ref[...],
        1,
        table,
        scale_ref,
        expand_ref,
        contract_ref,
        lift_ref,
        lambda: ready(6),
        keep,
    )
    both_buf[:, 0:width] = following
    both_buf[:, width:] = hidden
    copies[6].start()
    projected = mm(following, readout_ref[...], 1, 1).astype(bf16)
    subs = lax.broadcasted_iota(jnp.int32, (state.shape[0], LANES), 0).astype(f32)
    for j in range(parts):
        pick = one_hot(subs, table[parts + j : parts + j + 1, :])
        chosen_buf[j * LANES : (j + 1) * LANES, :] = mm(pick, projected, 0, 0).astype(bf16)
    copies[0].start()
    for copy in copies:
        copy.wait()


def mates_kernel(
    channels,
    ready,
    lift_ref,
    scale_ref,
    expand_ref,
    contract_ref,
    parcel_ref,
    normed_ref,
    bend_ref,
    both_out,
    table_ref,
    both_buf,
    sems,
):
    mates = table_ref.shape[0]
    width = both_buf.shape[2] // 2
    ready(*range(5))
    copies = [pltpu.make_async_copy(both_buf.at[m], both_out.at[m], sems.at[m]) for m in range(mates)]
    for m in range(mates):
        table = parcel_ref[m, channels:, 0:LANES].astype(f32)
        table_ref[m] = table
        _, _, normed, bend, following, hidden = node_forward(
            parcel_ref[m, 0:channels, :], 0, table, scale_ref, expand_ref, contract_ref, lift_ref, lambda: None
        )
        normed_ref[m] = normed
        bend_ref[m] = bend
        both_buf[m, :, 0:width] = following
        both_buf[m, :, width:] = hidden
        copies[m].start()
    for copy in copies:
        copy.wait()


def backward_kernel(
    group,
    channels,
    mate_count,
    grad_ref,
    chain_ref,
    table_ref,
    normed_ref,
    bend_ref,
    both_ref,
    *rest,
):
    mate_refs, own_ref, piece_refs = rest[:mate_count], rest[mate_count], rest[mate_count + 1 : -8]
    value_ref, node_ref, up_ref, small_ref, normed_buf, bend_buf, both_buf, sems = rest[-8:]
    bands = grad_ref.shape[0]
    slots = value_ref.shape[1]
    node_rows = normed_ref.shape[0]
    cap = slots // bands
    crew = grad_ref.shape[0] // group
    band = lax.axis_index("band")
    z, xy = band // crew, band % crew
    subs = lax.broadcasted_iota(jnp.int32, (node_rows, LANES), 0).astype(f32)
    held = [(table_ref[...], bend_ref, normed_ref, both_ref)]
    for at in range(0, mate_count, 4):
        mate_normed, mate_bend, mate_both, mate_table = mate_refs[at : at + 4]
        held += [
            (mate_table[m], mate_bend.at[m], mate_normed.at[m], mate_both.at[m]) for m in range(mate_table.shape[0])
        ]
    copies = [
        [
            pltpu.make_async_copy(ref, buf.at[s], sems.at[i, s])
            for i, (ref, buf) in enumerate(zip(held[s][1:], (bend_buf, normed_buf, both_buf)))
        ]
        for s in range(group)
    ]
    for line in copies:
        for copy in line:
            copy.start()

    def turn(b, carry):
        values = grad_ref[b].astype(f32).T.astype(bf16)
        value_ref[:, pl.ds(pl.multiple_of(b * cap, cap), cap), :] = values.reshape(group, cap, channels)
        return carry

    lax.fori_loop(0, bands, turn, 0, unroll=True)
    parts = slots // LANES
    for s in range(group):
        table = held[s][0]
        pick = jnp.concatenate(
            [one_hot(subs, table[parts + j : parts + j + 1, :]) for j in range(parts)], axis=1
        )
        node_grad = mm(pick, value_ref[z ^ s], 1, 0)
        if s == 0:
            own_ref[...] = node_grad
        node_b = node_grad.astype(bf16)
        node_ref[s * node_rows : (s + 1) * node_rows, :] = node_b
        copies[s][0].wait()
        pre = mm(node_b, chain_ref[...], 1, 0)
        bend_buf[s] = (pre * bend_buf[s].astype(f32)).astype(bf16)
    for line in copies:
        for copy in line[1:]:
            copy.wait()
    everything = (group * node_rows, -1)
    up_ref[...] = 2.0 * mm(normed_buf[...].reshape(everything), bend_buf[...].reshape(everything), 0, 0)
    small_ref[...] = mm(node_ref[...], both_buf[...].reshape(everything), 0, 0)
    count = len(piece_refs)
    rows = up_ref.shape[0] // count
    half = up_ref.shape[1] // 2
    lanes = small_ref.shape[1] // count
    for p, piece_ref in enumerate(piece_refs):
        to = xy ^ p
        at = pl.ds(pl.multiple_of(to * rows, rows), rows)
        piece_ref[0:rows, :] = up_ref[at, 0:half].astype(bf16)
        piece_ref[rows : 2 * rows, :] = up_ref[at, half:].astype(bf16)
        piece_ref[2 * rows :, :] = small_ref[:, pl.ds(pl.multiple_of(to * lanes, lanes), lanes)].astype(bf16)


def finish_kernel(factor, scale_ref, expand_ref, readout_ref, *rest):
    count = len(rest) - 11
    piece_refs = rest[:count]
    up_out, down_out, dec_out, gain_out, small_ref, up_ref, down_ref, dec_ref, gain_ref, sems, last_sems = rest[count:]
    rows = up_ref.shape[0] // count
    half = up_ref.shape[1] // 2
    lanes = small_ref.shape[1] // count
    width = up_ref.shape[0]
    xy = lax.axis_index("band") % count
    places = [pl.ds(pl.multiple_of((xy ^ p) * rows, rows), rows) for p in range(count)]
    up_copies = [pltpu.make_async_copy(up_ref.at[at], up_out.at[at], sems.at[0, p]) for p, at in enumerate(places)]
    down_copies = [
        pltpu.make_async_copy(down_ref.at[at], down_out.at[at], sems.at[1, p])
        for p, at in enumerate(pl.ds(p * rows, rows) for p in range(count))
    ]
    for p, piece_ref in enumerate(piece_refs):
        up_ref[places[p], 0:half] = piece_ref[0:rows, :].astype(f32) * factor
        up_ref[places[p], half:] = piece_ref[rows : 2 * rows, :].astype(f32) * factor
        up_copies[p].start()
        at = pl.ds(pl.multiple_of((xy ^ p) * lanes, lanes), lanes)
        small_ref[:, at] = piece_ref[2 * rows :, :].astype(f32) * factor
    dec_ref[...] = small_ref[:, 0:width]
    last_copies = [
        pltpu.make_async_copy(dec_ref, dec_out, last_sems.at[0]),
        pltpu.make_async_copy(gain_ref, gain_out, last_sems.at[1]),
    ]
    last_copies[0].start()
    high = small_ref[:, width:].astype(bf16)
    low = (small_ref[:, width:] - high.astype(f32)).astype(bf16)
    for p in range(count):
        at = slice(p * rows, (p + 1) * rows)
        down_ref[at, :] = mm(high[:, at], readout_ref[...], 0, 0) + mm(low[:, at], readout_ref[...], 0, 0)
        down_copies[p].start()
    for at in places:
        gain = up_ref[at, :] * expand_ref[at, :].astype(f32)
        gain = sum(gain[:, j : j + LANES] for j in range(0, 2 * half, LANES))
        gain_ref[:, at] = jnp.sum(gain.T, axis=0, keepdims=True) / scale_ref[:, at]
    last_copies[1].start()
    for copy in up_copies + down_copies + last_copies:
        copy.wait()


def vmem_call(kernel, outs, scratch=(), sems=(), budget=24, left_in=(), left_out=(), fetched=(), vmem_in=(), vmem_out=()):
    vmem = pl.BlockSpec(memory_space=pltpu.VMEM)
    smem = pl.BlockSpec(memory_space=pltpu.SMEM)
    left = pl.BlockSpec(memory_space=pltpu.HBM)
    fetched = list(fetched)

    def call(scalars, *operands):
        first = 0 if scalars is None else 1
        outside = set(left_in) | set(fetched)

        def run(*refs):
            refs = list(refs)
            if fetched:
                bufs, sem = refs[-1 - len(fetched) : -1], refs[-1]
                refs = refs[: -1 - len(fetched)]
                copies = {
                    at: pltpu.make_async_copy(refs[first + at], buf, sem.at[i])
                    for i, (at, buf) in enumerate(zip(fetched, bufs))
                }
                for at, buf in zip(fetched, bufs):
                    copies[at].start()
                    refs[first + at] = buf

                def ready(*which):
                    for at in which:
                        copies[at].wait()

                kernel(ready, *refs)
            else:
                kernel(*refs)

        return pl.pallas_call(
            run,
            out_shape=[
                (pltpu.HBM if i in left_out else pltpu.VMEM if i in vmem_out else jax.ShapeDtypeStruct)(s, d)
                for i, (s, d) in enumerate(outs)
            ],
            in_specs=[smem] * first + [left if i in outside else vmem for i in range(len(operands))],
            out_specs=[left if i in left_out else vmem for i in range(len(outs))],
            scratch_shapes=[pltpu.VMEM(s, d) for s, d in scratch]
            + [pltpu.SemaphoreType.DMA(s) for s in sems]
            + [pltpu.VMEM(operands[i].shape, operands[i].dtype) for i in fetched]
            + ([pltpu.SemaphoreType.DMA((len(fetched),))] if fetched else []),
            compiler_params=pltpu.CompilerParams(vmem_limit_bytes=budget * 2**20),
        )(
            *([] if scalars is None else [scalars]),
            *[
                pltpu.with_memory_space_constraint(x, pltpu.HBM)
                if i in outside
                else pltpu.with_memory_space_constraint(x, pltpu.VMEM)
                if i in vmem_in
                else x
                for i, x in enumerate(operands)
            ],
        )

    return call


def all_to_all(x):
    return lax.all_to_all(x, "band", split_axis=0, concat_axis=0, tiled=True)


def member_terms(student_outputs, target, weight_map):
    all_pred, all_target = (
        lax.all_gather(student_outputs[None], "member", axis=0, tiled=True),
        lax.all_gather(target, "member", axis=0, tiled=True),
    )
    teacher_terms = jnp.sum(slope(student_outputs[None] - all_target.astype(f32)), axis=0)
    own_terms = jnp.sum(slope(student_outputs[None] - all_pred), axis=0)
    return weight_map.astype(f32) * (teacher_terms - own_terms)


def state_gradient(node_grad, mesh_state, hidden_pre, scale, expand, contract, readout):
    recip = lax.rsqrt(jnp.mean(mesh_state * mesh_state, axis=1, keepdims=True) + norm_eps)
    next_grad = mm2(node_grad, readout, 1, 1)
    hidden_grad = mm2(next_grad, contract, 1, 1)
    sigma = jax.nn.sigmoid(hidden_pre)
    pre_grad = hidden_grad * sigma * (1.0 + hidden_pre * (1.0 - sigma))
    normed_grad = mm2(pre_grad, expand, 1, 1)
    gained = normed_grad * scale
    return (
        next_grad
        + recip * gained
        - mesh_state * (recip * recip * recip) * jnp.mean(gained * mesh_state, axis=1, keepdims=True)
    ).astype(bf16)


def column_body(
    group,
    scaled_atmosphere_field,
    perturbation,
    target,
    weight_map,
    enc_send,
    enc_recv,
    dec_send,
    dec_recv,
    lattice_lift_matrix,
    mixing_rescale_factor,
    expand_matrix,
    contract_matrix,
    readout_matrix,
):
    bands = lax.axis_size("band")
    channels, grid_rows = scaled_atmosphere_field.shape
    node_rows = MESH_DEV
    width, hid = expand_matrix.shape
    slots = bands * enc_send.shape[2]
    crew = bands // group
    cell_ids = jnp.arange(grid_rows, dtype=jnp.int32)
    cap = enc_send.shape[2]
    block = ((bands, cap, channels), bf16)
    weights = (lattice_lift_matrix, expand_matrix, contract_matrix, readout_matrix.T)
    outgoing, table, *near_weights = vmem_call(
        functools.partial(encode_kernel, group),
        [block, ((TABLE_ROWS, LANES), f32)] + [(w.shape, w.dtype) for w in weights],
        scratch=[block],
        sems=[(5,)],
        left_in=range(5, 9),
        left_out=(0,),
        vmem_out=range(2, 6),
        fetched=range(5),
    )(None, scaled_atmosphere_field, perturbation, enc_send, enc_recv, dec_send, *weights)
    arrived = all_to_all(outgoing).reshape(slots, channels)
    half_scale = 0.5 * mixing_rescale_factor[None, :]
    kept = [((node_rows, width), bf16), ((node_rows, hid), bf16), ((node_rows, width + hid), bf16)]
    sent = [((slots, channels), bf16), ((channels + TABLE_ROWS, slots), bf16), ((node_rows, width), f32), ((node_rows, hid), f32)] + kept
    chosen, parcel, mesh_state, half_pre, normed, bend, both = vmem_call(
        functools.partial(own_kernel, channels),
        sent,
        scratch=sent,
        sems=[(len(sent),)],
        left_out=range(len(sent)),
        fetched=(6,),
        vmem_in=(2, 3, 4, 5),
    )(None, arrived, table, *near_weights, half_scale)
    parcels, mates = parcel[None], []
    while parcels.shape[0] < group:
        held = parcels.shape[0]
        more = lax.ppermute(parcels, "band", [(i, i ^ (held * crew)) for i in range(bands)])
        parcels = jnp.concatenate([parcels, more])
        mate_kept = [((held,) + shape, dtype) for shape, dtype in kept]
        mates += vmem_call(
            functools.partial(mates_kernel, channels),
            mate_kept + [((held, TABLE_ROWS, LANES), f32)],
            scratch=mate_kept[2:],
            sems=[(held,)],
            left_out=(2,),
            vmem_out=(0, 1),
            fetched=range(5),
        )(None, lattice_lift_matrix, half_scale, expand_matrix, contract_matrix, more)
    chain = (0.5 * mm(readout_matrix, contract_matrix, 0, 1)).astype(bf16)
    slot_values = exchange(chosen, bands)
    fill_map = (cell_ids[:, None] == dec_recv[0].reshape(-1)[None, :]).astype(bf16)
    inverse = 1.0 / jnp.maximum(jnp.sum(fill_map.astype(f32), axis=1), 1.0)
    student_outputs = scaled_atmosphere_field + mm(slot_values, fill_map, 0, 1) * inverse[None, :]
    members = lax.axis_size("member")
    turns = [[(m, (m + t) % members) for m in range(members)] for t in range(1, members)]
    others = [lax.ppermute(student_outputs, "member", turn) for turn in turns]
    all_target = lax.all_gather(target[0], "member", axis=0)
    outgoing = vmem_call(
        functools.partial(loss_kernel, group),
        [((bands, channels, LANES), bf16)],
        scratch=[((crew, channels, LANES), bf16)],
        sems=[(group,)],
        left_out=(0,),
    )(None, student_outputs, all_target, weight_map, inverse[None, :], dec_recv, *others)[0]
    returned = all_to_all(outgoing)
    piece_rows = 2 * (width // crew) + channels
    node_grad, *pieces = vmem_call(
        functools.partial(backward_kernel, group, channels, len(mates)),
        [((node_rows, channels), f32)] + [((piece_rows, hid // 2), bf16)] * crew,
        scratch=[
            ((group, slots, channels), bf16),
            ((group * node_rows, channels), bf16),
            ((width, hid), f32),
            ((channels, width + hid), f32),
        ]
        + [((group,) + shape, dtype) for shape, dtype in kept],
        sems=[(3, group)],
        left_in=[3, 4, 5] + [6 + i for i in range(len(mates)) if i % 4 == 2],
        vmem_in=[6 + i for i in range(len(mates)) if i % 4 < 2],
    )(None, returned, chain, table, normed, bend, both, *mates)
    swaps = [[(i, i ^ p) for i in range(bands)] for p in range(1, crew)]
    others = [lax.ppermute(piece, "band", swap) for piece, swap in zip(pieces[1:], swaps)]
    total = sum(x.astype(f32) for x in [pieces[0]] + others).astype(bf16)
    totals = [total] + [lax.ppermute(total, "band", swap) for swap in swaps]
    state_grad = state_gradient(
        node_grad,
        mesh_state,
        2.0 * half_pre,
        mixing_rescale_factor,
        expand_matrix,
        contract_matrix,
        readout_matrix,
    )
    factor = 1.0 / math.sqrt(bands * node_rows)
    whole = [((width, hid), f32), ((hid, width), f32), ((channels, width), f32), ((1, width), f32)]
    grad_up, grad_down, grad_dec, grad_gain = vmem_call(
        functools.partial(finish_kernel, factor),
        whole,
        scratch=[((channels, width + hid), f32)] + whole,
        sems=[(2, crew), (2,)],
        left_out=range(4),
    )(None, mixing_rescale_factor[None, :], expand_matrix, readout_matrix.T, *totals)
    return (
        student_outputs[None],
        state_grad[None],
        grad_up[None],
        grad_down[None],
        grad_dec.T[None],
        grad_gain,
    )


def band_body(
    scaled_atmosphere_field,
    perturbation,
    target,
    weight_map,
    enc_send,
    enc_recv,
    dec_send,
    dec_recv,
    lattice_lift_matrix,
    mixing_rescale_factor,
    expand_matrix,
    contract_matrix,
    readout_matrix,
):
    band_count = lax.axis_size("band")
    channels, grid_rows = scaled_atmosphere_field.shape
    node_rows = MESH_DEV
    cell_ids = jnp.arange(grid_rows, dtype=jnp.int32)
    node_ids = jnp.arange(node_rows, dtype=jnp.int32)
    inputs_b = (scaled_atmosphere_field + perturbation[0].astype(f32)).astype(bf16)
    picker = (enc_send[0].reshape(-1)[:, None] == cell_ids[None, :]).astype(bf16)
    outgoing = mm(picker, inputs_b, 1, 1).astype(bf16)
    arrived = exchange(outgoing, band_count)
    slot_rows = jax.nn.silu(mm(arrived, lattice_lift_matrix, 1, 0)).astype(bf16)
    landing = (node_ids[:, None] == enc_recv[0].reshape(-1)[None, :]).astype(bf16)
    edge_count = jnp.sum(landing.astype(f32), axis=1, keepdims=True)
    mesh_state = mm(landing, slot_rows, 1, 0) / jnp.maximum(edge_count, 1.0)
    recip = lax.rsqrt(jnp.mean(mesh_state * mesh_state, axis=1, keepdims=True) + norm_eps)
    normed_b = (mesh_state * recip * mixing_rescale_factor).astype(bf16)
    hidden_pre = mm(normed_b, expand_matrix, 1, 0)
    hidden_b = jax.nn.silu(hidden_pre).astype(bf16)
    next_b = (mesh_state + mm(hidden_b, contract_matrix, 1, 0)).astype(bf16)
    mesh_picker = (dec_send[0].reshape(-1)[:, None] == node_ids[None, :]).astype(bf16)
    fill_map = (cell_ids[:, None] == dec_recv[0].reshape(-1)[None, :]).astype(bf16)
    inverse = 1.0 / jnp.maximum(jnp.sum(fill_map.astype(f32), axis=1), 1.0)
    projected = mm(next_b, readout_matrix, 1, 0).astype(bf16)
    chosen = mm(mesh_picker, projected, 1, 0).astype(bf16)
    slot_values = exchange(chosen, band_count)
    grid_sum = mm(slot_values, fill_map, 0, 1)
    student_outputs = scaled_atmosphere_field + grid_sum * inverse[None, :]
    pred_grad = member_terms(student_outputs, target, weight_map)
    scaled = (pred_grad * inverse[None, :]).astype(bf16)
    slot_grad = mm(fill_map, scaled, 0, 1).astype(bf16)
    returned = exchange(slot_grad, band_count)
    node_grad = mm(mesh_picker, returned, 0, 0)
    grad_hi, grad_lo = split3(node_grad)
    states = jnp.concatenate([next_b, hidden_b], axis=1)
    small = mm(states, grad_hi, 0, 0) + mm(states, grad_lo, 0, 0)
    hidden_grad = mm2(mm2(node_grad, readout_matrix, 1, 1), contract_matrix, 1, 1)
    sigma = jax.nn.sigmoid(hidden_pre)
    pre_hi, pre_lo = split3(hidden_grad * sigma * (1.0 + hidden_pre * (1.0 - sigma)))
    up_part = mm(normed_b, pre_hi, 0, 0) + mm(normed_b, pre_lo, 0, 0)
    state_grad = state_gradient(
        node_grad, mesh_state, hidden_pre, mixing_rescale_factor, expand_matrix, contract_matrix, readout_matrix
    )
    width, hid = up_part.shape
    factor = 1.0 / math.sqrt(band_count * node_rows)
    packed = jnp.concatenate([up_part, small[:width], small[width:]], axis=1)
    packed = jnp.pad(packed, ((0, 0), (0, -packed.shape[1] % 16)))
    total = sum_over_bands(packed, band_count) * factor
    grad_up = total[:, :hid]
    grad_dec = total[:, hid : hid + channels]
    grad_down = mm2(total[:, hid + channels : hid + 2 * channels], readout_matrix, 1, 1)
    grad_gain = jnp.sum(grad_up * expand_matrix.astype(f32), axis=1) / mixing_rescale_factor
    return (
        student_outputs[None],
        state_grad[None],
        grad_up[None],
        grad_down[None],
        grad_dec[None],
        grad_gain[None],
    )


def body(*args):
    field, enc_send, dec_send, expand = args[0], args[4], args[6], args[10]
    bands, cap = enc_send.shape[1:]
    channels, grid_rows = field.shape
    group = LANES // cap
    column = (
        dec_send.shape[2] == cap
        and LANES % cap == 0
        and cap % 16 == 0
        and group * group == bands
        and channels % 16 == 0
        and max(grid_rows, MESH_DEV) <= 256
        and bands * cap * 2 <= TABLE_ROWS * LANES
        and expand.shape[0] == expand.shape[1]
    )
    return column_body(group, *args) if column else band_body(*args)


def solution(mesh):
    return jax.shard_map(
        body,
        mesh=mesh,
        in_specs=(
            P(None, "band"),
            P("member", None, "band"),
            P("member", None, "band"),
            P(None, "band"),
            P("band", None, None),
            P("band", None, None),
            P("band", None, None),
            P("band", None, None),
            P(),
            P(),
            P(),
            P(),
            P(),
        ),
        out_specs=(
            P("member", None, "band"),
            P("member", "band", None),
            P("member", None, None),
            P("member", None, None),
            P("member", None, None),
            P("member", None),
        ),
        check_vma=False,
    )
```

```python
import functools
import math

import jax
import jax.numpy as jnp
from jax import lax
from jax.experimental import pallas as pl
from jax.experimental.pallas import tpu as pltpu
from jax.sharding import PartitionSpec as P


MESH_DEV = 256


smooth_sq = 0.01
norm_eps = 1e-05

bf16 = jnp.bfloat16
f32 = jnp.float32


def slope(diff):
    return diff * lax.rsqrt(diff * diff + smooth_sq)


def mm(a, b, ca, cb):
    return lax.dot_general(a, b, (((ca,), (cb,)), ((), ())), preferred_element_type=f32)


def split3(x):
    hi = x.astype(bf16)
    return hi, (x - hi.astype(f32)).astype(bf16)


def mm2(a, b, ca, cb):
    hi, lo = split3(a)
    return mm(hi, b, ca, cb) + mm(lo, b, ca, cb)


def exchange(x, band_count):
    rows, width = x.shape
    y = lax.all_to_all(
        x.reshape(band_count, rows // band_count, width), "band", split_axis=0, concat_axis=0, tiled=True
    )
    return y.reshape(rows, width)


def sum_over_bands(x, band_count):
    rows, width = x.shape
    parts = lax.all_to_all(
        x.astype(bf16).reshape(band_count, rows // band_count, width),
        "band",
        split_axis=0,
        concat_axis=0,
        tiled=True,
    )
    own = jnp.sum(parts.astype(f32), axis=0).astype(bf16)
    spread = jnp.broadcast_to(own[None], parts.shape)
    full = lax.all_to_all(spread, "band", split_axis=0, concat_axis=0, tiled=True)
    return full.reshape(rows, width).astype(f32)


TABLE_ROWS = 8
LANES = 128


def one_hot(a, b):
    return jnp.where(a == b, 1.0, 0.0).astype(bf16)


def lane_blocks(table, group, rows, row_of):
    bands, cap = table.shape
    r = lax.broadcasted_iota(jnp.int32, (rows, bands), 0)
    b = lax.broadcasted_iota(jnp.int32, (rows, bands), 1)
    slot = lax.broadcasted_iota(jnp.int32, (cap, LANES), 0)
    lane = lax.broadcasted_iota(jnp.int32, (cap, LANES), 1)
    out = jnp.zeros((rows, LANES), f32)
    for j in range(group):
        rows_j = mm(jnp.where(row_of(r, j) == b, 1.0, 0.0).astype(bf16), table, 1, 0).astype(bf16)
        out = out + mm(rows_j, one_hot(lane, slot + j * cap), 1, 0)
    return out


def column_order(table_ref, group):
    table = table_ref[0].astype(f32).astype(bf16)
    crew = table.shape[0] // group
    return lane_blocks(table, group, 8, lambda r, j: jnp.where(r < crew, j * crew + r, -1)), crew


def send_copies(group, crew, block_ref, out_ref, sems):
    return [
        pltpu.make_async_copy(block_ref, out_ref.at[j * crew : (j + 1) * crew], sems.at[j]) for j in range(group)
    ]


def encode_kernel(
    group,
    ready,
    field_ref,
    noise_ref,
    send_ref,
    recv_ref,
    mesh_ref,
    fill_ref,
    lift_in,
    expand_in,
    contract_in,
    readout_in,
    out_ref,
    table_ref,
    order_ref,
    lift_ref,
    expand_ref,
    contract_ref,
    readout_ref,
    block_ref,
    sems,
):
    grid_rows = field_ref.shape[1]
    bands, _ = send_ref.shape[1:]
    rows = bands // group
    pairs = [(lift_in, lift_ref), (expand_in, expand_ref), (contract_in, contract_ref), (readout_in, readout_ref)]
    weights = [pltpu.make_async_copy(a, b, sems.at[i + 1]) for i, (a, b) in enumerate(pairs)]
    for copy in weights:
        copy.start()
    ready(0, 1, 2, 3, 4, 5)
    inputs = (field_ref[...] + noise_ref[0].astype(f32)).astype(bf16) * 0.5

    def in_rows(ref, first):
        table = ref[0].astype(f32).astype(bf16)
        return lane_blocks(
            table,
            group,
            TABLE_ROWS,
            lambda r, j: jnp.where((r >= first) & (r < first + rows), (r - first) * group + j, -1),
        )

    order = in_rows(send_ref, 0)
    table_ref[...] = in_rows(recv_ref, 0) + in_rows(mesh_ref, rows)
    subs = lax.broadcasted_iota(jnp.int32, (grid_rows, LANES), 0).astype(f32)
    pick = jnp.concatenate([one_hot(subs, order[r : r + 1, :]) for r in range(rows)], axis=1)
    block_ref[...] = mm(inputs, pick, 1, 0).T.astype(bf16).reshape(block_ref.shape)
    copy = pltpu.make_async_copy(block_ref, out_ref, sems.at[0])
    copy.start()
    order_ref[...] = column_order(fill_ref, group)[0]
    for copy in [copy] + weights:
        copy.wait()


def loss_kernel(group, student_ref, target_ref, weight_ref, inverse_ref, order_ref, *rest):
    other_refs, (out_ref, block_ref, sems) = rest[:-3], rest[-3:]
    grid_rows = student_ref.shape[1]
    student = student_ref[...]
    terms = jnp.zeros_like(student)
    for j in range(target_ref.shape[0]):
        terms = terms + slope(student - target_ref[j].astype(f32))
    for other_ref in (student_ref,) + other_refs:
        terms = terms - slope(student - other_ref[...])
    scaled = (weight_ref[...].astype(f32) * terms * inverse_ref[...]).astype(bf16)
    order, crew = order_ref[...], block_ref.shape[0]
    subs = lax.broadcasted_iota(jnp.int32, (grid_rows, LANES), 0).astype(f32)
    for c in range(crew):
        block_ref[c] = mm(scaled, one_hot(subs, order[c : c + 1, :]), 1, 0).astype(bf16)
    copies = send_copies(group, crew, block_ref, out_ref, sems)
    for copy in copies:
        copy.start()
    for copy in copies:
        copy.wait()


def node_forward(cells, channel_dim, table, scale_ref, expand_ref, contract_ref, lift_ref, ready, keep=None):
    node_rows = MESH_DEV
    slots = cells.shape[1 - channel_dim]
    subs = lax.broadcasted_iota(jnp.int32, (node_rows, LANES), 0).astype(f32)
    latent = mm(cells, lift_ref[...], channel_dim, 0)
    latent = (latent + latent * jnp.tanh(latent)).astype(bf16)
    parts = slots // LANES
    landing = jnp.concatenate([one_hot(subs, table[j : j + 1, :]) for j in range(parts)], axis=1)
    count = mm(landing, jnp.ones((slots, LANES), bf16), 1, 0)[:, 0:1]
    state = mm(landing, latent, 1, 0) * (1.0 / jnp.maximum(count, 1.0))
    recip = lax.rsqrt(jnp.mean(state * state, axis=1, keepdims=True) + norm_eps)
    if keep:
        keep(2, state)
    ready()
    normed = (state * recip * scale_ref[...]).astype(bf16)
    if keep:
        keep(4, normed)
    pre = mm(normed, expand_ref[...], 1, 0)
    if keep:
        keep(3, pre)
    bent = jnp.tanh(pre)
    above = 1.0 + bent
    bend = (above * (1.0 + pre * (1.0 - bent))).astype(bf16)
    if keep:
        keep(5, bend)
    hidden = (pre * above).astype(bf16)
    following = (state + mm(hidden, contract_ref[...], 1, 0)).astype(bf16)
    return state, pre, normed, bend, following, hidden


def own_kernel(
    channels,
    ready,
    cells_ref,
    table_ref,
    lift_ref,
    expand_ref,
    contract_ref,
    readout_ref,
    scale_ref,
    chosen_ref,
    *rest,
):
    count = len(rest) // 2
    out_refs, bufs, sems = (chosen_ref,) + rest[: count - 1], rest[count - 1 : -1], rest[-1]
    copies = [pltpu.make_async_copy(a, b, sems.at[i]) for i, (a, b) in enumerate(zip(bufs, out_refs))]
    chosen_buf, parcel_buf, _, _, _, _, both_buf = bufs
    slots = cells_ref.shape[0]
    width = both_buf.shape[1] // 2
    parts = slots // LANES
    table = table_ref[...]
    parcel_buf[0:channels, :] = cells_ref[...].astype(f32).T.astype(bf16)
    parcel_buf[channels:, :] = jnp.concatenate([table] * parts, axis=1).astype(bf16)
    copies[1].start()

    def keep(at, value):
        bufs[at][...] = value
        copies[at].start()

    state, _, _, _, following, hidden = node_forward(
        cells_ref[...],
        1,
        table,
        scale_ref,
        expand_ref,
        contract_ref,
        lift_ref,
        lambda: ready(6),
        keep,
    )
    both_buf[:, 0:width] = following
    both_buf[:, width:] = hidden
    copies[6].start()
    projected = mm(following, readout_ref[...], 1, 1).astype(bf16)
    subs = lax.broadcasted_iota(jnp.int32, (state.shape[0], LANES), 0).astype(f32)
    for j in range(parts):
        pick = one_hot(subs, table[parts + j : parts + j + 1, :])
        chosen_buf[j * LANES : (j + 1) * LANES, :] = mm(pick, projected, 0, 0).astype(bf16)
    copies[0].start()
    for copy in copies:
        copy.wait()


def mates_kernel(
    channels,
    ready,
    lift_ref,
    scale_ref,
    expand_ref,
    contract_ref,
    parcel_ref,
    normed_ref,
    bend_ref,
    both_out,
    table_ref,
    both_buf,
    sems,
):
    mates = table_ref.shape[0]
    width = both_buf.shape[2] // 2
    ready(*range(5))
    copies = [pltpu.make_async_copy(both_buf.at[m], both_out.at[m], sems.at[m]) for m in range(mates)]
    for m in range(mates):
        table = parcel_ref[m, channels:, 0:LANES].astype(f32)
        table_ref[m] = table
        _, _, normed, bend, following, hidden = node_forward(
            parcel_ref[m, 0:channels, :], 0, table, scale_ref, expand_ref, contract_ref, lift_ref, lambda: None
        )
        normed_ref[m] = normed
        bend_ref[m] = bend
        both_buf[m, :, 0:width] = following
        both_buf[m, :, width:] = hidden
        copies[m].start()
    for copy in copies:
        copy.wait()


def backward_kernel(
    group,
    channels,
    mate_count,
    grad_ref,
    chain_ref,
    table_ref,
    normed_ref,
    bend_ref,
    both_ref,
    *rest,
):
    mate_refs, own_ref, piece_refs = rest[:mate_count], rest[mate_count], rest[mate_count + 1 : -8]
    value_ref, node_ref, up_ref, small_ref, normed_buf, bend_buf, both_buf, sems = rest[-8:]
    bands = grad_ref.shape[0]
    slots = value_ref.shape[1]
    node_rows = normed_ref.shape[0]
    cap = slots // bands
    crew = grad_ref.shape[0] // group
    band = lax.axis_index("band")
    z, xy = band // crew, band % crew
    subs = lax.broadcasted_iota(jnp.int32, (node_rows, LANES), 0).astype(f32)
    held = [(table_ref[...], bend_ref, normed_ref, both_ref)]
    for at in range(0, mate_count, 4):
        mate_normed, mate_bend, mate_both, mate_table = mate_refs[at : at + 4]
        held += [
            (mate_table[m], mate_bend.at[m], mate_normed.at[m], mate_both.at[m]) for m in range(mate_table.shape[0])
        ]
    copies = [
        [
            pltpu.make_async_copy(ref, buf.at[s], sems.at[i, s])
            for i, (ref, buf) in enumerate(zip(held[s][1:], (bend_buf, normed_buf, both_buf)))
        ]
        for s in range(group)
    ]
    for line in copies:
        for copy in line:
            copy.start()

    def turn(b, carry):
        values = grad_ref[b].astype(f32).T.astype(bf16)
        value_ref[:, pl.ds(pl.multiple_of(b * cap, cap), cap), :] = values.reshape(group, cap, channels)
        return carry

    lax.fori_loop(0, bands, turn, 0, unroll=True)
    parts = slots // LANES
    for s in range(group):
        table = held[s][0]
        pick = jnp.concatenate(
            [one_hot(subs, table[parts + j : parts + j + 1, :]) for j in range(parts)], axis=1
        )
        node_grad = mm(pick, value_ref[z ^ s], 1, 0)
        if s == 0:
            own_ref[...] = node_grad
        node_b = node_grad.astype(bf16)
        node_ref[s * node_rows : (s + 1) * node_rows, :] = node_b
        copies[s][0].wait()
        pre = mm(node_b, chain_ref[...], 1, 0)
        bend_buf[s] = (pre * bend_buf[s].astype(f32)).astype(bf16)
    for line in copies:
        for copy in line[1:]:
            copy.wait()
    everything = (group * node_rows, -1)
    up_ref[...] = 2.0 * mm(normed_buf[...].reshape(everything), bend_buf[...].reshape(everything), 0, 0)
    small_ref[...] = mm(node_ref[...], both_buf[...].reshape(everything), 0, 0)
    count = len(piece_refs)
    rows = up_ref.shape[0] // count
    half = up_ref.shape[1] // 2
    lanes = small_ref.shape[1] // count
    for p, piece_ref in enumerate(piece_refs):
        to = xy ^ p
        at = pl.ds(pl.multiple_of(to * rows, rows), rows)
        piece_ref[0:rows, :] = up_ref[at, 0:half].astype(bf16)
        piece_ref[rows : 2 * rows, :] = up_ref[at, half:].astype(bf16)
        piece_ref[2 * rows :, :] = small_ref[:, pl.ds(pl.multiple_of(to * lanes, lanes), lanes)].astype(bf16)


def finish_kernel(factor, scale_ref, expand_ref, readout_ref, *rest):
    count = len(rest) - 11
    piece_refs = rest[:count]
    up_out, down_out, dec_out, gain_out, small_ref, up_ref, down_ref, dec_ref, gain_ref, sems, last_sems = rest[count:]
    rows = up_ref.shape[0] // count
    half = up_ref.shape[1] // 2
    lanes = small_ref.shape[1] // count
    width = up_ref.shape[0]
    xy = lax.axis_index("band") % count
    places = [pl.ds(pl.multiple_of((xy ^ p) * rows, rows), rows) for p in range(count)]
    up_copies = [pltpu.make_async_copy(up_ref.at[at], up_out.at[at], sems.at[0, p]) for p, at in enumerate(places)]
    down_copies = [
        pltpu.make_async_copy(down_ref.at[at], down_out.at[at], sems.at[1, p])
        for p, at in enumerate(pl.ds(p * rows, rows) for p in range(count))
    ]
    for p, piece_ref in enumerate(piece_refs):
        up_ref[places[p], 0:half] = piece_ref[0:rows, :].astype(f32) * factor
        up_ref[places[p], half:] = piece_ref[rows : 2 * rows, :].astype(f32) * factor
        up_copies[p].start()
        at = pl.ds(pl.multiple_of((xy ^ p) * lanes, lanes), lanes)
        small_ref[:, at] = piece_ref[2 * rows :, :].astype(f32) * factor
    dec_ref[...] = small_ref[:, 0:width]
    last_copies = [
        pltpu.make_async_copy(dec_ref, dec_out, last_sems.at[0]),
        pltpu.make_async_copy(gain_ref, gain_out, last_sems.at[1]),
    ]
    last_copies[0].start()
    high = small_ref[:, width:].astype(bf16)
    low = (small_ref[:, width:] - high.astype(f32)).astype(bf16)
    for p in range(count):
        at = slice(p * rows, (p + 1) * rows)
        down_ref[at, :] = mm(high[:, at], readout_ref[...], 0, 0) + mm(low[:, at], readout_ref[...], 0, 0)
        down_copies[p].start()
    for at in places:
        gain = up_ref[at, :] * expand_ref[at, :].astype(f32)
        gain = sum(gain[:, j : j + LANES] for j in range(0, 2 * half, LANES))
        gain_ref[:, at] = jnp.sum(gain.T, axis=0, keepdims=True) / scale_ref[:, at]
    last_copies[1].start()
    for copy in up_copies + down_copies + last_copies:
        copy.wait()


def vmem_call(kernel, outs, scratch=(), sems=(), budget=24, left_in=(), left_out=(), fetched=(), vmem_in=(), vmem_out=()):
    vmem = pl.BlockSpec(memory_space=pltpu.VMEM)
    smem = pl.BlockSpec(memory_space=pltpu.SMEM)
    left = pl.BlockSpec(memory_space=pltpu.HBM)
    fetched = list(fetched)

    def call(scalars, *operands):
        first = 0 if scalars is None else 1
        outside = set(left_in) | set(fetched)

        def run(*refs):
            refs = list(refs)
            if fetched:
                bufs, sem = refs[-1 - len(fetched) : -1], refs[-1]
                refs = refs[: -1 - len(fetched)]
                copies = {
                    at: pltpu.make_async_copy(refs[first + at], buf, sem.at[i])
                    for i, (at, buf) in enumerate(zip(fetched, bufs))
                }
                for at, buf in zip(fetched, bufs):
                    copies[at].start()
                    refs[first + at] = buf

                def ready(*which):
                    for at in which:
                        copies[at].wait()

                kernel(ready, *refs)
            else:
                kernel(*refs)

        return pl.pallas_call(
            run,
            out_shape=[
                (pltpu.HBM if i in left_out else pltpu.VMEM if i in vmem_out else jax.ShapeDtypeStruct)(s, d)
                for i, (s, d) in enumerate(outs)
            ],
            in_specs=[smem] * first + [left if i in outside else vmem for i in range(len(operands))],
            out_specs=[left if i in left_out else vmem for i in range(len(outs))],
            scratch_shapes=[pltpu.VMEM(s, d) for s, d in scratch]
            + [pltpu.SemaphoreType.DMA(s) for s in sems]
            + [pltpu.VMEM(operands[i].shape, operands[i].dtype) for i in fetched]
            + ([pltpu.SemaphoreType.DMA((len(fetched),))] if fetched else []),
            compiler_params=pltpu.CompilerParams(vmem_limit_bytes=budget * 2**20),
        )(
            *([] if scalars is None else [scalars]),
            *[
                pltpu.with_memory_space_constraint(x, pltpu.HBM)
                if i in outside
                else pltpu.with_memory_space_constraint(x, pltpu.VMEM)
                if i in vmem_in
                else x
                for i, x in enumerate(operands)
            ],
        )

    return call


def all_to_all(x):
    return lax.all_to_all(x, "band", split_axis=0, concat_axis=0, tiled=True)


def member_terms(student_outputs, target, weight_map):
    all_pred, all_target = (
        lax.all_gather(student_outputs[None], "member", axis=0, tiled=True),
        lax.all_gather(target, "member", axis=0, tiled=True),
    )
    teacher_terms = jnp.sum(slope(student_outputs[None] - all_target.astype(f32)), axis=0)
    own_terms = jnp.sum(slope(student_outputs[None] - all_pred), axis=0)
    return weight_map.astype(f32) * (teacher_terms - own_terms)


def state_gradient(node_grad, mesh_state, hidden_pre, scale, expand, contract, readout):
    recip = lax.rsqrt(jnp.mean(mesh_state * mesh_state, axis=1, keepdims=True) + norm_eps)
    next_grad = mm2(node_grad, readout, 1, 1)
    hidden_grad = mm2(next_grad, contract, 1, 1)
    sigma = jax.nn.sigmoid(hidden_pre)
    pre_grad = hidden_grad * sigma * (1.0 + hidden_pre * (1.0 - sigma))
    normed_grad = mm2(pre_grad, expand, 1, 1)
    gained = normed_grad * scale
    return (
        next_grad
        + recip * gained
        - mesh_state * (recip * recip * recip) * jnp.mean(gained * mesh_state, axis=1, keepdims=True)
    ).astype(bf16)


def column_body(
    group,
    scaled_atmosphere_field,
    perturbation,
    target,
    weight_map,
    enc_send,
    enc_recv,
    dec_send,
    dec_recv,
    lattice_lift_matrix,
    mixing_rescale_factor,
    expand_matrix,
    contract_matrix,
    readout_matrix,
):
    bands = lax.axis_size("band")
    channels, grid_rows = scaled_atmosphere_field.shape
    node_rows = MESH_DEV
    width, hid = expand_matrix.shape
    slots = bands * enc_send.shape[2]
    crew = bands // group
    cell_ids = jnp.arange(grid_rows, dtype=jnp.int32)
    cap = enc_send.shape[2]
    block = ((bands, cap, channels), bf16)
    weights = (lattice_lift_matrix, expand_matrix, contract_matrix, readout_matrix.T)
    outgoing, table, column_slots, *near_weights = vmem_call(
        functools.partial(encode_kernel, group),
        [block, ((TABLE_ROWS, LANES), f32), ((8, LANES), f32)] + [(w.shape, w.dtype) for w in weights],
        scratch=[block],
        sems=[(5,)],
        left_in=range(6, 10),
        left_out=(0,),
        vmem_out=range(3, 7),
        fetched=range(6),
    )(None, scaled_atmosphere_field, perturbation, enc_send, enc_recv, dec_send, dec_recv, *weights)
    arrived = all_to_all(outgoing).reshape(slots, channels)
    half_scale = 0.5 * mixing_rescale_factor[None, :]
    kept = [((node_rows, width), bf16), ((node_rows, hid), bf16), ((node_rows, width + hid), bf16)]
    sent = [((slots, channels), bf16), ((channels + TABLE_ROWS, slots), bf16), ((node_rows, width), f32), ((node_rows, hid), f32)] + kept
    chosen, parcel, mesh_state, half_pre, normed, bend, both = vmem_call(
        functools.partial(own_kernel, channels),
        sent,
        scratch=sent,
        sems=[(len(sent),)],
        left_out=range(len(sent)),
        fetched=(6,),
        vmem_in=(2, 3, 4, 5),
    )(None, arrived, table, *near_weights, half_scale)
    parcels, mates = parcel[None], []
    while parcels.shape[0] < group:
        held = parcels.shape[0]
        more = lax.ppermute(parcels, "band", [(i, i ^ (held * crew)) for i in range(bands)])
        parcels = jnp.concatenate([parcels, more])
        mate_kept = [((held,) + shape, dtype) for shape, dtype in kept]
        mates += vmem_call(
            functools.partial(mates_kernel, channels),
            mate_kept + [((held, TABLE_ROWS, LANES), f32)],
            scratch=mate_kept[2:],
            sems=[(held,)],
            left_out=(2,),
            vmem_out=(0, 1),
            fetched=range(5),
        )(None, lattice_lift_matrix, half_scale, expand_matrix, contract_matrix, more)
    chain = (0.5 * mm(readout_matrix, contract_matrix, 0, 1)).astype(bf16)
    slot_values = exchange(chosen, bands)
    fill_map = (cell_ids[:, None] == dec_recv[0].reshape(-1)[None, :]).astype(bf16)
    inverse = 1.0 / jnp.maximum(jnp.sum(fill_map.astype(f32), axis=1), 1.0)
    student_outputs = scaled_atmosphere_field + mm(slot_values, fill_map, 0, 1) * inverse[None, :]
    members = lax.axis_size("member")
    turns = [[(m, (m + t) % members) for m in range(members)] for t in range(1, members)]
    others = [lax.ppermute(student_outputs, "member", turn) for turn in turns]
    all_target = lax.all_gather(target[0], "member", axis=0)
    outgoing = vmem_call(
        functools.partial(loss_kernel, group),
        [((bands, channels, LANES), bf16)],
        scratch=[((crew, channels, LANES), bf16)],
        sems=[(group,)],
        left_out=(0,),
    )(None, student_outputs, all_target, weight_map, inverse[None, :], column_slots, *others)[0]
    returned = all_to_all(outgoing)
    piece_rows = 2 * (width // crew) + channels
    node_grad, *pieces = vmem_call(
        functools.partial(backward_kernel, group, channels, len(mates)),
        [((node_rows, channels), f32)] + [((piece_rows, hid // 2), bf16)] * crew,
        scratch=[
            ((group, slots, channels), bf16),
            ((group * node_rows, channels), bf16),
            ((width, hid), f32),
            ((channels, width + hid), f32),
        ]
        + [((group,) + shape, dtype) for shape, dtype in kept],
        sems=[(3, group)],
        left_in=[3, 4, 5] + [6 + i for i in range(len(mates)) if i % 4 == 2],
        vmem_in=[6 + i for i in range(len(mates)) if i % 4 < 2],
    )(None, returned, chain, table, normed, bend, both, *mates)
    swaps = [[(i, i ^ p) for i in range(bands)] for p in range(1, crew)]
    others = [lax.ppermute(piece, "band", swap) for piece, swap in zip(pieces[1:], swaps)]
    total = sum(x.astype(f32) for x in [pieces[0]] + others).astype(bf16)
    totals = [total] + [lax.ppermute(total, "band", swap) for swap in swaps]
    state_grad = state_gradient(
        node_grad,
        mesh_state,
        2.0 * half_pre,
        mixing_rescale_factor,
        expand_matrix,
        contract_matrix,
        readout_matrix,
    )
    factor = 1.0 / math.sqrt(bands * node_rows)
    whole = [((width, hid), f32), ((hid, width), f32), ((channels, width), f32), ((1, width), f32)]
    grad_up, grad_down, grad_dec, grad_gain = vmem_call(
        functools.partial(finish_kernel, factor),
        whole,
        scratch=[((channels, width + hid), f32)] + whole,
        sems=[(2, crew), (2,)],
        left_out=range(4),
    )(None, mixing_rescale_factor[None, :], expand_matrix, readout_matrix.T, *totals)
    return (
        student_outputs[None],
        state_grad[None],
        grad_up[None],
        grad_down[None],
        grad_dec.T[None],
        grad_gain,
    )


def band_body(
    scaled_atmosphere_field,
    perturbation,
    target,
    weight_map,
    enc_send,
    enc_recv,
    dec_send,
    dec_recv,
    lattice_lift_matrix,
    mixing_rescale_factor,
    expand_matrix,
    contract_matrix,
    readout_matrix,
):
    band_count = lax.axis_size("band")
    channels, grid_rows = scaled_atmosphere_field.shape
    node_rows = MESH_DEV
    cell_ids = jnp.arange(grid_rows, dtype=jnp.int32)
    node_ids = jnp.arange(node_rows, dtype=jnp.int32)
    inputs_b = (scaled_atmosphere_field + perturbation[0].astype(f32)).astype(bf16)
    picker = (enc_send[0].reshape(-1)[:, None] == cell_ids[None, :]).astype(bf16)
    outgoing = mm(picker, inputs_b, 1, 1).astype(bf16)
    arrived = exchange(outgoing, band_count)
    slot_rows = jax.nn.silu(mm(arrived, lattice_lift_matrix, 1, 0)).astype(bf16)
    landing = (node_ids[:, None] == enc_recv[0].reshape(-1)[None, :]).astype(bf16)
    edge_count = jnp.sum(landing.astype(f32), axis=1, keepdims=True)
    mesh_state = mm(landing, slot_rows, 1, 0) / jnp.maximum(edge_count, 1.0)
    recip = lax.rsqrt(jnp.mean(mesh_state * mesh_state, axis=1, keepdims=True) + norm_eps)
    normed_b = (mesh_state * recip * mixing_rescale_factor).astype(bf16)
    hidden_pre = mm(normed_b, expand_matrix, 1, 0)
    hidden_b = jax.nn.silu(hidden_pre).astype(bf16)
    next_b = (mesh_state + mm(hidden_b, contract_matrix, 1, 0)).astype(bf16)
    mesh_picker = (dec_send[0].reshape(-1)[:, None] == node_ids[None, :]).astype(bf16)
    fill_map = (cell_ids[:, None] == dec_recv[0].reshape(-1)[None, :]).astype(bf16)
    inverse = 1.0 / jnp.maximum(jnp.sum(fill_map.astype(f32), axis=1), 1.0)
    projected = mm(next_b, readout_matrix, 1, 0).astype(bf16)
    chosen = mm(mesh_picker, projected, 1, 0).astype(bf16)
    slot_values = exchange(chosen, band_count)
    grid_sum = mm(slot_values, fill_map, 0, 1)
    student_outputs = scaled_atmosphere_field + grid_sum * inverse[None, :]
    pred_grad = member_terms(student_outputs, target, weight_map)
    scaled = (pred_grad * inverse[None, :]).astype(bf16)
    slot_grad = mm(fill_map, scaled, 0, 1).astype(bf16)
    returned = exchange(slot_grad, band_count)
    node_grad = mm(mesh_picker, returned, 0, 0)
    grad_hi, grad_lo = split3(node_grad)
    states = jnp.concatenate([next_b, hidden_b], axis=1)
    small = mm(states, grad_hi, 0, 0) + mm(states, grad_lo, 0, 0)
    hidden_grad = mm2(mm2(node_grad, readout_matrix, 1, 1), contract_matrix, 1, 1)
    sigma = jax.nn.sigmoid(hidden_pre)
    pre_hi, pre_lo = split3(hidden_grad * sigma * (1.0 + hidden_pre * (1.0 - sigma)))
    up_part = mm(normed_b, pre_hi, 0, 0) + mm(normed_b, pre_lo, 0, 0)
    state_grad = state_gradient(
        node_grad, mesh_state, hidden_pre, mixing_rescale_factor, expand_matrix, contract_matrix, readout_matrix
    )
    width, hid = up_part.shape
    factor = 1.0 / math.sqrt(band_count * node_rows)
    packed = jnp.concatenate([up_part, small[:width], small[width:]], axis=1)
    packed = jnp.pad(packed, ((0, 0), (0, -packed.shape[1] % 16)))
    total = sum_over_bands(packed, band_count) * factor
    grad_up = total[:, :hid]
    grad_dec = total[:, hid : hid + channels]
    grad_down = mm2(total[:, hid + channels : hid + 2 * channels], readout_matrix, 1, 1)
    grad_gain = jnp.sum(grad_up * expand_matrix.astype(f32), axis=1) / mixing_rescale_factor
    return (
        student_outputs[None],
        state_grad[None],
        grad_up[None],
        grad_down[None],
        grad_dec[None],
        grad_gain[None],
    )


def body(*args):
    field, enc_send, dec_send, expand = args[0], args[4], args[6], args[10]
    bands, cap = enc_send.shape[1:]
    channels, grid_rows = field.shape
    group = LANES // cap
    column = (
        dec_send.shape[2] == cap
        and LANES % cap == 0
        and cap % 16 == 0
        and group * group == bands
        and channels % 16 == 0
        and max(grid_rows, MESH_DEV) <= 256
        and bands * cap * 2 <= TABLE_ROWS * LANES
        and expand.shape[0] == expand.shape[1]
    )
    return column_body(group, *args) if column else band_body(*args)


def solution(mesh):
    return jax.shard_map(
        body,
        mesh=mesh,
        in_specs=(
            P(None, "band"),
            P("member", None, "band"),
            P("member", None, "band"),
            P(None, "band"),
            P("band", None, None),
            P("band", None, None),
            P("band", None, None),
            P("band", None, None),
            P(),
            P(),
            P(),
            P(),
            P(),
        ),
        out_specs=(
            P("member", None, "band"),
            P("member", "band", None),
            P("member", None, None),
            P("member", None, None),
            P("member", None, None),
            P("member", None),
        ),
        check_vma=False,
    )
```
